256 devices in a mesh: axial: 16 (over z, core), circ: 16 (over x, y).
Axes of the slice: x: 4, y: 4, z: 8, core: 2. Of those that a mesh axis runs over, the one named last changes fastest.
Arguments:
- right_side: float32 [128, 256, 256], P('axial', 'circ'), may hold values from -6 to 6
- stiffness: float32 [128, 256, 256], P('axial', 'circ'), may hold values from 0.03 to 0.3
- material: int32 [128, 256, 256], P('axial', 'circ'), may hold values from 0 to 15
- groups: int32 [128, 256, 256], P('axial', 'circ'), may hold values from 0 to 7, as said below
Outputs:
- solution: float32 [128, 256, 256], P('axial', 'circ')
- residual: float32 [128, 256, 256], P('axial', 'circ')
The draws below stay inside these ranges and needn't reach their ends.
Inputs may be any that keep to these rules, and one draw needn't show every extreme that they name: `groups`: in every column of cells along the third dimension every group number from 0 to 7 occurs.
All inputs are finite; a program needn't handle non-finite values.
Results may differ from the reference program's by a relative error of at most 0.0003.
Values sent between devices are 32-bit elements; how exact they have to be, the bound alone decides.
No kernel may reach another device: no remote copies, remote signals or barrier semaphores. Data moves between devices by JAX's collectives and lax.ppermute only.
A program may use at most 128 MiB of HBM per device.

```python
import math
import jax
import jax.numpy as jnp
import numpy as np
from jax import lax

NZ = 256
LABELS = 8
CLASSES = 16
ITERS = 2
NX = 128
NY = 256
N_AXIAL = 16
N_CIRC = 16


def draw_groups(key, part):
    own_key = jax.random.fold_in(key, 7)
    key_swap, key_other = jax.random.split(own_key)
    full_shape = (NX, NY, NZ)
    radial_pos = lax.broadcasted_iota(jnp.int32, full_shape, 2)
    layer_cells = NZ // LABELS
    base_label = radial_pos // layer_cells
    swapped = jax.random.randint(key_swap, full_shape, 0, 4, dtype=jnp.int32) == 0
    replacement = jax.random.randint(key_other, full_shape, 0, LABELS, dtype=jnp.int32)
    anchored = radial_pos % layer_cells == 0
    return jnp.where(jnp.logical_and(swapped, jnp.logical_not(anchored)), replacement, base_label).astype(jnp.int32)


def plant(entries, stream_key, low, top_value):
    index_at = [jax.random.randint(jax.random.fold_in(stream_key, axis), (), 0, length) for axis, length in enumerate(entries.shape)]
    widest = entries.shape.index(max(entries.shape))
    next_to = index_at[:widest] + [(index_at[widest] + 1) % entries.shape[widest]] + index_at[widest + 1:]
    return entries.at[tuple(index_at)].set(low).at[tuple(next_to)].set(top_value)


def level_of(key, dims, pieces, low, top_value):
    level = 1.0
    for axis_at, blocks in pieces:
        heights = jax.random.uniform(jax.random.fold_in(jax.random.fold_in(key, 6), axis_at), (blocks,), jnp.float32, low / len(pieces), top_value / len(pieces))
        level = level * jnp.repeat(jnp.exp(heights), dims[axis_at] // blocks).reshape((-1,) + (1,) * (len(dims) - 1 - axis_at))
    return level


def noise(stream_key, extent, scale, limit, pieces=(), kind=jnp.bfloat16):
    values = jax.random.normal(stream_key, extent, jnp.float32) * scale
    if len(pieces) > 0:
        values = level_of(stream_key, extent, pieces, -0.22, 0.18) * values
    return jnp.clip(values, min=-limit, max=limit).astype(kind)


def setup_inputs(seed: int = 0) -> dict:
    seeds = jax.random.split(jax.random.key(seed), 5)
    right_side = noise(seeds[0], (NX, NY, NZ), 1.0, 6.0, ((0, 16), (1, 16)), jnp.float32)
    stiffness = jnp.clip(jnp.exp(math.log(0.3) - 2.3025852 * jax.random.uniform(seeds[1], (NX, NY, NZ), jnp.float32) ** level_of(seeds[1], (NX, NY, NZ), ((0, 16), (1, 16)), -0.2, 0.2)), 0.03, 0.3)
    material = plant(jax.random.randint(seeds[2], (NX, NY, NZ), 0, CLASSES), jax.random.fold_in(seeds[2], 1), 0, CLASSES - 1).astype(jnp.int32)
    groups = draw_groups(jax.random.fold_in(seeds[4], 71), 0)
    return {"right_side": right_side, "stiffness": stiffness, "material": material, "groups": groups}


MASS_SHIFT = 0.02
PRECISE = lax.Precision.HIGHEST
HALF_STEPS = ((0, 0, 1), (0, 1, -1), (0, 1, 0), (0, 1, 1), (1, -1, -1), (1, -1, 0), (1, -1, 1), (1, 0, -1), (1, 0, 0), (1, 0, 1), (1, 1, -1), (1, 1, 0), (1, 1, 1))

def coefficient_table():
    rows_out = []
    for material_id in range(CLASSES):
        fiber_angle = math.pi * (material_id % 8) / 8.0
        if material_id < 8:
            fiber_dir = (math.cos(fiber_angle), math.sin(fiber_angle), 0.0)
            strength, anisotropy = (1.0, 6.0)
        else:
            fiber_dir = (0.6 * math.cos(fiber_angle), 0.6 * math.sin(fiber_angle), 0.8)
            strength, anisotropy = (0.35, 2.0)
        line_values = []
        for offset in HALF_STEPS:
            length_sq = float(offset[0] * offset[0] + offset[1] * offset[1] + offset[2] * offset[2])
            along_fiber = fiber_dir[0] * offset[0] + fiber_dir[1] * offset[1] + fiber_dir[2] * offset[2]
            line_values.append(strength * (0.15 + anisotropy * along_fiber * along_fiber / length_sq) / length_sq)
        rows_out.append(line_values)
    return np.array(rows_out, dtype=np.float32)

def shift_radial(values_in, amount):
    if amount == 0:
        return values_in
    blank_edge = jnp.zeros(values_in.shape[:-1] + (1,), values_in.dtype)
    if amount > 0:
        return jnp.concatenate([values_in[..., 1:], blank_edge], axis=-1)
    return jnp.concatenate([blank_edge, values_in[..., :-1]], axis=-1)

def neighbour(padded, move_axial, move_circ, move_radial):
    rows_axial = padded.shape[-3] - 2
    rows_circ = padded.shape[-2] - 2
    window = padded[..., 1 + move_axial:1 + move_axial + rows_axial, 1 + move_circ:1 + move_circ + rows_circ, :]
    return shift_radial(window, move_radial)

def pad_plane(values_in):
    wrapped = jnp.concatenate([values_in[:, -1:], values_in, values_in[:, :1]], axis=1)
    blank_rows = jnp.zeros((1,) + wrapped.shape[1:], wrapped.dtype)
    return jnp.concatenate([blank_rows, wrapped, blank_rows], axis=0)

def edge_weights(stiff_pad, class_pad):
    coef_table = jnp.asarray(coefficient_table())
    weights = []
    diagonal = None
    for position, offset in enumerate(HALF_STEPS):
        coefficient = stiff_pad * coef_table[:, position][class_pad]
        centre = coefficient[1:-1, 1:-1]
        forward_weight = 0.5 * (centre + neighbour(coefficient, offset[0], offset[1], offset[2]))
        backward_weight = 0.5 * (centre + neighbour(coefficient, -offset[0], -offset[1], -offset[2]))
        weights.append((forward_weight, backward_weight))
        pair_sum = forward_weight + backward_weight
        diagonal = pair_sum if diagonal is None else diagonal + pair_sum
    return (weights, MASS_SHIFT + diagonal)

def stencil_apply(padded, weights, diagonal):
    result = diagonal * padded[1:-1, 1:-1]
    for position, offset in enumerate(HALF_STEPS):
        forward_weight, backward_weight = weights[position]
        result = result - forward_weight * neighbour(padded, offset[0], offset[1], offset[2])
        result = result - backward_weight * neighbour(padded, -offset[0], -offset[1], -offset[2])
    return result

def block_factor(diagonal_blocks, upper_blocks):
    block_size = diagonal_blocks.shape[1]
    identity = jnp.eye(block_size, dtype=jnp.float32)

    def advance(carried, inputs):
        inverse_prev, upper_prev = carried
        diagonal_now, upper_now = inputs
        coupling = jnp.dot(inverse_prev, upper_prev, precision=PRECISE)
        schur_block = diagonal_now - jnp.dot(coupling.T, coupling, precision=PRECISE)
        factor_now = jnp.linalg.cholesky(schur_block)
        inverse_now = lax.linalg.triangular_solve(factor_now, identity, left_side=True, lower=True)
        return ((inverse_now, upper_now), (inverse_now, coupling))
    start = (identity, jnp.zeros((block_size, block_size), jnp.float32))
    unused, (inverses, couplings) = lax.scan(advance, start, (diagonal_blocks, upper_blocks))
    return (inverses, couplings)

def coarse_solve(inverses, couplings, coarse_rhs):
    cycle_count, block_size = (inverses.shape[0], inverses.shape[1])
    parts = coarse_rhs.reshape(cycle_count, block_size)

    def forward(previous, members):
        inverse_now, coupling, part_now = members
        target = part_now - jnp.dot(coupling.T, previous, precision=PRECISE)
        solved = jnp.dot(inverse_now, target, precision=PRECISE)
        return (solved, solved)
    unused, middle = lax.scan(forward, jnp.zeros((block_size,), jnp.float32), (inverses, couplings, parts))
    couplings_next = jnp.concatenate([couplings[1:], jnp.zeros((1, block_size, block_size), jnp.float32)], axis=0)

    def backward(solved_next, members):
        inverse_now, coupling_next, middle_now = members
        target = middle_now - jnp.dot(coupling_next, solved_next, precision=PRECISE)
        solved = jnp.dot(inverse_now.T, target, precision=PRECISE)
        return (solved, solved)
    unused_last, solution_parts = lax.scan(backward, jnp.zeros((block_size,), jnp.float32), (inverses, couplings_next, middle), reverse=True)
    return solution_parts.reshape(-1)

def reference(right_side, stiffness, material, groups):
    cells_axial, cells_circ, cells_radial = right_side.shape
    rows_axial = cells_axial // N_AXIAL
    rows_circ = cells_circ // N_CIRC
    coarse_count = LABELS * N_AXIAL * N_CIRC
    block_size = LABELS * N_CIRC
    weights, diagonal = edge_weights(pad_plane(stiffness), pad_plane(material))
    owner_axial = jnp.arange(cells_axial, dtype=jnp.int32) // rows_axial
    owner_circ = jnp.arange(cells_circ, dtype=jnp.int32) // rows_circ
    owner_id = owner_axial[:, None] * N_CIRC + owner_circ[None, :]
    coarse_index = (owner_id[:, :, None] * LABELS + groups).astype(jnp.int32)
    index_pad = pad_plane(coarse_index)
    inside_pad = pad_plane(jnp.ones_like(right_side))
    stencil_terms = [((0, 0, 0), diagonal)]
    for position, offset in enumerate(HALF_STEPS):
        forward_weight, backward_weight = weights[position]
        stencil_terms.append((offset, -forward_weight))
        stencil_terms.append(((-offset[0], -offset[1], -offset[2]), -backward_weight))
    coarse_flat = jnp.zeros((coarse_count * coarse_count,), jnp.float32)
    for offset, entry_value in stencil_terms:
        column_ids = neighbour(index_pad, offset[0], offset[1], offset[2]).astype(jnp.int32)
        inside = neighbour(inside_pad, offset[0], offset[1], offset[2])
        flat_ids = (coarse_index * coarse_count + column_ids).astype(jnp.int32)
        coarse_flat = coarse_flat.at[flat_ids.reshape(-1)].add((entry_value * inside).reshape(-1))
    coarse_four = coarse_flat.reshape(N_AXIAL, block_size, N_AXIAL, block_size)
    cycle_ids = jnp.arange(N_AXIAL, dtype=jnp.int32)
    diagonal_blocks = coarse_four[cycle_ids, :, cycle_ids, :]
    upper_blocks = jnp.concatenate([coarse_four[cycle_ids[:-1], :, cycle_ids[1:], :], jnp.zeros((1, block_size, block_size), jnp.float32)], axis=0)
    inverses, couplings = block_factor(diagonal_blocks, upper_blocks)

    def project(field):
        return jax.ops.segment_sum(field.reshape(-1), coarse_index.reshape(-1), num_segments=coarse_count)

    def spread(coarse_rhs):
        return coarse_solve(inverses, couplings, coarse_rhs)[coarse_index]

    def apply_global(field):
        return stencil_apply(pad_plane(field), weights, diagonal)
    solution = spread(project(right_side))
    residual = right_side - apply_global(solution)
    residual_image = apply_global(residual)
    norm_now = jnp.sum(residual * residual)
    direction = residual - spread(project(residual_image))
    for iteration in range(ITERS):
        direction_image = apply_global(direction)
        step_length = norm_now / jnp.sum(direction * direction_image)
        solution = solution + step_length * direction
        residual = residual - step_length * direction_image
        if iteration + 1 < ITERS:
            residual_image = apply_global(residual)
            norm_next = jnp.sum(residual * residual)
            shifted = spread(project(residual_image))
            beta_ratio = norm_next / norm_now
            direction = beta_ratio * direction + residual - shifted
            norm_now = norm_next
    return (solution, residual)
```

```python
import math

import jax
import jax.numpy as jnp
import numpy as np
from jax import lax
from jax.experimental import pallas as pl
from jax.experimental.pallas import tpu as pltpu
from jax.sharding import Mesh
from jax.sharding import PartitionSpec as P

LABELS = 8
CLASSES = 16
CIRC = ("circ_0", "circ_1")
AXIAL = ("axial_0", "axial_1")
AXIAL_CIRC = ("axial_0", "axial_1", "circ_0", "circ_1")
MASS_SHIFT = 0.02
HIGH = lax.Precision.HIGHEST
HALF_STEPS = (
    (0, 0, 1),
    (0, 1, -1),
    (0, 1, 0),
    (0, 1, 1),
    (1, -1, -1),
    (1, -1, 0),
    (1, -1, 1),
    (1, 0, -1),
    (1, 0, 0),
    (1, 0, 1),
    (1, 1, -1),
    (1, 1, 0),
    (1, 1, 1),
)
STEP_OF = {step: place for place, step in enumerate(HALF_STEPS)}
SHIFTS = [(sy, sz) for sy in (-1, 0, 1) for sz in (-1, 0, 1)]
ROWS = 24
EDGE = 4
DEPTH = 3
BLOCK = 128
F32 = jnp.float32
BF16 = jnp.bfloat16


def coefficient_table():
    rows_out = []
    for material_id in range(CLASSES):
        fiber_angle = math.pi * (material_id % 8) / 8.0
        if material_id < 8:
            fiber_dir = (math.cos(fiber_angle), math.sin(fiber_angle), 0.0)
            strength, anisotropy = (1.0, 6.0)
        else:
            fiber_dir = (0.6 * math.cos(fiber_angle), 0.6 * math.sin(fiber_angle), 0.8)
            strength, anisotropy = (0.35, 2.0)
        line_values = []
        for offset in HALF_STEPS:
            length_sq = float(offset[0] * offset[0] + offset[1] * offset[1] + offset[2] * offset[2])
            along_fiber = (
                fiber_dir[0] * offset[0] + fiber_dir[1] * offset[1] + fiber_dir[2] * offset[2]
            )
            line_values.append(
                strength * (0.15 + anisotropy * along_fiber * along_fiber / length_sq) / length_sq
            )
        rows_out.append(line_values)
    return np.array(rows_out, dtype=np.float32)


def inverse_scales():
    table = coefficient_table().astype(np.float64)
    widest = MASS_SHIFT + 0.3 * (table.sum(axis=1).max() + table.max(axis=0).sum())
    low = 0.5 * MASS_SHIFT / widest
    scales = []
    while 1.0 - low > 2e-7:
        scales.append(2.0 / (1.0 + low))
        low = 4.0 * low / (1.0 + low) ** 2
    return scales


SCALES = inverse_scales()


def lanes(shape):
    return lax.broadcasted_iota(jnp.int32, shape, len(shape) - 1)


def sublanes(shape):
    return lax.broadcasted_iota(jnp.int32, shape, len(shape) - 2)


def shift_z(values, move, fill):
    if move == 0:
        return values
    length = values.shape[-1]
    turned = pltpu.roll(values, (-move) % length, axis=1)
    edge = length - 1 if move > 0 else 0
    return jnp.where(lanes(values.shape) == edge, fill, turned)


def shift_y(values, move):
    if move == 0:
        return values
    return pltpu.roll(values, (-move) % values.shape[0], axis=0)


def shifted(values, fill):
    by_z = {sz: shift_z(values, sz, fill) for sz in (-1, 0, 1)}
    return {(sy, sz): shift_y(by_z[sz], sy) for sy, sz in SHIFTS}


def present_flags(place_ref, plane):
    if plane < 0:
        return place_ref[0] > 0
    if plane > 7:
        return place_ref[0] < 15
    return None


def masked(values, flag):
    if flag is None:
        return values
    return values * jnp.where(flag, 1.0, 0.0).astype(F32)


def stencil(v_at, k_ref, diag_ref, start, stop, emit):
    wide = {}
    made = {}

    def prepare(plane):
        values = v_at(plane)
        wide[plane] = shifted(values, 0.0)
        made[plane] = [k_ref[plane + DEPTH, j] * values for j in range(13)]

    prepare(start - 1)
    prepare(start)
    for plane in range(start, stop):
        prepare(plane + 1)
        total = None
        for j, (ox, oy, oz) in enumerate(HALF_STEPS):
            pair = wide[plane + ox][(oy, oz)] + wide[plane - ox][(-oy, -oz)]
            term = k_ref[plane + DEPTH, j] * pair
            total = term if total is None else total + term
        for sz in (-1, 0, 1):
            by_y = None
            for sy in (-1, 0, 1):
                part = made[plane + 1][STEP_OF[(1, sy, sz)]] + made[plane - 1][STEP_OF[(1, -sy, -sz)]]
                if (0, sy, sz) in STEP_OF:
                    part = part + made[plane][STEP_OF[(0, sy, sz)]]
                elif (0, -sy, -sz) in STEP_OF:
                    part = part + made[plane][STEP_OF[(0, -sy, -sz)]]
                part = shift_y(part, sy)
                by_y = part if by_y is None else by_y + part
            total = total + shift_z(by_y, sz, 0.0)
        emit(plane, diag_ref[plane + 2] * wide[plane][(0, 0)] - 0.5 * total)
        del wide[plane - 1], made[plane - 1]


def piece(low_ref, mid_ref, high_ref, field, plane):
    if plane < 0:
        return low_ref[field, plane + DEPTH]
    if plane > 7:
        return high_ref[field, plane - 8]
    return mid_ref[field, plane]


def split3(values):
    high = values.astype(BF16)
    rest = values - high.astype(F32)
    mid = rest.astype(BF16)
    low = (rest - mid.astype(F32)).astype(BF16)
    return high, mid, low


def dot(a, b, dims=((1,), (0,))):
    return lax.dot_general(a, b, (dims, ((), ())), preferred_element_type=F32)


def dot_high(a, b, dims=((1,), (0,))):
    return lax.dot_general(
        a, b, (dims, ((), ())), precision=HIGH, preferred_element_type=F32
    )


def pick(values, chooser):
    return sum(dot(part, chooser) for part in split3(values))


def setup_kernel(low_ref, mid_ref, high_ref, table_ref, place_ref, k_ref, diag_ref, slot_ref, label_ref):
    for plane in range(-DEPTH, 8 + DEPTH):
        stiff = piece(low_ref, mid_ref, high_ref, 1, plane)
        kind = piece(low_ref, mid_ref, high_ref, 2, plane).astype(jnp.int32)
        for j in range(13):
            row = jnp.broadcast_to(table_ref[j : j + 1, :], (8, 128))
            parts = []
            for top in range(0, ROWS, 8):
                line = []
                for left in (0, 128):
                    line.append(
                        jnp.take_along_axis(
                            row,
                            kind[top : top + 8, left : left + 128],
                            axis=1,
                            mode="promise_in_bounds",
                        )
                    )
                parts.append(jnp.concatenate(line, axis=1))
            k_ref[plane + DEPTH, j] = stiff * jnp.concatenate(parts, axis=0)
    for plane in range(-2, 10):
        own = None
        total = None
        for j in range(13):
            term = k_ref[plane + DEPTH, j]
            own = term if own is None else own + term
        for sz in (-1, 0, 1):
            by_y = None
            for sy in (-1, 0, 1):
                part = k_ref[plane + 1 + DEPTH, STEP_OF[(1, sy, sz)]]
                part = part + k_ref[plane - 1 + DEPTH, STEP_OF[(1, -sy, -sz)]]
                if (0, sy, sz) in STEP_OF:
                    part = part + k_ref[plane + DEPTH, STEP_OF[(0, sy, sz)]]
                elif (0, -sy, -sz) in STEP_OF:
                    part = part + k_ref[plane + DEPTH, STEP_OF[(0, -sy, -sz)]]
                part = shift_y(part, sy)
                by_y = part if by_y is None else by_y + part
            by_y = shift_z(by_y, sz, 0.0)
            total = by_y if total is None else total + by_y
        diag_ref[plane + 2] = MASS_SHIFT + own + 0.5 * total
    for plane in range(0, 9):
        spots = shifted(piece(low_ref, mid_ref, high_ref, 3, plane), -1.0)
        for place, shift in enumerate(SHIFTS):
            label_ref[plane, place] = spots[shift][:16]
    row16 = sublanes((16, 256))
    sums = {}
    for plane in range(8):
        pairs = {"own": [], "up": [], "down": [], "next": [], "nextup": [], "nextdown": []}
        for j, (ox, oy, oz) in enumerate(HALF_STEPS):
            across = shift_z(shift_y(k_ref[plane + ox + DEPTH, j], oy), oz, 0.0)[:16]
            weight = -0.5 * (k_ref[plane + DEPTH, j, 0:16] + across)
            target = label_ref[plane + ox, SHIFTS.index((oy, oz))]
            outside = ox == 1 and plane == 7
            if oy == 0:
                pairs["next" if outside else "own"].append((weight, target))
            elif oy == 1:
                pairs["next" if outside else "own"].append((jnp.where(row16 == 15, 0.0, weight), target))
                pairs["nextup" if outside else "up"].append(
                    (jnp.where(row16 == 15, weight, 0.0)[8:], target[8:])
                )
            else:
                pairs["next" if outside else "own"].append((jnp.where(row16 == 0, 0.0, weight), target))
                pairs["nextdown" if outside else "down"].append(
                    (jnp.where(row16 == 0, weight, 0.0)[:8], target[:8])
                )
        home = label_ref[plane, SHIFTS.index((0, 0))]
        pairs["own"].append((0.5 * diag_ref[plane + 2, 0:16], home))
        load = mid_ref[0, plane, 0:16]

        def by_label(region):
            out = []
            for label in range(LABELS):
                total = None
                for weight, target in pairs[region]:
                    term = jnp.where(target == float(label), weight, 0.0)
                    total = term if total is None else total + term
                if total is None:
                    total = jnp.zeros((8, 256), F32)
                out.append(total)
            return out

        own = by_label("own")
        sides = (by_label("down"), by_label("up"))
        for half in (0, 1):
            rows = slice(8 * half, 8 * half + 8)
            chosen = jnp.concatenate(
                [jnp.where(home[rows] == float(k), 1.0, 0.0) for k in range(LABELS)], axis=0
            ).astype(BF16)
            right = jnp.concatenate([o[rows] for o in own] + [load[rows]] + sides[half], axis=0)
            got = sum(dot(chosen, part, ((1,), (1,))) for part in split3(right))
            sums[half] = got if half not in sums else sums[half] + got
            if plane == 7:
                if half == 0:
                    nexts = by_label("next")
                    corners = (by_label("nextdown"), by_label("nextup"))
                right = jnp.concatenate([o[rows] for o in nexts] + corners[half], axis=0)
                sums[2 + half] = sum(dot(chosen, part, ((1,), (1,))) for part in split3(right))

    def place_of(col, half, ahead):
        group = col // 8
        if ahead:
            side = 24 + (16 if half else 0)
            return jnp.where(group < 8, 24 + 8 + group, side + group - 8)
        side = 16 if half else 0
        return jnp.where(group < 8, 8 + group, jnp.where(group == 8, 48, side + group - 9))

    collected = None
    for which in range(4):
        width = sums[which].shape[1]
        shape = (64, width)
        kept = jnp.where(sublanes(shape) % 8 == lanes(shape) % 8, sums[which], 0.0)
        shape = (width, 128)
        chooser = jnp.where(
            lanes(shape) % 64 == place_of(sublanes(shape), which % 2, which >= 2), 1.0, 0.0
        )
        part = pick(kept, chooser.astype(BF16))
        collected = part if collected is None else collected + part
    shape = (64, 128)
    kept = jnp.where((sublanes(shape) // 8) % 2 == lanes(shape) // 64, collected, 0.0)
    shape = (8, 64)
    joiner = jnp.where(lanes(shape) // 16 == sublanes(shape) % 4, 1.0, 0.0).astype(BF16)
    slot = sum(dot(joiner, part) for part in split3(kept))
    for device in range(128):
        slot_ref[8 * device : 8 * device + 8, :] = slot


def coarse_rows(values, chooser):
    spread = pick(values, chooser)
    shape = (256, BLOCK)
    kept = jnp.where(sublanes(shape) % 16 == lanes(shape) % 16, spread, 0.0)
    return jnp.sum(kept.reshape(16, 16, BLOCK), axis=1)


def as_columns(rows):
    count = len(rows)
    stacked = jnp.concatenate(rows + [jnp.zeros((1, BLOCK), F32)] * (8 - count), axis=0)
    turned = stacked.T
    return [turned[:, i : i + 1] for i in range(count)]


def coarse_solve(coarse_rhs, right_ref, left_ref, last_ref):
    now = [coarse_rhs[i : i + 1, :] for i in range(16)]
    begin = 0
    stages = []
    while len(now) > 1:
        count = len(now)
        odd = now[1::2]
        even = now[0::2]
        solved = []
        for q, column in enumerate(as_columns(odd)):
            product = jnp.sum(right_ref[begin + q] * column, axis=0, keepdims=True)
            solved.append(product[:, :BLOCK])
            even[q] = even[q] - product[:, BLOCK : 2 * BLOCK]
            if q + 1 < len(even):
                even[q + 1] = even[q + 1] - product[:, 2 * BLOCK :]
        stages.append((begin, solved))
        begin += count // 2
        now = even
    (column,) = as_columns(now)
    found = [jnp.sum(last_ref[...] * column, axis=0, keepdims=True)]
    for begin, solved in reversed(stages):
        columns = as_columns(found)
        merged = []
        for q, value in enumerate(solved):
            value = value - jnp.sum(left_ref[begin + q, :BLOCK] * columns[q], axis=0, keepdims=True)
            if q + 1 < len(found):
                value = value - jnp.sum(
                    left_ref[begin + q, BLOCK:] * columns[q + 1], axis=0, keepdims=True
                )
            merged += [found[q], value]
        found = merged
    return jnp.concatenate(found, axis=0)


def split2(values):
    high = values.astype(BF16)
    return high, (values - high.astype(F32)).astype(BF16)


def dot_split(a, b):
    return dot(a[0], b[0]) + (dot(a[0], b[1]) + dot(a[1], b[0]))


def invert(blocks, scale_ref, s_ref, x_ref):
    shape = (BLOCK, BLOCK)
    eye = jnp.where(lanes(shape) == sublanes(shape), 1.0, 0.0).astype(F32)
    for q, block in enumerate(blocks):
        kept = eye * block
        across = 1.0 / jnp.sum(kept, axis=0, keepdims=True)
        down = 1.0 / jnp.sum(kept, axis=1, keepdims=True)
        c = 0.5 * SCALES[0]
        x_ref[q] = (2.0 * c * eye - (c * c) * (block * down)) * across
        high, low = split2(block)
        s_ref[q, 0] = high
        s_ref[q, 1] = low

    def step(k, carry):
        c = scale_ref[k]
        for q in range(len(blocks)):
            x = split2(x_ref[q])
            product = dot_split((s_ref[q, 0], s_ref[q, 1]), x)
            x_ref[q] = dot_split(x, split2((2.0 * c) * eye - (c * c) * product))
        return carry

    lax.fori_loop(1, len(SCALES) - 1, step, 0)
    out = []
    for q, block in enumerate(blocks):
        x = x_ref[q]
        left = eye - dot_high(block, x)
        out.append(x + dot_split(split2(x), split2(left)))
    return out


def factor_kernel(
    slots_ref, scale_ref, right_ref, left_ref, last_ref, y_ref, d_ref, b_ref, bt_ref, s_ref, x_ref
):
    shape = (256, BLOCK)
    device = sublanes(shape) % 16
    ring = lanes(shape) % 16
    near = [(device + c + 15) % 16 == ring for c in range(3)]
    coarse_rhs = None
    for pair in range(4):
        values = split3(slots_ref[pl.ds(pair, 256, stride=4), :])
        for half in (0, 1):
            label = 2 * pair + half
            shape = (128, 7 * BLOCK)
            group = lanes(shape) // BLOCK
            column = jnp.where(group < 6, group * 8 + (lanes(shape) % BLOCK) // 16, 48) + 64 * half
            chooser = jnp.where(sublanes(shape) == column, 1.0, 0.0).astype(BF16)
            wide = sum(dot(part, chooser) for part in values)
            for r, target in enumerate((d_ref, b_ref)):
                total = None
                for c in range(3):
                    at = (3 * r + c) * BLOCK
                    term = jnp.where(near[c], wide[:, at : at + BLOCK], 0.0)
                    total = term if total is None else total + term
                target[:, 16 * label : 16 * label + 16, :] = total.reshape(16, 16, BLOCK)
            mine = jnp.logical_and(device == ring, lanes((256, BLOCK)) // 16 == label)
            term = jnp.where(mine, wide[:, 6 * BLOCK :], 0.0)
            coarse_rhs = term if coarse_rhs is None else coarse_rhs + term
    coarse_rhs = jnp.sum(coarse_rhs.reshape(16, 16, BLOCK), axis=1)
    b_ref[15] = jnp.zeros((BLOCK, BLOCK), F32)
    for i in range(16):
        d_ref[i] = d_ref[i] + d_ref[i].T
        bt_ref[i] = b_ref[i].T
    begin = 0
    stride = 1
    while stride < 16:
        count = 8 // stride
        odd = [(2 * q + 1) * stride for q in range(count)]
        inverses = invert([d_ref[i] for i in odd], scale_ref, s_ref, x_ref)
        for q, i in enumerate(odd):
            before = i - stride
            after = i + stride
            inverse = inverses[q]
            c_rows = jnp.concatenate([b_ref[before], bt_ref[i]], axis=0)
            c_cols = jnp.concatenate([bt_ref[before], b_ref[i]], axis=1)
            left_ref[begin + q] = dot_high(c_rows, inverse)
            products = dot_high(inverse, c_cols)
            right_ref[begin + q, :, :BLOCK] = inverse
            right_ref[begin + q, :, BLOCK:] = products
            gram = dot_high(c_rows, products)
            d_ref[before] = d_ref[before] - gram[:BLOCK, :BLOCK]
            b_ref[before] = -gram[:BLOCK, BLOCK:]
            bt_ref[before] = -gram[BLOCK:, :BLOCK]
            if after < 16:
                d_ref[after] = d_ref[after] - gram[BLOCK:, BLOCK:]
        begin += count
        stride *= 2
    (last,) = invert([d_ref[0]], scale_ref, s_ref, x_ref)
    last_ref[...] = last
    y_ref[...] = coarse_solve(coarse_rhs, right_ref, left_ref, last_ref)


def spread_field(y_ref, place_ref, label_of, plane):
    axial = place_ref[0]
    if plane < 0:
        axial = jnp.maximum(axial - 1, 0)
    elif plane > 7:
        axial = jnp.minimum(axial + 1, 15)
    line = jnp.broadcast_to(y_ref[pl.ds(axial, 1), :], (8, BLOCK))
    ring = sublanes((ROWS, 256))
    move = jnp.where(ring < 16, 0, jnp.where(ring < 16 + EDGE, 1, 15))
    spot = label_of(plane).astype(jnp.int32) * 16 + (place_ref[1] + move) % 16
    parts = []
    for top in range(0, ROWS, 8):
        parts.append(
            jnp.concatenate(
                [
                    jnp.take_along_axis(
                        line,
                        spot[top : top + 8, left : left + 128],
                        axis=1,
                        mode="promise_in_bounds",
                    )
                    for left in (0, 128)
                ],
                axis=1,
            )
        )
    return masked(jnp.concatenate(parts, axis=0), present_flags(place_ref, plane))


def fold(values):
    half = values[:8] + values[8:]
    return half[:, :128] + half[:, 128:]


def slot_row(totals):
    count = len(totals)
    stacked = jnp.concatenate(totals, axis=0)
    shape = (8 * count, 128)
    sums = jnp.sum(stacked, axis=1, keepdims=True)
    kept = jnp.where(sublanes(shape) // 8 == lanes(shape), sums, 0.0)
    return jnp.sum(kept, axis=0, keepdims=True)


class Totals:
    def __init__(self, count):
        self.values = [None] * count

    def add(self, at, term):
        self.values[at] = term if self.values[at] is None else self.values[at] + term

    def by_label(self, labels, field):
        for k in range(LABELS):
            self.add(k, fold(jnp.where(labels == float(k), field, 0.0)))


def start_kernel(
    low_ref, mid_ref, high_ref, k_ref, diag_ref, y_ref, place_ref,
    x_out, r_out, image_ref, slot_ref, v_ref, w_ref,
):
    def label_of(plane):
        return piece(low_ref, mid_ref, high_ref, 3, plane)

    for plane in range(-3, 11):
        v_ref[plane + 3] = spread_field(y_ref, place_ref, label_of, plane)

    def put_residual(plane, image):
        load = piece(low_ref, mid_ref, high_ref, 0, plane)
        w_ref[plane + 2] = masked(load - image, present_flags(place_ref, plane))

    stencil(lambda plane: v_ref[plane + 3], k_ref, diag_ref, -2, 10, put_residual)
    totals = Totals(9)

    def put_image(plane, image):
        image_ref[plane + 1] = image
        if 0 <= plane < 8:
            totals.by_label(mid_ref[3, plane, 0:16], image[:16])
            own = w_ref[plane + 2, 0:16]
            totals.add(8, fold(own * own))

    stencil(lambda plane: w_ref[plane + 2], k_ref, diag_ref, -1, 9, put_image)
    for plane in range(8):
        x_out[plane] = v_ref[plane + 3, 0:16]
        r_out[plane] = w_ref[plane + 2, 0:16]
    slot_ref[...] = jnp.broadcast_to(slot_row(totals.values), (256, 128))


def label_chooser():
    shape = (128, BLOCK)
    return jnp.where(sublanes(shape) == lanes(shape) // 16, 1.0, 0.0).astype(BF16)


def first_kernel(
    got_ref, right_ref, left_ref, last_ref, low_ref, mid_ref, high_ref, k_ref, diag_ref, image_ref,
    r_ref, place_ref, w_out, d_out, aw_out, slot_ref, y_ref, v_ref, w_ref,
):
    got = got_ref[...]
    coarse_rhs = coarse_rows(got, label_chooser())
    y_ref[...] = coarse_solve(coarse_rhs, right_ref, left_ref, last_ref)

    def label_of(plane):
        return piece(low_ref, mid_ref, high_ref, 3, plane)

    for plane in range(-2, 10):
        v_ref[plane + 2] = spread_field(y_ref, place_ref, label_of, plane)
    totals = Totals(12)

    def put_direction_image(plane, image):
        w_ref[plane + 1] = masked(image_ref[plane + 1] - image, present_flags(place_ref, plane))

    stencil(lambda plane: v_ref[plane + 2], k_ref, diag_ref, -1, 9, put_direction_image)

    def put_second(plane, image):
        own = w_ref[plane + 1, 0:16]
        image = image[:16]
        residual = r_ref[plane]
        direction = residual - v_ref[plane + 2, 0:16]
        w_out[plane] = own
        d_out[plane] = direction
        aw_out[plane] = image
        totals.by_label(mid_ref[3, plane, 0:16], image)
        totals.add(8, fold(direction * own))
        totals.add(9, fold(own * own))
        totals.add(10, fold(residual * own))
        totals.add(11, fold(own * image))

    stencil(lambda plane: w_ref[plane + 1], k_ref, diag_ref, 0, 8, put_second)
    square = jnp.sum(got, axis=0, keepdims=True) * (1.0 / 256.0)
    shape = (1, 128)
    square = jnp.sum(jnp.where(lanes(shape) == 8, square, 0.0), axis=1, keepdims=True)
    row = slot_row(totals.values) + jnp.where(lanes(shape) == 12, square, 0.0)
    slot_ref[...] = jnp.broadcast_to(row, (256, 128))


def last_kernel(
    got_ref, right_ref, left_ref, last_ref, low_ref, mid_ref, high_ref, k_ref, diag_ref,
    x_ref, r_ref, w_ref, d_ref, aw_ref, place_ref, x_out, r_out, y_ref, v_ref,
):
    got = got_ref[...]
    coarse_rhs = coarse_rows(got, label_chooser())
    solved = coarse_solve(coarse_rhs, right_ref, left_ref, last_ref)
    y_ref[...] = solved
    row = jnp.sum(got, axis=0, keepdims=True)

    def scalar(at):
        return jnp.sum(jnp.where(lanes((1, 128)) == at, row, 0.0), axis=1, keepdims=True)

    dw, ww, rw, waw, rr = (scalar(at) for at in (8, 9, 10, 11, 12))
    hq = jnp.sum(jnp.sum(coarse_rhs * solved, axis=1, keepdims=True), axis=0, keepdims=True)
    alpha = rr / dw
    rr_next = rr - 2.0 * alpha * rw + alpha * alpha * ww
    beta = rr_next / rr
    gain = 1.0 + beta
    curvature = gain * gain * dw - 2.0 * gain * alpha * ww + alpha * alpha * (waw - hq)
    alpha_next = rr_next / curvature

    def label_of(plane):
        return piece(low_ref, mid_ref, high_ref, 3, plane)

    for plane in range(-1, 9):
        v_ref[plane + 1] = spread_field(y_ref, place_ref, label_of, plane)

    def put(plane, image):
        w = w_ref[plane]
        d = d_ref[plane]
        u = aw_ref[plane] - image[:16]
        d_next = gain * d - alpha * (w - v_ref[plane + 1, 0:16])
        w_next = gain * w - alpha * u
        x_out[plane] = x_ref[plane] + alpha * d + alpha_next * d_next
        r_out[plane] = r_ref[plane] - alpha * w - alpha_next * w_next

    stencil(lambda plane: v_ref[plane + 1], k_ref, diag_ref, 0, 8, put)


VMEM = pl.BlockSpec(memory_space=pltpu.VMEM)
SMEM = pl.BlockSpec(memory_space=pltpu.SMEM)
BIG = pltpu.CompilerParams(vmem_limit_bytes=56 * 1024 * 1024)


def shape_of(*dims):
    return jax.ShapeDtypeStruct(dims, F32)


def call(kernel, name, outs, scratch, in_specs):
    return pl.pallas_call(
        kernel,
        name=name,
        out_shape=outs,
        in_specs=in_specs,
        out_specs=tuple(VMEM for _ in outs),
        scratch_shapes=scratch,
        compiler_params=BIG,
    )


def ring_pairs(peers, wrap):
    up = [(i, (i + 1) % peers) for i in range(peers if wrap else peers - 1)]
    return up, [(j, i) for i, j in up]


def exchange(slots, count):
    return lax.all_to_all(slots.reshape(256, count, 128), AXIAL_CIRC, 0, 0, tiled=True).reshape(
        256 * count, 128
    )


def shards(right_side, stiffness, material, groups):
    place = jnp.stack([lax.axis_index(AXIAL), lax.axis_index(CIRC)]).astype(jnp.int32)
    fields = jnp.stack([right_side, stiffness, material.astype(F32), groups.astype(F32)])
    up, down = ring_pairs(16, True)
    before = lax.ppermute(fields[:, :, 16 - EDGE :], CIRC, up)
    after = lax.ppermute(fields[:, :, :EDGE], CIRC, down)
    middle = jnp.concatenate([fields, after, before], axis=2)
    up, down = ring_pairs(16, False)
    low = lax.ppermute(middle[:, 8 - DEPTH :], AXIAL, up)
    high = lax.ppermute(middle[:, :DEPTH], AXIAL, down)
    table = np.zeros((16, 128), np.float32)
    table[:13, :CLASSES] = coefficient_table().T
    ext = (ROWS, 256)
    k, diag, slots = call(
        setup_kernel,
        "setup",
        (shape_of(14, 13, *ext), shape_of(12, *ext), shape_of(1024, 128)),
        [pltpu.VMEM((9, 9, 16, 256), F32)],
        [VMEM, VMEM, VMEM, VMEM, SMEM],
    )(low, middle, high, jnp.asarray(table), place)
    gathered = exchange(slots, 4)
    square = (BLOCK, BLOCK)
    right, left, last, y = call(
        factor_kernel,
        "factor",
        (shape_of(15, BLOCK, 3 * BLOCK), shape_of(15, 2 * BLOCK, BLOCK), shape_of(*square), shape_of(16, BLOCK)),
        [
            pltpu.VMEM((16, *square), F32),
            pltpu.VMEM((16, *square), F32),
            pltpu.VMEM((16, *square), F32),
            pltpu.VMEM((8, 2, *square), BF16),
            pltpu.VMEM((8, *square), F32),
        ],
        [VMEM, SMEM],
    )(gathered, jnp.asarray(np.array(SCALES, np.float32)))
    own = (8, 16, 256)
    x0, r0, image, slots = call(
        start_kernel,
        "start",
        (shape_of(*own), shape_of(*own), shape_of(10, *ext), shape_of(256, 128)),
        [pltpu.VMEM((14, *ext), F32), pltpu.VMEM((12, *ext), F32)],
        [VMEM] * 6 + [SMEM],
    )(low, middle, high, k, diag, y, place)
    gathered = exchange(slots, 1)
    w0, d0, aw0, slots = call(
        first_kernel,
        "first",
        (shape_of(*own), shape_of(*own), shape_of(*own), shape_of(256, 128)),
        [pltpu.VMEM((16, BLOCK), F32), pltpu.VMEM((12, *ext), F32), pltpu.VMEM((10, *ext), F32)],
        [VMEM] * 11 + [SMEM],
    )(gathered, right, left, last, low, middle, high, k, diag, image, r0, place)
    gathered = exchange(slots, 1)
    return call(
        last_kernel,
        "last",
        (shape_of(*own), shape_of(*own)),
        [pltpu.VMEM((16, BLOCK), F32), pltpu.VMEM((10, *ext), F32)],
        [VMEM] * 14 + [SMEM],
    )(gathered, right, left, last, low, middle, high, k, diag, x0, r0, w0, d0, aw0, place)


def solution(mesh):
    split = Mesh(mesh.devices.reshape(8, 2, 4, 4), ("axial_0", "axial_1", "circ_0", "circ_1"))
    placed = P(AXIAL, CIRC, None)
    return jax.shard_map(
        shards,
        mesh=split,
        in_specs=(placed,) * 4,
        out_specs=(placed, placed),
        check_vma=False,
    )
```

```python
import math

import jax
import jax.numpy as jnp
import numpy as np
from jax import lax
from jax.experimental import pallas as pl
from jax.experimental.pallas import tpu as pltpu
from jax.sharding import Mesh
from jax.sharding import PartitionSpec as P

LABELS = 8
CLASSES = 16
CIRC = ("circ_0", "circ_1")
AXIAL = ("axial_0", "axial_1")
AXIAL_CIRC = ("axial_0", "axial_1", "circ_0", "circ_1")
MASS_SHIFT = 0.02
HIGH = lax.Precision.HIGHEST
HALF_STEPS = (
    (0, 0, 1),
    (0, 1, -1),
    (0, 1, 0),
    (0, 1, 1),
    (1, -1, -1),
    (1, -1, 0),
    (1, -1, 1),
    (1, 0, -1),
    (1, 0, 0),
    (1, 0, 1),
    (1, 1, -1),
    (1, 1, 0),
    (1, 1, 1),
)
STEP_OF = {step: place for place, step in enumerate(HALF_STEPS)}
SHIFTS = [(sy, sz) for sy in (-1, 0, 1) for sz in (-1, 0, 1)]
ROWS = 24
EDGE = 4
DEPTH = 3
BLOCK = 128
F32 = jnp.float32
BF16 = jnp.bfloat16


def coefficient_table():
    rows_out = []
    for material_id in range(CLASSES):
        fiber_angle = math.pi * (material_id % 8) / 8.0
        if material_id < 8:
            fiber_dir = (math.cos(fiber_angle), math.sin(fiber_angle), 0.0)
            strength, anisotropy = (1.0, 6.0)
        else:
            fiber_dir = (0.6 * math.cos(fiber_angle), 0.6 * math.sin(fiber_angle), 0.8)
            strength, anisotropy = (0.35, 2.0)
        line_values = []
        for offset in HALF_STEPS:
            length_sq = float(offset[0] * offset[0] + offset[1] * offset[1] + offset[2] * offset[2])
            along_fiber = (
                fiber_dir[0] * offset[0] + fiber_dir[1] * offset[1] + fiber_dir[2] * offset[2]
            )
            line_values.append(
                strength * (0.15 + anisotropy * along_fiber * along_fiber / length_sq) / length_sq
            )
        rows_out.append(line_values)
    return np.array(rows_out, dtype=np.float32)


def inverse_scales():
    table = coefficient_table().astype(np.float64)
    widest = MASS_SHIFT + 0.3 * (table.sum(axis=1).max() + table.max(axis=0).sum())
    low = 0.5 * MASS_SHIFT / widest
    scales = []
    while 1.0 - low > 2e-7:
        scales.append(2.0 / (1.0 + low))
        low = 4.0 * low / (1.0 + low) ** 2
    return scales


SCALES = inverse_scales()


def lanes(shape):
    return lax.broadcasted_iota(jnp.int32, shape, len(shape) - 1)


def sublanes(shape):
    return lax.broadcasted_iota(jnp.int32, shape, len(shape) - 2)


def shift_z(values, move, fill):
    if move == 0:
        return values
    length = values.shape[-1]
    turned = pltpu.roll(values, (-move) % length, axis=1)
    edge = length - 1 if move > 0 else 0
    return jnp.where(lanes(values.shape) == edge, fill, turned)


def shift_y(values, move):
    if move == 0:
        return values
    return pltpu.roll(values, (-move) % values.shape[0], axis=0)


def shifted(values, fill):
    by_z = {sz: shift_z(values, sz, fill) for sz in (-1, 0, 1)}
    return {(sy, sz): shift_y(by_z[sz], sy) for sy, sz in SHIFTS}


def present_flags(place_ref, plane):
    if plane < 0:
        return place_ref[0] > 0
    if plane > 7:
        return place_ref[0] < 15
    return None


def masked(values, flag):
    if flag is None:
        return values
    return values * jnp.where(flag, 1.0, 0.0).astype(F32)


def stencil(v_at, k_ref, diag_ref, start, stop, emit):
    wide = {}
    made = {}

    def prepare(plane):
        values = v_at(plane)
        wide[plane] = shifted(values, 0.0)
        made[plane] = [k_ref[plane + DEPTH, j] * values for j in range(13)]

    prepare(start - 1)
    prepare(start)
    for plane in range(start, stop):
        prepare(plane + 1)
        total = None
        for j, (ox, oy, oz) in enumerate(HALF_STEPS):
            pair = wide[plane + ox][(oy, oz)] + wide[plane - ox][(-oy, -oz)]
            term = k_ref[plane + DEPTH, j] * pair
            total = term if total is None else total + term
        for sz in (-1, 0, 1):
            by_y = None
            for sy in (-1, 0, 1):
                part = made[plane + 1][STEP_OF[(1, sy, sz)]] + made[plane - 1][STEP_OF[(1, -sy, -sz)]]
                if (0, sy, sz) in STEP_OF:
                    part = part + made[plane][STEP_OF[(0, sy, sz)]]
                elif (0, -sy, -sz) in STEP_OF:
                    part = part + made[plane][STEP_OF[(0, -sy, -sz)]]
                part = shift_y(part, sy)
                by_y = part if by_y is None else by_y + part
            total = total + shift_z(by_y, sz, 0.0)
        emit(plane, diag_ref[plane + 2] * wide[plane][(0, 0)] - 0.5 * total)
        del wide[plane - 1], made[plane - 1]


def piece(low_ref, mid_ref, high_ref, field, plane):
    if plane < 0:
        return low_ref[field, plane + DEPTH]
    if plane > 7:
        return high_ref[field, plane - 8]
    return mid_ref[field, plane]


def split3(values):
    high = values.astype(BF16)
    rest = values - high.astype(F32)
    mid = rest.astype(BF16)
    low = (rest - mid.astype(F32)).astype(BF16)
    return high, mid, low


def dot(a, b, dims=((1,), (0,))):
    return lax.dot_general(a, b, (dims, ((), ())), preferred_element_type=F32)


def dot_high(a, b, dims=((1,), (0,))):
    return lax.dot_general(
        a, b, (dims, ((), ())), precision=HIGH, preferred_element_type=F32
    )


def pick(values, chooser):
    return sum(dot(part, chooser) for part in split3(values))


def setup_kernel(low_ref, mid_ref, high_ref, table_ref, place_ref, k_ref, diag_ref, slot_ref, label_ref):
    for plane in range(-DEPTH, 8 + DEPTH):
        stiff = masked(piece(low_ref, mid_ref, high_ref, 1, plane), present_flags(place_ref, plane))
        kind = piece(low_ref, mid_ref, high_ref, 2, plane).astype(jnp.int32)
        for j in range(13):
            row = jnp.broadcast_to(table_ref[j : j + 1, :], (8, 128))
            parts = []
            for top in range(0, ROWS, 8):
                line = []
                for left in (0, 128):
                    line.append(
                        jnp.take_along_axis(
                            row,
                            kind[top : top + 8, left : left + 128],
                            axis=1,
                            mode="promise_in_bounds",
                        )
                    )
                parts.append(jnp.concatenate(line, axis=1))
            k_ref[plane + DEPTH, j] = stiff * jnp.concatenate(parts, axis=0)
    for plane in range(-2, 10):
        own = None
        total = None
        for j in range(13):
            term = k_ref[plane + DEPTH, j]
            own = term if own is None else own + term
        for sz in (-1, 0, 1):
            by_y = None
            for sy in (-1, 0, 1):
                part = k_ref[plane + 1 + DEPTH, STEP_OF[(1, sy, sz)]]
                part = part + k_ref[plane - 1 + DEPTH, STEP_OF[(1, -sy, -sz)]]
                if (0, sy, sz) in STEP_OF:
                    part = part + k_ref[plane + DEPTH, STEP_OF[(0, sy, sz)]]
                elif (0, -sy, -sz) in STEP_OF:
                    part = part + k_ref[plane + DEPTH, STEP_OF[(0, -sy, -sz)]]
                part = shift_y(part, sy)
                by_y = part if by_y is None else by_y + part
            by_y = shift_z(by_y, sz, 0.0)
            total = by_y if total is None else total + by_y
        diag_ref[plane + 2] = MASS_SHIFT + own + 0.5 * total
    for plane in range(0, 9):
        spots = shifted(piece(low_ref, mid_ref, high_ref, 3, plane), -1.0)
        for place, shift in enumerate(SHIFTS):
            label_ref[plane, place] = spots[shift][:16]
    row16 = sublanes((16, 256))
    sums = {}
    for plane in range(8):
        pairs = {"own": [], "up": [], "down": [], "next": [], "nextup": [], "nextdown": []}
        for j, (ox, oy, oz) in enumerate(HALF_STEPS):
            across = shift_z(shift_y(k_ref[plane + ox + DEPTH, j], oy), oz, 0.0)[:16]
            weight = -0.5 * (k_ref[plane + DEPTH, j, 0:16] + across)
            target = label_ref[plane + ox, SHIFTS.index((oy, oz))]
            outside = ox == 1 and plane == 7
            if oy == 0:
                pairs["next" if outside else "own"].append((weight, target))
            elif oy == 1:
                pairs["next" if outside else "own"].append((jnp.where(row16 == 15, 0.0, weight), target))
                pairs["nextup" if outside else "up"].append(
                    (jnp.where(row16 == 15, weight, 0.0)[8:], target[8:])
                )
            else:
                pairs["next" if outside else "own"].append((jnp.where(row16 == 0, 0.0, weight), target))
                pairs["nextdown" if outside else "down"].append(
                    (jnp.where(row16 == 0, weight, 0.0)[:8], target[:8])
                )
        home = label_ref[plane, SHIFTS.index((0, 0))]
        pairs["own"].append((0.5 * diag_ref[plane + 2, 0:16], home))
        load = mid_ref[0, plane, 0:16]

        def by_label(region):
            out = []
            for label in range(LABELS):
                total = None
                for weight, target in pairs[region]:
                    term = jnp.where(target == float(label), weight, 0.0)
                    total = term if total is None else total + term
                if total is None:
                    total = jnp.zeros((8, 256), F32)
                out.append(total)
            return out

        own = by_label("own")
        sides = (by_label("down"), by_label("up"))
        for half in (0, 1):
            rows = slice(8 * half, 8 * half + 8)
            chosen = jnp.concatenate(
                [jnp.where(home[rows] == float(k), 1.0, 0.0) for k in range(LABELS)], axis=0
            ).astype(BF16)
            right = jnp.concatenate([o[rows] for o in own] + [load[rows]] + sides[half], axis=0)
            got = sum(dot(chosen, part, ((1,), (1,))) for part in split3(right))
            sums[half] = got if half not in sums else sums[half] + got
            if plane == 7:
                if half == 0:
                    nexts = by_label("next")
                    corners = (by_label("nextdown"), by_label("nextup"))
                right = jnp.concatenate([o[rows] for o in nexts] + corners[half], axis=0)
                sums[2 + half] = sum(dot(chosen, part, ((1,), (1,))) for part in split3(right))

    def place_of(col, half, ahead):
        group = col // 8
        if ahead:
            side = 24 + (16 if half else 0)
            return jnp.where(group < 8, 24 + 8 + group, side + group - 8)
        side = 16 if half else 0
        return jnp.where(group < 8, 8 + group, jnp.where(group == 8, 48, side + group - 9))

    collected = None
    for which in range(4):
        width = sums[which].shape[1]
        shape = (64, width)
        kept = jnp.where(sublanes(shape) % 8 == lanes(shape) % 8, sums[which], 0.0)
        shape = (width, 128)
        chooser = jnp.where(
            lanes(shape) % 64 == place_of(sublanes(shape), which % 2, which >= 2), 1.0, 0.0
        )
        part = pick(kept, chooser.astype(BF16))
        collected = part if collected is None else collected + part
    shape = (64, 128)
    kept = jnp.where((sublanes(shape) // 8) % 2 == lanes(shape) // 64, collected, 0.0)
    shape = (8, 64)
    joiner = jnp.where(lanes(shape) // 16 == sublanes(shape) % 4, 1.0, 0.0).astype(BF16)
    slot = sum(dot(joiner, part) for part in split3(kept))
    for device in range(8):
        slot_ref[8 * device : 8 * device + 8, :] = slot


def coarse_rows(values, chooser):
    spread = pick(values, chooser)
    shape = (256, BLOCK)
    kept = jnp.where(sublanes(shape) % 16 == lanes(shape) % 16, spread, 0.0)
    return jnp.sum(kept.reshape(16, 16, BLOCK), axis=1)


def as_columns(rows):
    count = len(rows)
    stacked = jnp.concatenate(rows + [jnp.zeros((1, BLOCK), F32)] * (8 - count), axis=0)
    turned = stacked.T
    return [turned[:, i : i + 1] for i in range(count)]


def coarse_solve(coarse_rhs, right_ref, left_ref, last_ref):
    now = [coarse_rhs[i : i + 1, :] for i in range(16)]
    begin = 0
    stages = []
    while len(now) > 1:
        count = len(now)
        odd = now[1::2]
        even = now[0::2]
        solved = []
        for q, column in enumerate(as_columns(odd)):
            product = jnp.sum(right_ref[begin + q] * column, axis=0, keepdims=True)
            solved.append(product[:, :BLOCK])
            even[q] = even[q] - product[:, BLOCK : 2 * BLOCK]
            if q + 1 < len(even):
                even[q + 1] = even[q + 1] - product[:, 2 * BLOCK :]
        stages.append((begin, solved))
        begin += count // 2
        now = even
    (column,) = as_columns(now)
    found = [jnp.sum(last_ref[...] * column, axis=0, keepdims=True)]
    for begin, solved in reversed(stages):
        columns = as_columns(found)
        merged = []
        for q, value in enumerate(solved):
            value = value - jnp.sum(left_ref[begin + q, :BLOCK] * columns[q], axis=0, keepdims=True)
            if q + 1 < len(found):
                value = value - jnp.sum(
                    left_ref[begin + q, BLOCK:] * columns[q + 1], axis=0, keepdims=True
                )
            merged += [found[q], value]
        found = merged
    return jnp.concatenate(found, axis=0)


def split2(values):
    high = values.astype(BF16)
    return high, (values - high.astype(F32)).astype(BF16)


def left_stack(values):
    high, low = split2(values)
    return jnp.concatenate([high, high, low], axis=1)


def right_stack(values):
    high, low = split2(values)
    return jnp.concatenate([high, low, high], axis=0)


def invert(blocks, scale_ref, x_ref, p_ref):
    shape = (BLOCK, BLOCK)
    eye = jnp.where(lanes(shape) == sublanes(shape), 1.0, 0.0).astype(F32)
    for q, block in enumerate(blocks):
        kept = eye * block
        across = 1.0 / jnp.sum(kept, axis=0, keepdims=True)
        down = 1.0 / jnp.sum(kept, axis=1, keepdims=True)
        c = 0.5 * SCALES[0]
        x_ref[q] = (2.0 * c * eye - (c * c) * (block * down)) * across
    for q, block in enumerate(blocks):
        p_ref[q] = dot(left_stack(block), right_stack(x_ref[q]))

    def step(k, carry):
        c = scale_ref[k]
        for q in range(len(blocks)):
            x = x_ref[q]
            p = p_ref[q]
            both = jnp.concatenate([left_stack(p), left_stack(x)], axis=0)
            product = dot(both, right_stack(p))
            p_ref[q] = (2.0 * c) * p - (c * c) * product[:BLOCK]
            x_ref[q] = (2.0 * c) * x - (c * c) * product[BLOCK:]
        return carry

    lax.fori_loop(1, len(SCALES) - 2, step, 0)
    values = [x_ref[q] for q in range(len(blocks))]
    rests = [eye - dot(left_stack(s), right_stack(x)) for s, x in zip(blocks, values)]
    values = [x + dot(x.astype(BF16), r.astype(BF16)) for x, r in zip(values, rests)]
    rests = [eye - dot_high(s, x) for s, x in zip(blocks, values)]
    return [x + dot(x.astype(BF16), r.astype(BF16)) for x, r in zip(values, rests)]


def turned(values):
    shape = (BLOCK, BLOCK)
    eye = jnp.where(lanes(shape) == sublanes(shape), 1.0, 0.0).astype(BF16)
    return sum(dot(eye, part, ((1,), (1,))) for part in split3(values))


def gather_lanes(values, spot):
    return jnp.take_along_axis(values, spot, axis=1, mode="promise_in_bounds")


def unpack_coarse(slots_ref, d_ref, b_ref, f_ref):
    for top in (0, 8):
        shape = (8, BLOCK)
        device = sublanes(shape) + top
        ring = lanes(shape) % 16
        column = lanes(shape) // 16
        side = (ring - device + 17) % 16
        near = side < 3
        spot = jnp.minimum(side, 2) * 8 + column
        for s in range(16):
            load = None
            for pair in range(4):
                values = slots_ref[pl.ds(64 * top + 4 * s + pair, 8, stride=64), :]
                for half in (0, 1):
                    row = 16 * (2 * pair + half) + top
                    for r, target in enumerate((d_ref, b_ref)):
                        if r == 1 and s == 15:
                            continue
                        got = gather_lanes(values, spot + (64 * half + 24 * r))
                        target[s, row : row + 8, :] = jnp.where(near, got, 0.0)
                got = gather_lanes(values, 48 + 64 * (column % 2))
                mine = jnp.logical_and(ring == device, column // 2 == pair)
                term = jnp.where(mine, got, 0.0)
                load = term if load is None else load + term
            load = jnp.sum(load, axis=0, keepdims=True)
            if top == 0:
                f_ref[s : s + 1, :] = load
            else:
                f_ref[s : s + 1, :] = f_ref[s : s + 1, :] + load


def factor_kernel(
    slots_ref, scale_ref, right_ref, left_ref, last_ref, y_ref, d_ref, b_ref, x_ref, p_ref, f_ref
):
    unpack_coarse(slots_ref, d_ref, b_ref, f_ref)
    b_ref[15] = jnp.zeros((BLOCK, BLOCK), F32)
    for i in range(16):
        d_ref[i] = d_ref[i] + turned(d_ref[i])
    begin = 0
    stride = 1
    while stride < 16:
        count = 8 // stride
        odd = [(2 * q + 1) * stride for q in range(count)]
        inverses = invert([d_ref[i] for i in odd], scale_ref, x_ref, p_ref)
        ups = [
            dot_high(inverse, b_ref[i - stride], ((1,), (1,))) for i, inverse in zip(odd, inverses)
        ]
        downs = [dot_high(inverse, b_ref[i]) for i, inverse in zip(odd, inverses)]
        products = [jnp.concatenate(pair, axis=1) for pair in zip(ups, downs)]
        for q in range(count):
            right_ref[begin + q, :, :BLOCK] = inverses[q]
            right_ref[begin + q, :, BLOCK:] = products[q]
        grams = [dot_high(b_ref[i - stride], product) for i, product in zip(odd, products)]
        for q in range(count):
            left_ref[begin + q, :BLOCK, :] = turned(ups[q])
            left_ref[begin + q, BLOCK:, :] = turned(downs[q])
        afters = [
            dot_high(left_ref[begin + q, BLOCK:, :], b_ref[i])
            for q, i in enumerate(odd)
            if i + stride < 16
        ]
        for q, i in enumerate(odd):
            change = grams[q][:, :BLOCK]
            if q > 0:
                change = change + afters[q - 1]
            d_ref[i - stride] = d_ref[i - stride] - change
            b_ref[i - stride] = -grams[q][:, BLOCK:]
        begin += count
        stride *= 2
    (last,) = invert([d_ref[0]], scale_ref, x_ref, p_ref)
    last_ref[...] = last
    y_ref[...] = coarse_solve(f_ref[...], right_ref, left_ref, last_ref)


def spread_field(y_ref, place_ref, label_of, plane):
    axial = place_ref[0]
    if plane < 0:
        axial = jnp.maximum(axial - 1, 0)
    elif plane > 7:
        axial = jnp.minimum(axial + 1, 15)
    line = jnp.broadcast_to(y_ref[pl.ds(axial, 1), :], (8, BLOCK))
    ring = sublanes((ROWS, 256))
    move = jnp.where(ring < 16, 0, jnp.where(ring < 16 + EDGE, 1, 15))
    spot = label_of(plane).astype(jnp.int32) * 16 + (place_ref[1] + move) % 16
    parts = []
    for top in range(0, ROWS, 8):
        parts.append(
            jnp.concatenate(
                [
                    jnp.take_along_axis(
                        line,
                        spot[top : top + 8, left : left + 128],
                        axis=1,
                        mode="promise_in_bounds",
                    )
                    for left in (0, 128)
                ],
                axis=1,
            )
        )
    return masked(jnp.concatenate(parts, axis=0), present_flags(place_ref, plane))


def fold(values):
    half = values[:8] + values[8:]
    return half[:, :128] + half[:, 128:]


def slot_row(totals):
    count = len(totals)
    stacked = jnp.concatenate(totals, axis=0)
    shape = (8 * count, 128)
    sums = jnp.sum(stacked, axis=1, keepdims=True)
    kept = jnp.where(sublanes(shape) // 8 == lanes(shape), sums, 0.0)
    return jnp.sum(kept, axis=0, keepdims=True)


class Totals:
    def __init__(self, count):
        self.values = [None] * count

    def add(self, at, term):
        self.values[at] = term if self.values[at] is None else self.values[at] + term

    def by_label(self, labels, field):
        for k in range(LABELS):
            self.add(k, fold(jnp.where(labels == float(k), field, 0.0)))


def start_kernel(
    low_ref, mid_ref, high_ref, k_ref, diag_ref, y_ref, place_ref,
    x_out, r_out, image_ref, slot_ref, v_ref, w_ref,
):
    def label_of(plane):
        return piece(low_ref, mid_ref, high_ref, 3, plane)

    for plane in range(-3, 11):
        v_ref[plane + 3] = spread_field(y_ref, place_ref, label_of, plane)

    def put_residual(plane, image):
        load = piece(low_ref, mid_ref, high_ref, 0, plane)
        w_ref[plane + 2] = masked(load - image, present_flags(place_ref, plane))

    stencil(lambda plane: v_ref[plane + 3], k_ref, diag_ref, -2, 10, put_residual)
    totals = Totals(9)

    def put_image(plane, image):
        image_ref[plane + 1] = image
        if 0 <= plane < 8:
            totals.by_label(mid_ref[3, plane, 0:16], image[:16])
            own = w_ref[plane + 2, 0:16]
            totals.add(8, fold(own * own))

    stencil(lambda plane: w_ref[plane + 2], k_ref, diag_ref, -1, 9, put_image)
    for plane in range(8):
        x_out[plane] = v_ref[plane + 3, 0:16]
        r_out[plane] = w_ref[plane + 2, 0:16]
    slot_ref[...] = jnp.broadcast_to(slot_row(totals.values), (256, 128))


def label_chooser():
    shape = (128, BLOCK)
    return jnp.where(sublanes(shape) == lanes(shape) // 16, 1.0, 0.0).astype(BF16)


def first_kernel(
    got_ref, right_ref, left_ref, last_ref, low_ref, mid_ref, high_ref, k_ref, diag_ref, image_ref,
    r_ref, place_ref, w_out, d_out, aw_out, slot_ref, y_ref, v_ref, w_ref,
):
    got = got_ref[...]
    coarse_rhs = coarse_rows(got, label_chooser())
    y_ref[...] = coarse_solve(coarse_rhs, right_ref, left_ref, last_ref)

    def label_of(plane):
        return piece(low_ref, mid_ref, high_ref, 3, plane)

    for plane in range(-2, 10):
        v_ref[plane + 2] = spread_field(y_ref, place_ref, label_of, plane)
    totals = Totals(12)

    def put_direction_image(plane, image):
        w_ref[plane + 1] = masked(image_ref[plane + 1] - image, present_flags(place_ref, plane))

    stencil(lambda plane: v_ref[plane + 2], k_ref, diag_ref, -1, 9, put_direction_image)

    def put_second(plane, image):
        own = w_ref[plane + 1, 0:16]
        image = image[:16]
        residual = r_ref[plane]
        direction = residual - v_ref[plane + 2, 0:16]
        w_out[plane] = own
        d_out[plane] = direction
        aw_out[plane] = image
        totals.by_label(mid_ref[3, plane, 0:16], image)
        totals.add(8, fold(direction * own))
        totals.add(9, fold(own * own))
        totals.add(10, fold(residual * own))
        totals.add(11, fold(own * image))

    stencil(lambda plane: w_ref[plane + 1], k_ref, diag_ref, 0, 8, put_second)
    square = jnp.sum(got, axis=0, keepdims=True) * (1.0 / 256.0)
    shape = (1, 128)
    square = jnp.sum(jnp.where(lanes(shape) == 8, square, 0.0), axis=1, keepdims=True)
    row = slot_row(totals.values) + jnp.where(lanes(shape) == 12, square, 0.0)
    slot_ref[...] = jnp.broadcast_to(row, (256, 128))


def last_kernel(
    got_ref, right_ref, left_ref, last_ref, low_ref, mid_ref, high_ref, k_ref, diag_ref,
    x_ref, r_ref, w_ref, d_ref, aw_ref, place_ref, x_out, r_out, y_ref, v_ref,
):
    got = got_ref[...]
    coarse_rhs = coarse_rows(got, label_chooser())
    solved = coarse_solve(coarse_rhs, right_ref, left_ref, last_ref)
    y_ref[...] = solved
    row = jnp.sum(got, axis=0, keepdims=True)

    def scalar(at):
        return jnp.sum(jnp.where(lanes((1, 128)) == at, row, 0.0), axis=1, keepdims=True)

    dw, ww, rw, waw, rr = (scalar(at) for at in (8, 9, 10, 11, 12))
    hq = jnp.sum(jnp.sum(coarse_rhs * solved, axis=1, keepdims=True), axis=0, keepdims=True)
    alpha = rr / dw
    rr_next = rr - 2.0 * alpha * rw + alpha * alpha * ww
    beta = rr_next / rr
    gain = 1.0 + beta
    curvature = gain * gain * dw - 2.0 * gain * alpha * ww + alpha * alpha * (waw - hq)
    alpha_next = rr_next / curvature

    def label_of(plane):
        return piece(low_ref, mid_ref, high_ref, 3, plane)

    for plane in range(-1, 9):
        v_ref[plane + 1] = spread_field(y_ref, place_ref, label_of, plane)

    def put(plane, image):
        w = w_ref[plane]
        d = d_ref[plane]
        u = aw_ref[plane] - image[:16]
        d_next = gain * d - alpha * (w - v_ref[plane + 1, 0:16])
        w_next = gain * w - alpha * u
        x_out[plane] = x_ref[plane] + alpha * d + alpha_next * d_next
        r_out[plane] = r_ref[plane] - alpha * w - alpha_next * w_next

    stencil(lambda plane: v_ref[plane + 1], k_ref, diag_ref, 0, 8, put)


VMEM = pl.BlockSpec(memory_space=pltpu.VMEM)
SMEM = pl.BlockSpec(memory_space=pltpu.SMEM)


def shape_of(*dims):
    return jax.ShapeDtypeStruct(dims, F32)


def call(kernel, name, outs, scratch, in_specs, mib):
    return pl.pallas_call(
        kernel,
        name=name,
        out_shape=outs,
        in_specs=in_specs,
        out_specs=tuple(VMEM for _ in outs),
        scratch_shapes=scratch,
        compiler_params=pltpu.CompilerParams(vmem_limit_bytes=mib * 1024 * 1024),
    )


def ring_pairs(peers):
    up = [(i, (i + 1) % peers) for i in range(peers)]
    return up, [(j, i) for i, j in up]


def exchange_all(slots, count):
    width = slots.shape[0] // 16
    held = lax.all_to_all(slots.reshape(16, width, 128), AXIAL, 0, 0, tiled=True)
    held = jnp.broadcast_to(held.reshape(1, 16 * width, 128), (16, 16 * width, 128))
    return lax.all_to_all(held, CIRC, 0, 0, tiled=True).reshape(256 * width, 128)


def exchange(slots, count):
    return lax.all_to_all(slots.reshape(256, count, 128), AXIAL_CIRC, 0, 0, tiled=True).reshape(
        256 * count, 128
    )


def shards(right_side, stiffness, material, groups):
    place = jnp.stack([lax.axis_index(AXIAL), lax.axis_index(CIRC)]).astype(jnp.int32)
    fields = jnp.stack([right_side, stiffness, material.astype(F32), groups.astype(F32)])
    up, down = ring_pairs(16)
    before = lax.ppermute(fields[:, :, 16 - EDGE :], CIRC, up)
    after = lax.ppermute(fields[:, :, :EDGE], CIRC, down)
    middle = jnp.concatenate([fields, after, before], axis=2)
    low = lax.ppermute(middle[:, 8 - DEPTH :], AXIAL, up)
    high = lax.ppermute(middle[:, :DEPTH], AXIAL, down)
    table = np.zeros((16, 128), np.float32)
    table[:13, :CLASSES] = coefficient_table().T
    ext = (ROWS, 256)
    k, diag, slots = call(
        setup_kernel,
        "setup",
        (shape_of(14, 13, *ext), shape_of(12, *ext), shape_of(64, 128)),
        [pltpu.VMEM((9, 9, 16, 256), F32)],
        [VMEM, VMEM, VMEM, VMEM, SMEM],
        24,
    )(low, middle, high, jnp.asarray(table), place)
    gathered = exchange_all(slots, 4)
    square = (BLOCK, BLOCK)
    right, left, last, y = call(
        factor_kernel,
        "factor",
        (shape_of(15, BLOCK, 3 * BLOCK), shape_of(15, 2 * BLOCK, BLOCK), shape_of(*square), shape_of(16, BLOCK)),
        [
            pltpu.VMEM((16, *square), F32),
            pltpu.VMEM((16, *square), F32),
            pltpu.VMEM((8, *square), F32),
            pltpu.VMEM((8, *square), F32),
            pltpu.VMEM((16, BLOCK), F32),
        ],
        [VMEM, SMEM],
        24,
    )(gathered, jnp.asarray(np.array(SCALES, np.float32)))
    own = (8, 16, 256)
    x0, r0, image, slots = call(
        start_kernel,
        "start",
        (shape_of(*own), shape_of(*own), shape_of(10, *ext), shape_of(256, 128)),
        [pltpu.VMEM((14, *ext), F32), pltpu.VMEM((12, *ext), F32)],
        [VMEM] * 6 + [SMEM],
        24,
    )(low, middle, high, k, diag, y, place)
    gathered = exchange(slots, 1)
    w0, d0, aw0, slots = call(
        first_kernel,
        "first",
        (shape_of(*own), shape_of(*own), shape_of(*own), shape_of(256, 128)),
        [pltpu.VMEM((16, BLOCK), F32), pltpu.VMEM((12, *ext), F32), pltpu.VMEM((10, *ext), F32)],
        [VMEM] * 11 + [SMEM],
        24,
    )(gathered, right, left, last, low, middle, high, k, diag, image, r0, place)
    gathered = exchange(slots, 1)
    return call(
        last_kernel,
        "last",
        (shape_of(*own), shape_of(*own)),
        [pltpu.VMEM((16, BLOCK), F32), pltpu.VMEM((10, *ext), F32)],
        [VMEM] * 14 + [SMEM],
        24,
    )(gathered, right, left, last, low, middle, high, k, diag, x0, r0, w0, d0, aw0, place)


def solution(mesh):
    split = Mesh(mesh.devices.reshape(8, 2, 4, 4), ("axial_0", "axial_1", "circ_0", "circ_1"))
    placed = P(AXIAL, CIRC, None)
    return jax.shard_map(
        shards,
        mesh=split,
        in_specs=(placed,) * 4,
        out_specs=(placed, placed),
        check_vma=False,
    )
```

```python
import math

import jax
import jax.numpy as jnp
import numpy as np
from jax import lax
from jax.experimental import pallas as pl
from jax.experimental.pallas import tpu as pltpu
from jax.sharding import Mesh
from jax.sharding import PartitionSpec as P

LABELS = 8
CLASSES = 16
CIRC = ("circ_0", "circ_1")
AXIAL = ("axial_0", "axial_1")
AXIAL_CIRC = ("axial_0", "axial_1", "circ_0", "circ_1")
MASS_SHIFT = 0.02
HIGH = lax.Precision.HIGHEST
HALF_STEPS = (
    (0, 0, 1),
    (0, 1, -1),
    (0, 1, 0),
    (0, 1, 1),
    (1, -1, -1),
    (1, -1, 0),
    (1, -1, 1),
    (1, 0, -1),
    (1, 0, 0),
    (1, 0, 1),
    (1, 1, -1),
    (1, 1, 0),
    (1, 1, 1),
)
STEP_OF = {step: place for place, step in enumerate(HALF_STEPS)}
SHIFTS = [(sy, sz) for sy in (-1, 0, 1) for sz in (-1, 0, 1)]
ROWS = 24
EDGE = 4
DEPTH = 3
BLOCK = 128
F32 = jnp.float32
BF16 = jnp.bfloat16


def coefficient_table():
    rows_out = []
    for material_id in range(CLASSES):
        fiber_angle = math.pi * (material_id % 8) / 8.0
        if material_id < 8:
            fiber_dir = (math.cos(fiber_angle), math.sin(fiber_angle), 0.0)
            strength, anisotropy = (1.0, 6.0)
        else:
            fiber_dir = (0.6 * math.cos(fiber_angle), 0.6 * math.sin(fiber_angle), 0.8)
            strength, anisotropy = (0.35, 2.0)
        line_values = []
        for offset in HALF_STEPS:
            length_sq = float(offset[0] * offset[0] + offset[1] * offset[1] + offset[2] * offset[2])
            along_fiber = (
                fiber_dir[0] * offset[0] + fiber_dir[1] * offset[1] + fiber_dir[2] * offset[2]
            )
            line_values.append(
                strength * (0.15 + anisotropy * along_fiber * along_fiber / length_sq) / length_sq
            )
        rows_out.append(line_values)
    return np.array(rows_out, dtype=np.float32)


def inverse_scales():
    table = coefficient_table().astype(np.float64)
    widest = MASS_SHIFT + 0.3 * (table.sum(axis=1).max() + table.max(axis=0).sum())
    low = 0.5 * MASS_SHIFT / widest
    scales, lows = [], []
    while 1.0 - low > 2e-7:
        scales.append(2.0 / (1.0 + low))
        lows.append(low)
        low = 4.0 * low / (1.0 + low) ** 2
    return scales, lows


SCALES, LOWS = inverse_scales()


def lanes(shape):
    return lax.broadcasted_iota(jnp.int32, shape, len(shape) - 1)


def sublanes(shape):
    return lax.broadcasted_iota(jnp.int32, shape, len(shape) - 2)


def shift_z(values, move, fill):
    if move == 0:
        return values
    length = values.shape[-1]
    turned = pltpu.roll(values, (-move) % length, axis=1)
    edge = length - 1 if move > 0 else 0
    return jnp.where(lanes(values.shape) == edge, fill, turned)


def shift_y(values, move):
    if move == 0:
        return values
    return pltpu.roll(values, (-move) % values.shape[0], axis=0)


def shifted(values, fill):
    by_z = {sz: shift_z(values, sz, fill) for sz in (-1, 0, 1)}
    return {(sy, sz): shift_y(by_z[sz], sy) for sy, sz in SHIFTS}


def present_flags(place_ref, plane):
    if plane < 0:
        return place_ref[0] > 0
    if plane > 7:
        return place_ref[0] < 15
    return None


def masked(values, flag):
    if flag is None:
        return values
    return values * jnp.where(flag, 1.0, 0.0).astype(F32)


def stencil(v_at, k_ref, diag_ref, start, stop, emit):
    wide = {}
    made = {}

    def prepare(plane):
        values = v_at(plane)
        wide[plane] = shifted(values, 0.0)
        made[plane] = [k_ref[plane + DEPTH, j] * values for j in range(13)]

    prepare(start - 1)
    prepare(start)
    for plane in range(start, stop):
        prepare(plane + 1)
        total = None
        for j, (ox, oy, oz) in enumerate(HALF_STEPS):
            pair = wide[plane + ox][(oy, oz)] + wide[plane - ox][(-oy, -oz)]
            term = k_ref[plane + DEPTH, j] * pair
            total = term if total is None else total + term
        for sz in (-1, 0, 1):
            by_y = None
            for sy in (-1, 0, 1):
                part = made[plane + 1][STEP_OF[(1, sy, sz)]] + made[plane - 1][STEP_OF[(1, -sy, -sz)]]
                if (0, sy, sz) in STEP_OF:
                    part = part + made[plane][STEP_OF[(0, sy, sz)]]
                elif (0, -sy, -sz) in STEP_OF:
                    part = part + made[plane][STEP_OF[(0, -sy, -sz)]]
                part = shift_y(part, sy)
                by_y = part if by_y is None else by_y + part
            total = total + shift_z(by_y, sz, 0.0)
        emit(plane, diag_ref[plane + 2] * wide[plane][(0, 0)] - 0.5 * total)
        del wide[plane - 1], made[plane - 1]


def piece(low_ref, mid_ref, high_ref, field, plane):
    if plane < 0:
        return low_ref[field, plane + DEPTH]
    if plane > 7:
        return high_ref[field, plane - 8]
    return mid_ref[field, plane]


def split3(values):
    high = values.astype(BF16)
    rest = values - high.astype(F32)
    mid = rest.astype(BF16)
    low = (rest - mid.astype(F32)).astype(BF16)
    return high, mid, low


def dot(a, b, dims=((1,), (0,))):
    return lax.dot_general(a, b, (dims, ((), ())), preferred_element_type=F32)


def dot_high(a, b, dims=((1,), (0,))):
    return lax.dot_general(
        a, b, (dims, ((), ())), precision=HIGH, preferred_element_type=F32
    )


def pick(values, chooser):
    return sum(dot(part, chooser) for part in split3(values))


def setup_kernel(low_ref, mid_ref, high_ref, table_ref, place_ref, k_ref, diag_ref, slot_ref, label_ref):
    for plane in range(-DEPTH, 8 + DEPTH):
        stiff = masked(piece(low_ref, mid_ref, high_ref, 1, plane), present_flags(place_ref, plane))
        kind = piece(low_ref, mid_ref, high_ref, 2, plane).astype(jnp.int32)
        for j in range(13):
            row = jnp.broadcast_to(table_ref[j : j + 1, :], (8, 128))
            parts = []
            for top in range(0, ROWS, 8):
                line = []
                for left in (0, 128):
                    line.append(
                        jnp.take_along_axis(
                            row,
                            kind[top : top + 8, left : left + 128],
                            axis=1,
                            mode="promise_in_bounds",
                        )
                    )
                parts.append(jnp.concatenate(line, axis=1))
            k_ref[plane + DEPTH, j] = stiff * jnp.concatenate(parts, axis=0)
    for plane in range(-2, 10):
        own = None
        total = None
        for j in range(13):
            term = k_ref[plane + DEPTH, j]
            own = term if own is None else own + term
        for sz in (-1, 0, 1):
            by_y = None
            for sy in (-1, 0, 1):
                part = k_ref[plane + 1 + DEPTH, STEP_OF[(1, sy, sz)]]
                part = part + k_ref[plane - 1 + DEPTH, STEP_OF[(1, -sy, -sz)]]
                if (0, sy, sz) in STEP_OF:
                    part = part + k_ref[plane + DEPTH, STEP_OF[(0, sy, sz)]]
                elif (0, -sy, -sz) in STEP_OF:
                    part = part + k_ref[plane + DEPTH, STEP_OF[(0, -sy, -sz)]]
                part = shift_y(part, sy)
                by_y = part if by_y is None else by_y + part
            by_y = shift_z(by_y, sz, 0.0)
            total = by_y if total is None else total + by_y
        diag_ref[plane + 2] = MASS_SHIFT + own + 0.5 * total
    for plane in range(0, 9):
        spots = shifted(piece(low_ref, mid_ref, high_ref, 3, plane), -1.0)
        for place, shift in enumerate(SHIFTS):
            label_ref[plane, place] = spots[shift][:16]
    row16 = sublanes((16, 256))
    sums = {}
    for plane in range(8):
        pairs = {"own": [], "up": [], "next": [], "nextup": [], "nextdown": []}
        for j, (ox, oy, oz) in enumerate(HALF_STEPS):
            across = shift_z(shift_y(k_ref[plane + ox + DEPTH, j], oy), oz, 0.0)[:16]
            weight = -0.5 * (k_ref[plane + DEPTH, j, 0:16] + across)
            target = label_ref[plane + ox, SHIFTS.index((oy, oz))]
            outside = ox == 1 and plane == 7
            if oy == 0:
                pairs["next" if outside else "own"].append((weight, target))
            elif oy == 1:
                pairs["next" if outside else "own"].append((jnp.where(row16 == 15, 0.0, weight), target))
                pairs["nextup" if outside else "up"].append(
                    (jnp.where(row16 == 15, weight, 0.0)[8:], target[8:])
                )
            else:
                pairs["next" if outside else "own"].append((jnp.where(row16 == 0, 0.0, weight), target))
                if outside:
                    pairs["nextdown"].append((jnp.where(row16 == 0, weight, 0.0)[:8], target[:8]))
                if plane > 0:
                    back = shift_z(shift_y(k_ref[plane - 1 + DEPTH, j], -oy), -oz, 0.0)[8:16]
                    back = -0.5 * (k_ref[plane + DEPTH, j, 8:16] + back)
                    source = label_ref[plane - 1, SHIFTS.index((-oy, -oz)), 8:16]
                    pairs["up"].append((jnp.where(row16[8:] == 15, back, 0.0), source))
        home = label_ref[plane, SHIFTS.index((0, 0))]
        pairs["own"].append((0.5 * diag_ref[plane + 2, 0:16], home))
        load = mid_ref[0, plane, 0:16]

        def by_label(region):
            out = []
            for label in range(LABELS):
                total = None
                for weight, target in pairs[region]:
                    term = jnp.where(target == float(label), weight, 0.0)
                    total = term if total is None else total + term
                if total is None:
                    total = jnp.zeros((8, 256), F32)
                out.append(total)
            return out

        own = by_label("own")
        sides = ([], by_label("up"))
        ones = jnp.ones((8, 256), F32)
        for half in (0, 1):
            rows = slice(8 * half, 8 * half + 8)
            chosen = jnp.concatenate(
                [jnp.where(home[rows] == float(k), 1.0, 0.0) for k in range(LABELS)], axis=0
            ).astype(BF16)
            right = jnp.concatenate([o[rows] for o in own] + [load[rows], ones] + sides[half], axis=0)
            got = sum(dot(chosen, part, ((1,), (1,))) for part in split3(right))
            sums[half] = got if half not in sums else sums[half] + got
            if plane == 7:
                if half == 0:
                    nexts = by_label("next")
                    corners = (by_label("nextdown"), by_label("nextup"))
                right = jnp.concatenate([o[rows] for o in nexts] + corners[half], axis=0)
                sums[2 + half] = sum(dot(chosen, part, ((1,), (1,))) for part in split3(right))

    total = None
    for which in range(4):
        width = sums[which].shape[1]
        shape = (64, width)
        kept = jnp.where(sublanes(shape) % 8 == lanes(shape) % 8, sums[which], 0.0)
        shape = (width, 3 * 128)
        group = sublanes(shape) // 8
        if which < 2:
            spot = jnp.where(group < 8, group, jnp.where(group < 10, 32 + group, group - 2))
        else:
            spot = jnp.where(group < 8, 24 + group, (8 if which == 2 else 24) + group)
        here = (lanes(shape) // 128) * 16 + lanes(shape) % 16
        part = pick(kept, jnp.where(here == spot, 1.0, 0.0).astype(BF16))
        total = part if total is None else total + part
    shape = (64, 3 * 128)
    total = jnp.where(sublanes(shape) // 8 == (lanes(shape) % 128) // 16, total, 0.0)
    total = jnp.sum(total, axis=0, keepdims=True)
    rows = [total[:, 128 * r : 128 * r + 128] for r in range(3)]
    slots = jnp.concatenate(rows * 8, axis=0)
    slot_ref[0:24, :] = slots
    slot_ref[24:48, :] = slots


def coarse_rows(values, chooser):
    spread = pick(values, chooser)
    shape = (256, BLOCK)
    kept = jnp.where(sublanes(shape) % 16 == lanes(shape) % 16, spread, 0.0)
    return jnp.sum(kept.reshape(16, 16, BLOCK), axis=1)


def as_columns(rows):
    count = len(rows)
    stacked = jnp.concatenate(rows + [jnp.zeros((1, BLOCK), F32)] * (8 - count), axis=0)
    turned = stacked.T
    return [turned[:, i : i + 1] for i in range(count)]


def coarse_solve(coarse_rhs, right_ref, left_ref, last_ref):
    now = [coarse_rhs[i : i + 1, :] for i in range(16)]
    begin = 0
    stages = []
    while len(now) > 1:
        count = len(now)
        odd = now[1::2]
        even = now[0::2]
        solved = []
        for q, column in enumerate(as_columns(odd)):
            product = jnp.sum(right_ref[begin + q] * column, axis=0, keepdims=True)
            solved.append(product[:, :BLOCK])
            even[q] = even[q] - product[:, BLOCK : 2 * BLOCK]
            if q + 1 < len(even):
                even[q + 1] = even[q + 1] - product[:, 2 * BLOCK :]
        stages.append((begin, solved))
        begin += count // 2
        now = even
    (column,) = as_columns(now)
    found = [jnp.sum(last_ref[...] * column, axis=0, keepdims=True)]
    for begin, solved in reversed(stages):
        columns = as_columns(found)
        merged = []
        for q, value in enumerate(solved):
            value = value - jnp.sum(left_ref[begin + q, :BLOCK] * columns[q], axis=0, keepdims=True)
            if q + 1 < len(found):
                value = value - jnp.sum(
                    left_ref[begin + q, BLOCK:] * columns[q + 1], axis=0, keepdims=True
                )
            merged += [found[q], value]
        found = merged
    return jnp.concatenate(found, axis=0)


def split2(values):
    high = values.astype(BF16)
    return high, (values - high.astype(F32)).astype(BF16)


def left_stack(halves):
    high, low = halves
    return jnp.concatenate([high, high, low], axis=1)


def right_stack(halves):
    high, low = halves
    return jnp.concatenate([high, low, high], axis=0)


def invert(blocks, begin, scale_ref, x_ref, p_ref):
    shape = (BLOCK, BLOCK)
    eye = jnp.where(lanes(shape) == sublanes(shape), 1.0, 0.0).astype(F32)
    for q, block in enumerate(blocks):
        kept = eye * block
        across = 1.0 / jnp.sum(kept, axis=0, keepdims=True)
        down = 1.0 / jnp.sum(kept, axis=1, keepdims=True)
        c = 0.5 * scale_ref[begin]
        x_ref[q] = (2.0 * c * eye - (c * c) * (block * down)) * across
    for q, block in enumerate(blocks):
        p_ref[q] = dot(left_stack(split2(block)), right_stack(split2(x_ref[q])))

    def step(k, carry):
        c = scale_ref[k]
        for q in range(len(blocks)):
            x = x_ref[q]
            p = p_ref[q]
            halves = split2(p)
            both = jnp.concatenate([left_stack(halves), left_stack(split2(x))], axis=0)
            product = dot(both, right_stack(halves))
            p_ref[q] = (2.0 * c) * p - (c * c) * product[:BLOCK]
            x_ref[q] = (2.0 * c) * x - (c * c) * product[BLOCK:]
        return carry

    lax.fori_loop(begin + 1, len(SCALES) - 2, step, 0)
    values = [x_ref[q] for q in range(len(blocks))]
    rests = [
        eye - dot(left_stack(split2(s)), right_stack(split2(x))) for s, x in zip(blocks, values)
    ]
    values = [x + dot(x.astype(BF16), r.astype(BF16)) for x, r in zip(values, rests)]
    rests = [eye - dot_high(s, x) for s, x in zip(blocks, values)]
    return [x + dot(x.astype(BF16), r.astype(BF16)) for x, r in zip(values, rests)]


def turned(values):
    shape = (BLOCK, BLOCK)
    eye = jnp.where(lanes(shape) == sublanes(shape), 1.0, 0.0).astype(BF16)
    return sum(dot(eye, part, ((1,), (1,))) for part in split3(values))


def gather_lanes(values, spot):
    return jnp.take_along_axis(values, spot, axis=1, mode="promise_in_bounds")


def unpack_coarse(slots_ref, d_ref, b_ref, f_ref, n_ref):
    for top in (0, 8):
        shape = (8, BLOCK)
        device = sublanes(shape) + top
        ring = lanes(shape) % 16
        column = lanes(shape) // 16
        ahead = (ring - device + 16) % 16
        side = (ahead + 1) % 16
        home = jnp.minimum(ahead, 1) * 8 + column
        cross = jnp.minimum(side, 1) * 8 + column
        for s in range(16):
            at = 48 * top + 3 * s
            rows = [slots_ref[pl.ds(at + r, 8, stride=48), :] for r in range(3)]
            for label in range(LABELS):
                row = 16 * label + top
                got = gather_lanes(rows[0], home + 16 * label)
                d_ref[s, row : row + 8, :] = jnp.where(ahead < 2, got, 0.0)
                if s < 15:
                    got = jnp.where(
                        side < 2,
                        gather_lanes(rows[1], cross + 16 * label),
                        gather_lanes(rows[2], column + 16 * label),
                    )
                    b_ref[s, row : row + 8, :] = jnp.where(side < 3, got, 0.0)
            for place, target in ((8, f_ref), (9, n_ref)):
                got = jnp.where(ring == device, gather_lanes(rows[2], 16 * column + place), 0.0)
                total = jnp.sum(got, axis=0, keepdims=True)
                if top > 0:
                    total = target[s : s + 1, :] + total
                target[s : s + 1, :] = total


def first_step(d_ref, n_ref):
    shape = (BLOCK, BLOCK)
    eye = lanes(shape) == sublanes(shape)
    diagonal = jnp.concatenate(
        [jnp.sum(jnp.where(eye, d_ref[s], 0.0), axis=0, keepdims=True) for s in range(16)], axis=0
    )
    low = jnp.min((0.5 * MASS_SHIFT) * n_ref[...] / diagonal)
    return sum(jnp.where(low >= bound, 1, 0).astype(jnp.int32) for bound in LOWS[1:-2])


def factor_kernel(
    slots_ref, scale_ref, right_ref, left_ref, last_ref, y_ref, d_ref, b_ref, x_ref, p_ref, f_ref, n_ref
):
    unpack_coarse(slots_ref, d_ref, b_ref, f_ref, n_ref)
    b_ref[15] = jnp.zeros((BLOCK, BLOCK), F32)
    for i in range(16):
        d_ref[i] = d_ref[i] + turned(d_ref[i])
    first = first_step(d_ref, n_ref)
    begin = 0
    stride = 1
    while stride < 16:
        count = 8 // stride
        odd = [(2 * q + 1) * stride for q in range(count)]
        inverses = invert([d_ref[i] for i in odd], first, scale_ref, x_ref, p_ref)
        ups = [
            dot_high(inverse, b_ref[i - stride], ((1,), (1,))) for i, inverse in zip(odd, inverses)
        ]
        downs = [dot_high(inverse, b_ref[i]) for i, inverse in zip(odd, inverses)]
        products = [jnp.concatenate(pair, axis=1) for pair in zip(ups, downs)]
        for q in range(count):
            right_ref[begin + q, :, :BLOCK] = inverses[q]
            right_ref[begin + q, :, BLOCK:] = products[q]
        grams = [dot_high(b_ref[i - stride], product) for i, product in zip(odd, products)]
        for q in range(count):
            left_ref[begin + q, :BLOCK, :] = turned(ups[q])
            left_ref[begin + q, BLOCK:, :] = turned(downs[q])
        afters = [
            dot_high(left_ref[begin + q, BLOCK:, :], b_ref[i])
            for q, i in enumerate(odd)
            if i + stride < 16
        ]
        for q, i in enumerate(odd):
            change = grams[q][:, :BLOCK]
            if q > 0:
                change = change + afters[q - 1]
            d_ref[i - stride] = d_ref[i - stride] - change
            b_ref[i - stride] = -grams[q][:, BLOCK:]
        begin += count
        stride *= 2
    (last,) = invert([d_ref[0]], first, scale_ref, x_ref, p_ref)
    last_ref[...] = last
    y_ref[...] = coarse_solve(f_ref[...], right_ref, left_ref, last_ref)


def spread_field(y_ref, place_ref, label_of, plane):
    axial = place_ref[0]
    if plane < 0:
        axial = jnp.maximum(axial - 1, 0)
    elif plane > 7:
        axial = jnp.minimum(axial + 1, 15)
    line = jnp.broadcast_to(y_ref[pl.ds(axial, 1), :], (8, BLOCK))
    ring = sublanes((ROWS, 256))
    move = jnp.where(ring < 16, 0, jnp.where(ring < 16 + EDGE, 1, 15))
    spot = label_of(plane).astype(jnp.int32) * 16 + (place_ref[1] + move) % 16
    parts = []
    for top in range(0, ROWS, 8):
        parts.append(
            jnp.concatenate(
                [
                    jnp.take_along_axis(
                        line,
                        spot[top : top + 8, left : left + 128],
                        axis=1,
                        mode="promise_in_bounds",
                    )
                    for left in (0, 128)
                ],
                axis=1,
            )
        )
    return masked(jnp.concatenate(parts, axis=0), present_flags(place_ref, plane))


def fold(values):
    half = values[:8] + values[8:]
    return half[:, :128] + half[:, 128:]


def slot_row(totals):
    count = len(totals)
    stacked = jnp.concatenate(totals, axis=0)
    shape = (8 * count, 128)
    sums = jnp.sum(stacked, axis=1, keepdims=True)
    kept = jnp.where(sublanes(shape) // 8 == lanes(shape), sums, 0.0)
    return jnp.sum(kept, axis=0, keepdims=True)


class Totals:
    def __init__(self, count):
        self.values = [None] * count

    def add(self, at, term):
        self.values[at] = term if self.values[at] is None else self.values[at] + term

    def by_label(self, labels, field):
        for k in range(LABELS):
            self.add(k, fold(jnp.where(labels == float(k), field, 0.0)))


def start_kernel(
    low_ref, mid_ref, high_ref, k_ref, diag_ref, y_ref, place_ref,
    x_out, r_out, image_ref, slot_ref, v_ref, w_ref,
):
    def label_of(plane):
        return piece(low_ref, mid_ref, high_ref, 3, plane)

    for plane in range(-3, 11):
        v_ref[plane + 3] = spread_field(y_ref, place_ref, label_of, plane)

    def put_residual(plane, image):
        load = piece(low_ref, mid_ref, high_ref, 0, plane)
        w_ref[plane + 2] = masked(load - image, present_flags(place_ref, plane))

    stencil(lambda plane: v_ref[plane + 3], k_ref, diag_ref, -2, 10, put_residual)
    totals = Totals(9)

    def put_image(plane, image):
        image_ref[plane + 1] = image
        if 0 <= plane < 8:
            totals.by_label(mid_ref[3, plane, 0:16], image[:16])
            own = w_ref[plane + 2, 0:16]
            totals.add(8, fold(own * own))

    stencil(lambda plane: w_ref[plane + 2], k_ref, diag_ref, -1, 9, put_image)
    for plane in range(8):
        x_out[plane] = v_ref[plane + 3, 0:16]
        r_out[plane] = w_ref[plane + 2, 0:16]
    slot_ref[...] = jnp.broadcast_to(slot_row(totals.values), (256, 128))


def label_chooser():
    shape = (128, BLOCK)
    return jnp.where(sublanes(shape) == lanes(shape) // 16, 1.0, 0.0).astype(BF16)


def first_kernel(
    got_ref, right_ref, left_ref, last_ref, low_ref, mid_ref, high_ref, k_ref, diag_ref, image_ref,
    r_ref, place_ref, w_out, d_out, aw_out, slot_ref, y_ref, v_ref, w_ref,
):
    got = got_ref[...]
    coarse_rhs = coarse_rows(got, label_chooser())
    y_ref[...] = coarse_solve(coarse_rhs, right_ref, left_ref, last_ref)

    def label_of(plane):
        return piece(low_ref, mid_ref, high_ref, 3, plane)

    for plane in range(-2, 10):
        v_ref[plane + 2] = spread_field(y_ref, place_ref, label_of, plane)
    totals = Totals(12)

    def put_direction_image(plane, image):
        w_ref[plane + 1] = masked(image_ref[plane + 1] - image, present_flags(place_ref, plane))

    stencil(lambda plane: v_ref[plane + 2], k_ref, diag_ref, -1, 9, put_direction_image)

    def put_second(plane, image):
        own = w_ref[plane + 1, 0:16]
        image = image[:16]
        residual = r_ref[plane]
        direction = residual - v_ref[plane + 2, 0:16]
        w_out[plane] = own
        d_out[plane] = direction
        aw_out[plane] = image
        totals.by_label(mid_ref[3, plane, 0:16], image)
        totals.add(8, fold(direction * own))
        totals.add(9, fold(own * own))
        totals.add(10, fold(residual * own))
        totals.add(11, fold(own * image))

    stencil(lambda plane: w_ref[plane + 1], k_ref, diag_ref, 0, 8, put_second)
    square = jnp.sum(got, axis=0, keepdims=True) * (1.0 / 256.0)
    shape = (1, 128)
    square = jnp.sum(jnp.where(lanes(shape) == 8, square, 0.0), axis=1, keepdims=True)
    row = slot_row(totals.values) + jnp.where(lanes(shape) == 12, square, 0.0)
    slot_ref[...] = jnp.broadcast_to(row, (256, 128))


def last_kernel(
    got_ref, right_ref, left_ref, last_ref, low_ref, mid_ref, high_ref, k_ref, diag_ref,
    x_ref, r_ref, w_ref, d_ref, aw_ref, place_ref, x_out, r_out, y_ref, v_ref,
):
    got = got_ref[...]
    coarse_rhs = coarse_rows(got, label_chooser())
    solved = coarse_solve(coarse_rhs, right_ref, left_ref, last_ref)
    y_ref[...] = solved
    row = jnp.sum(got, axis=0, keepdims=True)

    def scalar(at):
        return jnp.sum(jnp.where(lanes((1, 128)) == at, row, 0.0), axis=1, keepdims=True)

    dw, ww, rw, waw, rr = (scalar(at) for at in (8, 9, 10, 11, 12))
    hq = jnp.sum(jnp.sum(coarse_rhs * solved, axis=1, keepdims=True), axis=0, keepdims=True)
    alpha = rr / dw
    rr_next = rr - 2.0 * alpha * rw + alpha * alpha * ww
    beta = rr_next / rr
    gain = 1.0 + beta
    curvature = gain * gain * dw - 2.0 * gain * alpha * ww + alpha * alpha * (waw - hq)
    alpha_next = rr_next / curvature

    def label_of(plane):
        return piece(low_ref, mid_ref, high_ref, 3, plane)

    for plane in range(-1, 9):
        v_ref[plane + 1] = spread_field(y_ref, place_ref, label_of, plane)

    def put(plane, image):
        w = w_ref[plane]
        d = d_ref[plane]
        u = aw_ref[plane] - image[:16]
        d_next = gain * d - alpha * (w - v_ref[plane + 1, 0:16])
        w_next = gain * w - alpha * u
        x_out[plane] = x_ref[plane] + alpha * d + alpha_next * d_next
        r_out[plane] = r_ref[plane] - alpha * w - alpha_next * w_next

    stencil(lambda plane: v_ref[plane + 1], k_ref, diag_ref, 0, 8, put)


VMEM = pl.BlockSpec(memory_space=pltpu.VMEM)
SMEM = pl.BlockSpec(memory_space=pltpu.SMEM)


def shape_of(*dims):
    return jax.ShapeDtypeStruct(dims, F32)


def call(kernel, name, outs, scratch, in_specs, mib):
    return pl.pallas_call(
        kernel,
        name=name,
        out_shape=outs,
        in_specs=in_specs,
        out_specs=tuple(VMEM for _ in outs),
        scratch_shapes=scratch,
        compiler_params=pltpu.CompilerParams(vmem_limit_bytes=mib * 1024 * 1024),
    )


def ring_pairs(peers):
    up = [(i, (i + 1) % peers) for i in range(peers)]
    return up, [(j, i) for i, j in up]


def exchange_all(slots):
    width = slots.shape[0] // 16
    held = lax.all_to_all(slots.reshape(16, width * 128), AXIAL, 0, 0, tiled=True)
    held = jnp.broadcast_to(held.reshape(1, 16 * width, 128), (16, 16 * width, 128))
    return lax.all_to_all(held, CIRC, 0, 0, tiled=True).reshape(256 * width, 128)


def exchange(slots, count):
    return lax.all_to_all(slots.reshape(256, count, 128), AXIAL_CIRC, 0, 0, tiled=True).reshape(
        256 * count, 128
    )


def shards(right_side, stiffness, material, groups):
    place = jnp.stack([lax.axis_index(AXIAL), lax.axis_index(CIRC)]).astype(jnp.int32)

    def fields(rows):
        parts = (right_side, stiffness, material, groups)
        return jnp.stack([part[:, rows].astype(F32) for part in parts])

    up, down = ring_pairs(16)
    before = lax.ppermute(fields(slice(16 - EDGE, 16)), CIRC, up)
    after = lax.ppermute(fields(slice(0, EDGE)), CIRC, down)
    middle = jnp.concatenate([fields(slice(0, 16)), after, before], axis=2)
    low = lax.ppermute(middle[:, 8 - DEPTH :], AXIAL, up)
    high = lax.ppermute(middle[:, :DEPTH], AXIAL, down)
    table = np.zeros((16, 128), np.float32)
    table[:13, :CLASSES] = coefficient_table().T
    ext = (ROWS, 256)
    k, diag, slots = call(
        setup_kernel,
        "setup",
        (shape_of(14, 13, *ext), shape_of(12, *ext), shape_of(48, 128)),
        [pltpu.VMEM((9, 9, 16, 256), F32)],
        [VMEM, VMEM, VMEM, VMEM, SMEM],
        24,
    )(low, middle, high, jnp.asarray(table), place)
    gathered = exchange_all(slots)
    square = (BLOCK, BLOCK)
    right, left, last, y = call(
        factor_kernel,
        "factor",
        (shape_of(15, BLOCK, 3 * BLOCK), shape_of(15, 2 * BLOCK, BLOCK), shape_of(*square), shape_of(16, BLOCK)),
        [
            pltpu.VMEM((16, *square), F32),
            pltpu.VMEM((16, *square), F32),
            pltpu.VMEM((8, *square), F32),
            pltpu.VMEM((8, *square), F32),
            pltpu.VMEM((16, BLOCK), F32),
            pltpu.VMEM((16, BLOCK), F32),
        ],
        [VMEM, SMEM],
        24,
    )(gathered, jnp.asarray(np.array(SCALES, np.float32)))
    own = (8, 16, 256)
    x0, r0, image, slots = call(
        start_kernel,
        "start",
        (shape_of(*own), shape_of(*own), shape_of(10, *ext), shape_of(256, 128)),
        [pltpu.VMEM((14, *ext), F32), pltpu.VMEM((12, *ext), F32)],
        [VMEM] * 6 + [SMEM],
        24,
    )(low, middle, high, k, diag, y, place)
    gathered = exchange(slots, 1)
    w0, d0, aw0, slots = call(
        first_kernel,
        "first",
        (shape_of(*own), shape_of(*own), shape_of(*own), shape_of(256, 128)),
        [pltpu.VMEM((16, BLOCK), F32), pltpu.VMEM((12, *ext), F32), pltpu.VMEM((10, *ext), F32)],
        [VMEM] * 11 + [SMEM],
        24,
    )(gathered, right, left, last, low, middle, high, k, diag, image, r0, place)
    gathered = exchange(slots, 1)
    return call(
        last_kernel,
        "last",
        (shape_of(*own), shape_of(*own)),
        [pltpu.VMEM((16, BLOCK), F32), pltpu.VMEM((10, *ext), F32)],
        [VMEM] * 14 + [SMEM],
        24,
    )(gathered, right, left, last, low, middle, high, k, diag, x0, r0, w0, d0, aw0, place)


def solution(mesh):
    split = Mesh(mesh.devices.reshape(8, 2, 4, 4), ("axial_0", "axial_1", "circ_0", "circ_1"))
    placed = P(AXIAL, CIRC, None)
    return jax.shard_map(
        shards,
        mesh=split,
        in_specs=(placed,) * 4,
        out_specs=(placed, placed),
        check_vma=False,
    )
```

```python
import math

import jax
import jax.numpy as jnp
import numpy as np
from jax import lax
from jax.experimental import pallas as pl
from jax.experimental.pallas import tpu as pltpu
from jax.sharding import Mesh
from jax.sharding import PartitionSpec as P

LABELS = 8
CLASSES = 16
CIRC = ("circ_0", "circ_1")
AXIAL = ("axial_0", "axial_1")
AXIAL_CIRC = ("axial_0", "axial_1", "circ_0", "circ_1")
MASS_SHIFT = 0.02
HIGH = lax.Precision.HIGHEST
HALF_STEPS = (
    (0, 0, 1),
    (0, 1, -1),
    (0, 1, 0),
    (0, 1, 1),
    (1, -1, -1),
    (1, -1, 0),
    (1, -1, 1),
    (1, 0, -1),
    (1, 0, 0),
    (1, 0, 1),
    (1, 1, -1),
    (1, 1, 0),
    (1, 1, 1),
)
STEP_OF = {step: place for place, step in enumerate(HALF_STEPS)}
SHIFTS = [(sy, sz) for sy in (-1, 0, 1) for sz in (-1, 0, 1)]
ROWS = 24
EDGE = 4
DEPTH = 3
BLOCK = 128
F32 = jnp.float32
BF16 = jnp.bfloat16


def coefficient_table():
    rows_out = []
    for material_id in range(CLASSES):
        fiber_angle = math.pi * (material_id % 8) / 8.0
        if material_id < 8:
            fiber_dir = (math.cos(fiber_angle), math.sin(fiber_angle), 0.0)
            strength, anisotropy = (1.0, 6.0)
        else:
            fiber_dir = (0.6 * math.cos(fiber_angle), 0.6 * math.sin(fiber_angle), 0.8)
            strength, anisotropy = (0.35, 2.0)
        line_values = []
        for offset in HALF_STEPS:
            length_sq = float(offset[0] * offset[0] + offset[1] * offset[1] + offset[2] * offset[2])
            along_fiber = (
                fiber_dir[0] * offset[0] + fiber_dir[1] * offset[1] + fiber_dir[2] * offset[2]
            )
            line_values.append(
                strength * (0.15 + anisotropy * along_fiber * along_fiber / length_sq) / length_sq
            )
        rows_out.append(line_values)
    return np.array(rows_out, dtype=np.float32)


def inverse_scales():
    table = coefficient_table().astype(np.float64)
    widest = MASS_SHIFT + 0.3 * (table.sum(axis=1).max() + table.max(axis=0).sum())
    low = 0.5 * MASS_SHIFT / widest
    scales, lows = [], []
    while 1.0 - low > 2e-7:
        scales.append(2.0 / (1.0 + low))
        lows.append(low)
        low = 4.0 * low / (1.0 + low) ** 2
    return scales, lows


SCALES, LOWS = inverse_scales()


def lanes(shape):
    return lax.broadcasted_iota(jnp.int32, shape, len(shape) - 1)


def sublanes(shape):
    return lax.broadcasted_iota(jnp.int32, shape, len(shape) - 2)


def shift_z(values, move, fill):
    if move == 0:
        return values
    length = values.shape[-1]
    turned = pltpu.roll(values, (-move) % length, axis=1)
    edge = length - 1 if move > 0 else 0
    return jnp.where(lanes(values.shape) == edge, fill, turned)


def shift_y(values, move):
    if move == 0:
        return values
    return pltpu.roll(values, (-move) % values.shape[0], axis=0)


def shifted(values, fill):
    by_z = {sz: shift_z(values, sz, fill) for sz in (-1, 0, 1)}
    return {(sy, sz): shift_y(by_z[sz], sy) for sy, sz in SHIFTS}


def present_flags(place_ref, plane):
    if plane < 0:
        return place_ref[0] > 0
    if plane > 7:
        return place_ref[0] < 15
    return None


def masked(values, flag):
    if flag is None:
        return values
    return values * jnp.where(flag, 1.0, 0.0).astype(F32)


def stencil(v_at, k_ref, diag_ref, start, stop, emit):
    wide = {}
    made = {}

    def prepare(plane):
        values = v_at(plane)
        wide[plane] = shifted(values, 0.0)
        made[plane] = [k_ref[plane + DEPTH, j] * values for j in range(13)]

    prepare(start - 1)
    prepare(start)
    for plane in range(start, stop):
        prepare(plane + 1)
        total = None
        for j, (ox, oy, oz) in enumerate(HALF_STEPS):
            pair = wide[plane + ox][(oy, oz)] + wide[plane - ox][(-oy, -oz)]
            term = k_ref[plane + DEPTH, j] * pair
            total = term if total is None else total + term
        for sz in (-1, 0, 1):
            by_y = None
            for sy in (-1, 0, 1):
                part = made[plane + 1][STEP_OF[(1, sy, sz)]] + made[plane - 1][STEP_OF[(1, -sy, -sz)]]
                if (0, sy, sz) in STEP_OF:
                    part = part + made[plane][STEP_OF[(0, sy, sz)]]
                elif (0, -sy, -sz) in STEP_OF:
                    part = part + made[plane][STEP_OF[(0, -sy, -sz)]]
                part = shift_y(part, sy)
                by_y = part if by_y is None else by_y + part
            total = total + shift_z(by_y, sz, 0.0)
        emit(plane, diag_ref[plane + 2] * wide[plane][(0, 0)] - 0.5 * total)
        del wide[plane - 1], made[plane - 1]


def piece(low_ref, mid_ref, high_ref, field, plane):
    if plane < 0:
        return low_ref[field, plane + DEPTH]
    if plane > 7:
        return high_ref[field, plane - 8]
    return mid_ref[field, plane]


def split3(values):
    high = values.astype(BF16)
    rest = values - high.astype(F32)
    mid = rest.astype(BF16)
    low = (rest - mid.astype(F32)).astype(BF16)
    return high, mid, low


def dot(a, b, dims=((1,), (0,))):
    return lax.dot_general(a, b, (dims, ((), ())), preferred_element_type=F32)


def dot_high(a, b, dims=((1,), (0,))):
    return lax.dot_general(
        a, b, (dims, ((), ())), precision=HIGH, preferred_element_type=F32
    )


def pick(values, chooser):
    return sum(dot(part, chooser) for part in split3(values))


class Planes:
    def __init__(self, mid_ref, end_ref):
        self.mid_ref = mid_ref
        self.end_ref = end_ref

    def place(self, key):
        plane = key[0] - DEPTH
        if 0 <= plane < 8:
            return self.mid_ref, (plane, *key[1:])
        return self.end_ref, ((plane + DEPTH if plane < 0 else plane - 5), *key[1:])

    def __getitem__(self, key):
        ref, at = self.place(key)
        return ref[at]

    def __setitem__(self, key, values):
        ref, at = self.place(key)
        ref[at] = values


def fill_stiffness(k_ref, table_ref, plane, stiff, kind):
    kind = kind.astype(jnp.int32)
    for j in range(13):
        row = jnp.broadcast_to(table_ref[j : j + 1, :], (8, 128))
        parts = []
        for top in range(0, ROWS, 8):
            line = [
                gather_lanes(row, kind[top : top + 8, left : left + 128]) for left in (0, 128)
            ]
            parts.append(jnp.concatenate(line, axis=1))
        k_ref[plane + DEPTH, j] = stiff * jnp.concatenate(parts, axis=0)


def by_label(pairs):
    out = []
    for label in range(LABELS):
        total = None
        for weight, target in pairs:
            term = jnp.where(target == float(label), weight, 0.0)
            total = term if total is None else total + term
        out.append(total)
    return out


def chosen_rows(home):
    return jnp.concatenate(
        [jnp.where(home == float(k), 1.0, 0.0) for k in range(LABELS)], axis=0
    ).astype(BF16)


def cell_sums(chosen, right):
    return sum(dot(chosen, part, ((1,), (1,))) for part in split3(right))


def inner_kernel(mid_ref, table_ref, km_ref, even_ref, odd_ref, label_ref):
    k_ref = Planes(km_ref, None)
    for plane in range(8):
        fill_stiffness(k_ref, table_ref, plane, mid_ref[1, plane], mid_ref[2, plane])
        spots = shifted(mid_ref[3, plane], -1.0)
        for place, shift in enumerate(SHIFTS):
            label_ref[plane, place] = spots[shift][:16]
    row16 = sublanes((16, 256))
    ones = jnp.ones((8, 256), F32)
    sums = {}
    for plane in range(8):
        own, up = [], []
        for j, (ox, oy, oz) in enumerate(HALF_STEPS):
            if ox == 0 or plane < 7:
                across = shift_z(shift_y(k_ref[plane + ox + DEPTH, j], oy), oz, 0.0)[:16]
                weight = -0.5 * (k_ref[plane + DEPTH, j, 0:16] + across)
                target = label_ref[plane + ox, SHIFTS.index((oy, oz))]
                if oy == 0:
                    own.append((weight, target))
                else:
                    edge = 15 if oy == 1 else 0
                    own.append((jnp.where(row16 == edge, 0.0, weight), target))
                    if oy == 1:
                        up.append((jnp.where(row16 == 15, weight, 0.0)[8:], target[8:]))
            if oy == -1 and plane > 0:
                back = shift_z(shift_y(k_ref[plane - 1 + DEPTH, j], -oy), -oz, 0.0)[8:16]
                back = -0.5 * (k_ref[plane + DEPTH, j, 8:16] + back)
                source = label_ref[plane - 1, SHIFTS.index((-oy, -oz)), 8:16]
                up.append((jnp.where(row16[8:] == 15, back, 0.0), source))
        own = by_label(own)
        sides = ([], by_label(up))
        load = mid_ref[0, plane, 0:16]
        home = label_ref[plane, SHIFTS.index((0, 0))]
        for half in (0, 1):
            rows = slice(8 * half, 8 * half + 8)
            right = jnp.concatenate([o[rows] for o in own] + [load[rows], ones] + sides[half], axis=0)
            got = cell_sums(chosen_rows(home[rows]), right)
            sums[half] = got if half not in sums else sums[half] + got
    even_ref[...] = sums[0]
    odd_ref[...] = sums[1]


def setup_kernel(
    low_ref, mid_ref, high_ref, table_ref, place_ref, km_ref, even_ref, odd_ref,
    ke_ref, diag_ref, slot_ref,
):
    k_ref = Planes(km_ref, ke_ref)
    for plane in (-3, -2, -1, 8, 9, 10):
        stiff = masked(piece(low_ref, mid_ref, high_ref, 1, plane), present_flags(place_ref, plane))
        kind = piece(low_ref, mid_ref, high_ref, 2, plane)
        fill_stiffness(k_ref, table_ref, plane, stiff, kind)
    for plane in range(-2, 10):
        own = None
        total = None
        for j in range(13):
            term = k_ref[plane + DEPTH, j]
            own = term if own is None else own + term
        for sz in (-1, 0, 1):
            by_y = None
            for sy in (-1, 0, 1):
                part = k_ref[plane + 1 + DEPTH, STEP_OF[(1, sy, sz)]]
                part = part + k_ref[plane - 1 + DEPTH, STEP_OF[(1, -sy, -sz)]]
                if (0, sy, sz) in STEP_OF:
                    part = part + k_ref[plane + DEPTH, STEP_OF[(0, sy, sz)]]
                elif (0, -sy, -sz) in STEP_OF:
                    part = part + k_ref[plane + DEPTH, STEP_OF[(0, -sy, -sz)]]
                part = shift_y(part, sy)
                by_y = part if by_y is None else by_y + part
            by_y = shift_z(by_y, sz, 0.0)
            total = by_y if total is None else total + by_y
        diag_ref[plane + 2] = MASS_SHIFT + own + 0.5 * total
    middle = None
    for plane in range(8):
        for top in (0, 8):
            rows = slice(top, top + 8)
            got = cell_sums(
                chosen_rows(mid_ref[3, plane, rows]), 0.5 * diag_ref[plane + 2, rows]
            )
            middle = got if middle is None else middle + got
    spots = {shift: value[:16] for shift, value in shifted(high_ref[3, 0], -1.0).items()}
    row16 = sublanes((16, 256))
    nexts, up, down = [], [], []
    for j, (ox, oy, oz) in enumerate(HALF_STEPS):
        if ox == 1:
            across = shift_z(shift_y(k_ref[8 + DEPTH, j], oy), oz, 0.0)[:16]
            weight = -0.5 * (k_ref[7 + DEPTH, j, 0:16] + across)
            target = spots[(oy, oz)]
            if oy == 0:
                nexts.append((weight, target))
            elif oy == 1:
                nexts.append((jnp.where(row16 == 15, 0.0, weight), target))
                up.append((jnp.where(row16 == 15, weight, 0.0)[8:], target[8:]))
            else:
                nexts.append((jnp.where(row16 == 0, 0.0, weight), target))
                down.append((jnp.where(row16 == 0, weight, 0.0)[:8], target[:8]))
    nexts, up, down = by_label(nexts), by_label(up), by_label(down)
    sums = [even_ref[...], odd_ref[...]]
    for half in (0, 1):
        rows = slice(8 * half, 8 * half + 8)
        right = jnp.concatenate([o[rows] for o in nexts] + (down, up)[half], axis=0)
        sums.append(cell_sums(chosen_rows(mid_ref[3, 7, rows]), right))

    shape = (64, 8)
    total = jnp.sum(
        jnp.where(sublanes(shape) % 8 == lanes(shape), middle, 0.0), axis=1, keepdims=True
    )
    shape = (64, 3 * 128)
    total = jnp.where(
        jnp.logical_and(lanes(shape) < 128, lanes(shape) % 16 == sublanes(shape) // 8), total, 0.0
    )
    for which in range(4):
        width = sums[which].shape[1]
        shape = (64, width)
        kept = jnp.where(sublanes(shape) % 8 == lanes(shape) % 8, sums[which], 0.0)
        shape = (width, 3 * 128)
        group = sublanes(shape) // 8
        if which < 2:
            spot = jnp.where(group < 8, group, jnp.where(group < 10, 32 + group, group - 2))
        else:
            spot = jnp.where(group < 8, 24 + group, (8 if which == 2 else 24) + group)
        here = (lanes(shape) // 128) * 16 + lanes(shape) % 16
        total = total + pick(kept, jnp.where(here == spot, 1.0, 0.0).astype(BF16))
    shape = (64, 3 * 128)
    total = jnp.where(sublanes(shape) // 8 == (lanes(shape) % 128) // 16, total, 0.0)
    total = jnp.sum(total, axis=0, keepdims=True)
    rows = [total[:, 128 * r : 128 * r + 128] for r in range(3)]
    slots = jnp.concatenate(rows * 8, axis=0)
    for at in range(0, 768, 24):
        slot_ref[at : at + 24, :] = slots


def coarse_rows(values, chooser):
    spread = pick(values, chooser)
    shape = (256, BLOCK)
    kept = jnp.where(sublanes(shape) % 16 == lanes(shape) % 16, spread, 0.0)
    return jnp.sum(kept.reshape(16, 16, BLOCK), axis=1)


def as_columns(rows):
    count = len(rows)
    stacked = jnp.concatenate(rows + [jnp.zeros((1, BLOCK), F32)] * (8 - count), axis=0)
    turned = stacked.T
    return [turned[:, i : i + 1] for i in range(count)]


def coarse_solve(coarse_rhs, right_ref, left_ref, last_ref):
    now = [coarse_rhs[i : i + 1, :] for i in range(16)]
    begin = 0
    stages = []
    while len(now) > 2:
        count = len(now)
        odd = now[1::2]
        even = now[0::2]
        solved = []
        for q, column in enumerate(as_columns(odd)):
            product = jnp.sum(right_ref[begin + q] * column, axis=0, keepdims=True)
            solved.append(product[:, :BLOCK])
            even[q] = even[q] - product[:, BLOCK : 2 * BLOCK]
            if q + 1 < len(even):
                even[q + 1] = even[q + 1] - product[:, 2 * BLOCK :]
        stages.append((begin, solved))
        begin += count // 2
        now = even
    column = jnp.concatenate(as_columns(now), axis=0)
    both = jnp.sum(last_ref[...] * column, axis=0, keepdims=True)
    found = [both[:, :BLOCK], both[:, BLOCK:]]
    for begin, solved in reversed(stages):
        columns = as_columns(found)
        merged = []
        for q, value in enumerate(solved):
            value = value - jnp.sum(left_ref[begin + q, :BLOCK] * columns[q], axis=0, keepdims=True)
            if q + 1 < len(found):
                value = value - jnp.sum(
                    left_ref[begin + q, BLOCK:] * columns[q + 1], axis=0, keepdims=True
                )
            merged += [found[q], value]
        found = merged
    return jnp.concatenate(found, axis=0)


def split2(values):
    high = values.astype(BF16)
    return high, (values - high.astype(F32)).astype(BF16)


def left_stack(halves):
    high, low = halves
    return jnp.concatenate([high, high, low], axis=1)


def right_stack(halves):
    high, low = halves
    return jnp.concatenate([high, low, high], axis=0)


def invert(blocks, begin, scale_ref, x_ref, p_ref):
    shape = blocks[0].shape
    size = shape[0]
    eye = jnp.where(lanes(shape) == sublanes(shape), 1.0, 0.0).astype(F32)
    for q, block in enumerate(blocks):
        kept = eye * block
        across = 1.0 / jnp.sum(kept, axis=0, keepdims=True)
        down = 1.0 / jnp.sum(kept, axis=1, keepdims=True)
        c = 0.5 * scale_ref[begin]
        x_ref[q] = (2.0 * c * eye - (c * c) * (block * down)) * across
    for q, block in enumerate(blocks):
        p_ref[q] = dot(left_stack(split2(block)), right_stack(split2(x_ref[q])))

    def step(k, carry):
        c = scale_ref[k]
        for q in range(len(blocks)):
            x = x_ref[q]
            p = p_ref[q]
            halves = split2(p)
            both = jnp.concatenate([left_stack(halves), left_stack(split2(x))], axis=0)
            product = dot(both, right_stack(halves))
            p_ref[q] = (2.0 * c) * p - (c * c) * product[:size]
            x_ref[q] = (2.0 * c) * x - (c * c) * product[size:]
        return carry

    lax.fori_loop(begin + 1, len(SCALES) - 2, step, 0)
    values = [x_ref[q] for q in range(len(blocks))]
    rests = [
        eye - dot(left_stack(split2(s)), right_stack(split2(x))) for s, x in zip(blocks, values)
    ]
    values = [x + dot(x.astype(BF16), r.astype(BF16)) for x, r in zip(values, rests)]
    rests = [eye - dot_high(s, x) for s, x in zip(blocks, values)]
    return [x + dot(x.astype(BF16), r.astype(BF16)) for x, r in zip(values, rests)]


def turned(values):
    shape = (BLOCK, BLOCK)
    eye = jnp.where(lanes(shape) == sublanes(shape), 1.0, 0.0).astype(BF16)
    return sum(dot(eye, part, ((1,), (1,))) for part in split3(values))


def gather_lanes(values, spot):
    return jnp.take_along_axis(values, spot, axis=1, mode="promise_in_bounds")


def unpack_coarse(slots_ref, d_ref, b_ref, f_ref, n_ref):
    for top in (0, 8):
        shape = (8, BLOCK)
        device = sublanes(shape) + top
        ring = lanes(shape) % 16
        column = lanes(shape) // 16
        ahead = (ring - device + 16) % 16
        side = (ahead + 1) % 16
        home = jnp.minimum(ahead, 1) * 8 + column
        cross = jnp.minimum(side, 1) * 8 + column
        for s in range(16):
            at = 48 * s + 3 * top
            rows = [slots_ref[pl.ds(at + r, 8, stride=3), :] for r in range(3)]
            for label in range(LABELS):
                row = 16 * label + top
                got = gather_lanes(rows[0], home + 16 * label)
                d_ref[s, row : row + 8, :] = jnp.where(ahead < 2, got, 0.0)
                if s < 15:
                    got = jnp.where(
                        side < 2,
                        gather_lanes(rows[1], cross + 16 * label),
                        gather_lanes(rows[2], column + 16 * label),
                    )
                    b_ref[s, row : row + 8, :] = jnp.where(side < 3, got, 0.0)
            for place, target in ((8, f_ref), (9, n_ref)):
                got = jnp.where(ring == device, gather_lanes(rows[2], 16 * column + place), 0.0)
                total = jnp.sum(got, axis=0, keepdims=True)
                if top > 0:
                    total = target[s : s + 1, :] + total
                target[s : s + 1, :] = total


def first_step(d_ref, n_ref):
    shape = (BLOCK, BLOCK)
    eye = lanes(shape) == sublanes(shape)
    diagonal = jnp.concatenate(
        [jnp.sum(jnp.where(eye, d_ref[s], 0.0), axis=0, keepdims=True) for s in range(16)], axis=0
    )
    low = jnp.min((0.5 * MASS_SHIFT) * n_ref[...] / diagonal)
    return sum(jnp.where(low >= bound, 1, 0).astype(jnp.int32) for bound in LOWS[1:-2])


def factor_kernel(
    slots_ref, scale_ref, right_ref, left_ref, last_ref, y_ref, d_ref, b_ref, x_ref, p_ref,
    xl_ref, pl_ref, f_ref, n_ref,
):
    unpack_coarse(slots_ref, d_ref, b_ref, f_ref, n_ref)
    b_ref[15] = jnp.zeros((BLOCK, BLOCK), F32)
    for i in range(16):
        d_ref[i] = d_ref[i] + turned(d_ref[i])
    first = first_step(d_ref, n_ref)
    begin = 0
    stride = 1
    while stride < 8:
        count = 8 // stride
        odd = [(2 * q + 1) * stride for q in range(count)]
        inverses = invert([d_ref[i] for i in odd], first, scale_ref, x_ref, p_ref)
        ups = [
            dot_high(inverse, b_ref[i - stride], ((1,), (1,))) for i, inverse in zip(odd, inverses)
        ]
        downs = [dot_high(inverse, b_ref[i]) for i, inverse in zip(odd, inverses)]
        products = [jnp.concatenate(pair, axis=1) for pair in zip(ups, downs)]
        for q in range(count):
            right_ref[begin + q, :, :BLOCK] = inverses[q]
            right_ref[begin + q, :, BLOCK:] = products[q]
        grams = [dot_high(b_ref[i - stride], product) for i, product in zip(odd, products)]
        for q in range(count):
            left_ref[begin + q, :BLOCK, :] = turned(ups[q])
            left_ref[begin + q, BLOCK:, :] = turned(downs[q])
        afters = [
            dot_high(left_ref[begin + q, BLOCK:, :], b_ref[i])
            for q, i in enumerate(odd)
            if i + stride < 16
        ]
        for q, i in enumerate(odd):
            change = grams[q][:, :BLOCK]
            if q > 0:
                change = change + afters[q - 1]
            d_ref[i - stride] = d_ref[i - stride] - change
            b_ref[i - stride] = -grams[q][:, BLOCK:]
        begin += count
        stride *= 2
    pair = jnp.concatenate(
        [
            jnp.concatenate([d_ref[0], b_ref[0]], axis=1),
            jnp.concatenate([turned(b_ref[0]), d_ref[8]], axis=1),
        ],
        axis=0,
    )
    (last,) = invert([pair], first, scale_ref, xl_ref, pl_ref)
    last_ref[...] = last
    y_ref[...] = coarse_solve(f_ref[...], right_ref, left_ref, last_ref)


def spread_field(y_ref, place_ref, label_of, plane):
    axial = place_ref[0]
    if plane < 0:
        axial = jnp.maximum(axial - 1, 0)
    elif plane > 7:
        axial = jnp.minimum(axial + 1, 15)
    line = jnp.broadcast_to(y_ref[pl.ds(axial, 1), :], (8, BLOCK))
    ring = sublanes((ROWS, 256))
    move = jnp.where(ring < 16, 0, jnp.where(ring < 16 + EDGE, 1, 15))
    spot = label_of(plane).astype(jnp.int32) * 16 + (place_ref[1] + move) % 16
    parts = []
    for top in range(0, ROWS, 8):
        parts.append(
            jnp.concatenate(
                [
                    jnp.take_along_axis(
                        line,
                        spot[top : top + 8, left : left + 128],
                        axis=1,
                        mode="promise_in_bounds",
                    )
                    for left in (0, 128)
                ],
                axis=1,
            )
        )
    return masked(jnp.concatenate(parts, axis=0), present_flags(place_ref, plane))


def fold(values):
    half = values[:8] + values[8:]
    return half[:, :128] + half[:, 128:]


def slot_row(totals):
    count = len(totals)
    stacked = jnp.concatenate(totals, axis=0)
    shape = (8 * count, 128)
    sums = jnp.sum(stacked, axis=1, keepdims=True)
    kept = jnp.where(sublanes(shape) // 8 == lanes(shape), sums, 0.0)
    return jnp.sum(kept, axis=0, keepdims=True)


class Totals:
    def __init__(self, count):
        self.values = [None] * count

    def add(self, at, term):
        self.values[at] = term if self.values[at] is None else self.values[at] + term

    def by_label(self, labels, field):
        for k in range(LABELS):
            self.add(k, fold(jnp.where(labels == float(k), field, 0.0)))


def start_kernel(
    low_ref, mid_ref, high_ref, km_ref, ke_ref, diag_ref, y_ref, place_ref,
    x_out, r_out, image_ref, slot_ref, v_ref, w_ref,
):
    k_ref = Planes(km_ref, ke_ref)
    def label_of(plane):
        return piece(low_ref, mid_ref, high_ref, 3, plane)

    for plane in range(-3, 11):
        v_ref[plane + 3] = spread_field(y_ref, place_ref, label_of, plane)

    def put_residual(plane, image):
        load = piece(low_ref, mid_ref, high_ref, 0, plane)
        w_ref[plane + 2] = masked(load - image, present_flags(place_ref, plane))

    stencil(lambda plane: v_ref[plane + 3], k_ref, diag_ref, -2, 10, put_residual)
    totals = Totals(9)

    def put_image(plane, image):
        image_ref[plane + 1] = image
        if 0 <= plane < 8:
            totals.by_label(mid_ref[3, plane, 0:16], image[:16])
            own = w_ref[plane + 2, 0:16]
            totals.add(8, fold(own * own))

    stencil(lambda plane: w_ref[plane + 2], k_ref, diag_ref, -1, 9, put_image)
    for plane in range(8):
        x_out[plane] = v_ref[plane + 3, 0:16]
        r_out[plane] = w_ref[plane + 2, 0:16]
    slot_ref[...] = jnp.broadcast_to(slot_row(totals.values), (256, 128))


def label_chooser():
    shape = (128, BLOCK)
    return jnp.where(sublanes(shape) == lanes(shape) // 16, 1.0, 0.0).astype(BF16)


def first_kernel(
    got_ref, right_ref, left_ref, last_ref, low_ref, mid_ref, high_ref, km_ref, ke_ref, diag_ref, image_ref,
    r_ref, place_ref, w_out, d_out, aw_out, slot_ref, y_ref, v_ref, w_ref,
):
    k_ref = Planes(km_ref, ke_ref)
    got = got_ref[...]
    coarse_rhs = coarse_rows(got, label_chooser())
    y_ref[...] = coarse_solve(coarse_rhs, right_ref, left_ref, last_ref)

    def label_of(plane):
        return piece(low_ref, mid_ref, high_ref, 3, plane)

    for plane in range(-2, 10):
        v_ref[plane + 2] = spread_field(y_ref, place_ref, label_of, plane)
    totals = Totals(12)

    def put_direction_image(plane, image):
        w_ref[plane + 1] = masked(image_ref[plane + 1] - image, present_flags(place_ref, plane))

    stencil(lambda plane: v_ref[plane + 2], k_ref, diag_ref, -1, 9, put_direction_image)

    def put_second(plane, image):
        own = w_ref[plane + 1, 0:16]
        image = image[:16]
        residual = r_ref[plane]
        direction = residual - v_ref[plane + 2, 0:16]
        w_out[plane] = own
        d_out[plane] = direction
        aw_out[plane] = image
        totals.by_label(mid_ref[3, plane, 0:16], image)
        totals.add(8, fold(direction * own))
        totals.add(9, fold(own * own))
        totals.add(10, fold(residual * own))
        totals.add(11, fold(own * image))

    stencil(lambda plane: w_ref[plane + 1], k_ref, diag_ref, 0, 8, put_second)
    square = jnp.sum(got, axis=0, keepdims=True) * (1.0 / 256.0)
    shape = (1, 128)
    square = jnp.sum(jnp.where(lanes(shape) == 8, square, 0.0), axis=1, keepdims=True)
    row = slot_row(totals.values) + jnp.where(lanes(shape) == 12, square, 0.0)
    slot_ref[...] = jnp.broadcast_to(row, (256, 128))


def last_kernel(
    got_ref, right_ref, left_ref, last_ref, low_ref, mid_ref, high_ref, km_ref, ke_ref, diag_ref,
    x_ref, r_ref, w_ref, d_ref, aw_ref, place_ref, x_out, r_out, y_ref, v_ref,
):
    k_ref = Planes(km_ref, ke_ref)
    got = got_ref[...]
    coarse_rhs = coarse_rows(got, label_chooser())
    solved = coarse_solve(coarse_rhs, right_ref, left_ref, last_ref)
    y_ref[...] = solved
    row = jnp.sum(got, axis=0, keepdims=True)

    def scalar(at):
        return jnp.sum(jnp.where(lanes((1, 128)) == at, row, 0.0), axis=1, keepdims=True)

    dw, ww, rw, waw, rr = (scalar(at) for at in (8, 9, 10, 11, 12))
    hq = jnp.sum(jnp.sum(coarse_rhs * solved, axis=1, keepdims=True), axis=0, keepdims=True)
    alpha = rr / dw
    rr_next = rr - 2.0 * alpha * rw + alpha * alpha * ww
    beta = rr_next / rr
    gain = 1.0 + beta
    curvature = gain * gain * dw - 2.0 * gain * alpha * ww + alpha * alpha * (waw - hq)
    alpha_next = rr_next / curvature

    def label_of(plane):
        return piece(low_ref, mid_ref, high_ref, 3, plane)

    for plane in range(-1, 9):
        v_ref[plane + 1] = spread_field(y_ref, place_ref, label_of, plane)

    def put(plane, image):
        w = w_ref[plane]
        d = d_ref[plane]
        u = aw_ref[plane] - image[:16]
        d_next = gain * d - alpha * (w - v_ref[plane + 1, 0:16])
        w_next = gain * w - alpha * u
        x_out[plane] = x_ref[plane] + alpha * d + alpha_next * d_next
        r_out[plane] = r_ref[plane] - alpha * w - alpha_next * w_next

    stencil(lambda plane: v_ref[plane + 1], k_ref, diag_ref, 0, 8, put)


VMEM = pl.BlockSpec(memory_space=pltpu.VMEM)
SMEM = pl.BlockSpec(memory_space=pltpu.SMEM)


def shape_of(*dims):
    return jax.ShapeDtypeStruct(dims, F32)


def call(kernel, name, outs, scratch, in_specs, mib, cost=None):
    return pl.pallas_call(
        kernel,
        name=name,
        out_shape=outs,
        in_specs=in_specs,
        out_specs=tuple(VMEM for _ in outs),
        scratch_shapes=scratch,
        cost_estimate=cost,
        compiler_params=pltpu.CompilerParams(vmem_limit_bytes=mib * 1024 * 1024),
    )


def ring_pairs(peers):
    up = [(i, (i + 1) % peers) for i in range(peers)]
    return up, [(j, i) for i, j in up]


def exchange_all(slots):
    width = slots.shape[0] // 256
    return lax.all_to_all(slots.reshape(256, width * 128), AXIAL_CIRC, 0, 0, tiled=True).reshape(
        256 * width, 128
    )


def exchange(slots, count):
    return lax.all_to_all(slots.reshape(256, count, 128), AXIAL_CIRC, 0, 0, tiled=True).reshape(
        256 * count, 128
    )


def shards(right_side, stiffness, material, groups):
    place = jnp.stack([lax.axis_index(AXIAL), lax.axis_index(CIRC)]).astype(jnp.int32)

    def fields(rows):
        parts = (right_side, stiffness, material, groups)
        return jnp.stack([part[:, rows].astype(F32) for part in parts])

    up, down = ring_pairs(16)
    before = lax.ppermute(fields(slice(16 - EDGE, 16)), CIRC, up)
    after = lax.ppermute(fields(slice(0, EDGE)), CIRC, down)
    middle = jnp.concatenate([fields(slice(0, 16)), after, before], axis=2)
    low = lax.ppermute(middle[:, 8 - DEPTH :], AXIAL, up)
    high = lax.ppermute(middle[:, :DEPTH], AXIAL, down)
    table = np.zeros((16, 128), np.float32)
    table[:13, :CLASSES] = coefficient_table().T
    ext = (ROWS, 256)
    table = jnp.asarray(table)
    k_mid, even, odd = call(
        inner_kernel,
        "inner",
        (shape_of(8, 13, *ext), shape_of(64, 80), shape_of(64, 144)),
        [pltpu.VMEM((8, 9, 16, 256), F32)],
        [VMEM, VMEM],
        20,
        pl.CostEstimate(flops=40_000_000, transcendentals=0, bytes_accessed=4_000_000),
    )(middle, table)
    k_end, diag, slots = call(
        setup_kernel,
        "setup",
        (shape_of(6, 13, *ext), shape_of(12, *ext), shape_of(768, 128)),
        [],
        [VMEM, VMEM, VMEM, VMEM, SMEM, VMEM, VMEM, VMEM],
        20,
    )(low, middle, high, table, place, k_mid, even, odd)
    gathered = exchange_all(slots)
    square = (BLOCK, BLOCK)
    double = (2 * BLOCK, 2 * BLOCK)
    right, left, last, y = call(
        factor_kernel,
        "factor",
        (shape_of(14, BLOCK, 3 * BLOCK), shape_of(14, 2 * BLOCK, BLOCK), shape_of(*double), shape_of(16, BLOCK)),
        [
            pltpu.VMEM((16, *square), F32),
            pltpu.VMEM((16, *square), F32),
            pltpu.VMEM((8, *square), F32),
            pltpu.VMEM((8, *square), F32),
            pltpu.VMEM((1, *double), F32),
            pltpu.VMEM((1, *double), F32),
            pltpu.VMEM((16, BLOCK), F32),
            pltpu.VMEM((16, BLOCK), F32),
        ],
        [VMEM, SMEM],
        24,
    )(gathered, jnp.asarray(np.array(SCALES, np.float32)))
    own = (8, 16, 256)
    x0, r0, image, slots = call(
        start_kernel,
        "start",
        (shape_of(*own), shape_of(*own), shape_of(10, *ext), shape_of(256, 128)),
        [pltpu.VMEM((14, *ext), F32), pltpu.VMEM((12, *ext), F32)],
        [VMEM] * 7 + [SMEM],
        24,
    )(low, middle, high, k_mid, k_end, diag, y, place)
    gathered = exchange(slots, 1)
    w0, d0, aw0, slots = call(
        first_kernel,
        "first",
        (shape_of(*own), shape_of(*own), shape_of(*own), shape_of(256, 128)),
        [pltpu.VMEM((16, BLOCK), F32), pltpu.VMEM((12, *ext), F32), pltpu.VMEM((10, *ext), F32)],
        [VMEM] * 12 + [SMEM],
        24,
    )(gathered, right, left, last, low, middle, high, k_mid, k_end, diag, image, r0, place)
    gathered = exchange(slots, 1)
    return call(
        last_kernel,
        "last",
        (shape_of(*own), shape_of(*own)),
        [pltpu.VMEM((16, BLOCK), F32), pltpu.VMEM((10, *ext), F32)],
        [VMEM] * 15 + [SMEM],
        24,
    )(gathered, right, left, last, low, middle, high, k_mid, k_end, diag, x0, r0, w0, d0, aw0, place)


def solution(mesh):
    split = Mesh(mesh.devices.reshape(8, 2, 4, 4), ("axial_0", "axial_1", "circ_0", "circ_1"))
    placed = P(AXIAL, CIRC, None)
    return jax.shard_map(
        shards,
        mesh=split,
        in_specs=(placed,) * 4,
        out_specs=(placed, placed),
        check_vma=False,
    )
```

```python
import math

import jax
import jax.numpy as jnp
import numpy as np
from jax import lax
from jax.experimental import pallas as pl
from jax.experimental.pallas import tpu as pltpu
from jax.sharding import Mesh
from jax.sharding import PartitionSpec as P

LABELS = 8
CLASSES = 16
CIRC = ("circ_0", "circ_1")
AXIAL = ("axial_0", "axial_1")
AXIAL_CIRC = ("axial_0", "axial_1", "circ_0", "circ_1")
MASS_SHIFT = 0.02
HIGH = lax.Precision.HIGHEST
HALF_STEPS = (
    (0, 0, 1),
    (0, 1, -1),
    (0, 1, 0),
    (0, 1, 1),
    (1, -1, -1),
    (1, -1, 0),
    (1, -1, 1),
    (1, 0, -1),
    (1, 0, 0),
    (1, 0, 1),
    (1, 1, -1),
    (1, 1, 0),
    (1, 1, 1),
)
STEP_OF = {step: place for place, step in enumerate(HALF_STEPS)}
SHIFTS = [(sy, sz) for sy in (-1, 0, 1) for sz in (-1, 0, 1)]
ROWS = 24
EDGE = 4
DEPTH = 3
BLOCK = 128
F32 = jnp.float32
BF16 = jnp.bfloat16


def coefficient_table():
    rows_out = []
    for material_id in range(CLASSES):
        fiber_angle = math.pi * (material_id % 8) / 8.0
        if material_id < 8:
            fiber_dir = (math.cos(fiber_angle), math.sin(fiber_angle), 0.0)
            strength, anisotropy = (1.0, 6.0)
        else:
            fiber_dir = (0.6 * math.cos(fiber_angle), 0.6 * math.sin(fiber_angle), 0.8)
            strength, anisotropy = (0.35, 2.0)
        line_values = []
        for offset in HALF_STEPS:
            length_sq = float(offset[0] * offset[0] + offset[1] * offset[1] + offset[2] * offset[2])
            along_fiber = (
                fiber_dir[0] * offset[0] + fiber_dir[1] * offset[1] + fiber_dir[2] * offset[2]
            )
            line_values.append(
                strength * (0.15 + anisotropy * along_fiber * along_fiber / length_sq) / length_sq
            )
        rows_out.append(line_values)
    return np.array(rows_out, dtype=np.float32)


def inverse_scales():
    table = coefficient_table().astype(np.float64)
    widest = MASS_SHIFT + 0.3 * (table.sum(axis=1).max() + table.max(axis=0).sum())
    low = 0.5 * MASS_SHIFT / widest
    scales, lows = [], []
    while 1.0 - low > 2e-7:
        scales.append(2.0 / (1.0 + low))
        lows.append(low)
        low = 4.0 * low / (1.0 + low) ** 2
    return scales, lows


SCALES, LOWS = inverse_scales()


def lanes(shape):
    return lax.broadcasted_iota(jnp.int32, shape, len(shape) - 1)


def sublanes(shape):
    return lax.broadcasted_iota(jnp.int32, shape, len(shape) - 2)


def shift_z(values, move, fill):
    if move == 0:
        return values
    length = values.shape[-1]
    turned = pltpu.roll(values, (-move) % length, axis=1)
    edge = length - 1 if move > 0 else 0
    return jnp.where(lanes(values.shape) == edge, fill, turned)


def shift_y(values, move):
    if move == 0:
        return values
    return pltpu.roll(values, (-move) % values.shape[0], axis=0)


def shifted(values, fill):
    by_z = {sz: shift_z(values, sz, fill) for sz in (-1, 0, 1)}
    return {(sy, sz): shift_y(by_z[sz], sy) for sy, sz in SHIFTS}


def present_flags(place_ref, plane):
    if plane < 0:
        return place_ref[0] > 0
    if plane > 7:
        return place_ref[0] < 15
    return None


def masked(values, flag):
    if flag is None:
        return values
    return values * jnp.where(flag, 1.0, 0.0).astype(F32)


def stencil(v_at, k_ref, diag_ref, start, stop, emit):
    wide = {}
    made = {}

    def prepare(plane):
        values = v_at(plane)
        wide[plane] = shifted(values, 0.0)
        made[plane] = [k_ref[plane + DEPTH, j] * values for j in range(13)]

    prepare(start - 1)
    prepare(start)
    for plane in range(start, stop):
        prepare(plane + 1)
        total = None
        for j, (ox, oy, oz) in enumerate(HALF_STEPS):
            pair = wide[plane + ox][(oy, oz)] + wide[plane - ox][(-oy, -oz)]
            term = k_ref[plane + DEPTH, j] * pair
            total = term if total is None else total + term
        for sz in (-1, 0, 1):
            by_y = None
            for sy in (-1, 0, 1):
                part = made[plane + 1][STEP_OF[(1, sy, sz)]] + made[plane - 1][STEP_OF[(1, -sy, -sz)]]
                if (0, sy, sz) in STEP_OF:
                    part = part + made[plane][STEP_OF[(0, sy, sz)]]
                elif (0, -sy, -sz) in STEP_OF:
                    part = part + made[plane][STEP_OF[(0, -sy, -sz)]]
                part = shift_y(part, sy)
                by_y = part if by_y is None else by_y + part
            total = total + shift_z(by_y, sz, 0.0)
        emit(plane, diag_ref[plane + 2] * wide[plane][(0, 0)] - 0.5 * total)
        del wide[plane - 1], made[plane - 1]


def piece(low_ref, mid_ref, high_ref, field, plane):
    if plane < 0:
        return low_ref[field, plane + DEPTH]
    if plane > 7:
        return high_ref[field, plane - 8]
    return mid_ref[field, plane]


def split3(values):
    high = values.astype(BF16)
    rest = values - high.astype(F32)
    mid = rest.astype(BF16)
    low = (rest - mid.astype(F32)).astype(BF16)
    return high, mid, low


def dot(a, b, dims=((1,), (0,))):
    return lax.dot_general(a, b, (dims, ((), ())), preferred_element_type=F32)


def dot_high(a, b, dims=((1,), (0,))):
    return lax.dot_general(
        a, b, (dims, ((), ())), precision=HIGH, preferred_element_type=F32
    )


def pick(values, chooser):
    return sum(dot(part, chooser) for part in split3(values))


class Planes:
    def __init__(self, mid_ref, end_ref):
        self.mid_ref = mid_ref
        self.end_ref = end_ref

    def place(self, key):
        plane = key[0] - DEPTH
        if 0 <= plane < 8:
            return self.mid_ref, (plane, *key[1:])
        return self.end_ref, ((plane + DEPTH if plane < 0 else plane - 5), *key[1:])

    def __getitem__(self, key):
        ref, at = self.place(key)
        return ref[at]

    def __setitem__(self, key, values):
        ref, at = self.place(key)
        ref[at] = values


def fill_stiffness(k_ref, table_ref, plane, stiff, kind):
    kind = kind.astype(jnp.int32)
    for j in range(13):
        row = jnp.broadcast_to(table_ref[j : j + 1, :], (8, 128))
        parts = []
        for top in range(0, ROWS, 8):
            line = [
                gather_lanes(row, kind[top : top + 8, left : left + 128]) for left in (0, 128)
            ]
            parts.append(jnp.concatenate(line, axis=1))
        k_ref[plane + DEPTH, j] = stiff * jnp.concatenate(parts, axis=0)


def by_label(pairs):
    out = []
    for label in range(LABELS):
        total = None
        for weight, target in pairs:
            term = jnp.where(target == float(label), weight, 0.0)
            total = term if total is None else total + term
        out.append(total)
    return out


def chosen_rows(home):
    return jnp.concatenate(
        [jnp.where(home == float(k), 1.0, 0.0) for k in range(LABELS)], axis=0
    ).astype(BF16)


def cell_sums(chosen, right):
    return sum(dot(chosen, part, ((1,), (1,))) for part in split3(right))


def inner_kernel(mid_ref, table_ref, km_ref, even_ref, odd_ref, label_ref):
    k_ref = Planes(km_ref, None)
    for plane in range(8):
        fill_stiffness(k_ref, table_ref, plane, mid_ref[1, plane], mid_ref[2, plane])
        spots = shifted(mid_ref[3, plane], -1.0)
        for place, shift in enumerate(SHIFTS):
            label_ref[plane, place] = spots[shift][:16]
    row16 = sublanes((16, 256))
    ones = jnp.ones((8, 256), F32)
    sums = {}
    for plane in range(8):
        own, up = [], []
        for j, (ox, oy, oz) in enumerate(HALF_STEPS):
            if ox == 0 or plane < 7:
                across = shift_z(shift_y(k_ref[plane + ox + DEPTH, j], oy), oz, 0.0)[:16]
                weight = -0.5 * (k_ref[plane + DEPTH, j, 0:16] + across)
                target = label_ref[plane + ox, SHIFTS.index((oy, oz))]
                if oy == 0:
                    own.append((weight, target))
                else:
                    edge = 15 if oy == 1 else 0
                    own.append((jnp.where(row16 == edge, 0.0, weight), target))
                    if oy == 1:
                        up.append((jnp.where(row16 == 15, weight, 0.0)[8:], target[8:]))
            if oy == -1 and plane > 0:
                back = shift_z(shift_y(k_ref[plane - 1 + DEPTH, j], -oy), -oz, 0.0)[8:16]
                back = -0.5 * (k_ref[plane + DEPTH, j, 8:16] + back)
                source = label_ref[plane - 1, SHIFTS.index((-oy, -oz)), 8:16]
                up.append((jnp.where(row16[8:] == 15, back, 0.0), source))
        own = by_label(own)
        sides = ([], by_label(up))
        load = mid_ref[0, plane, 0:16]
        home = label_ref[plane, SHIFTS.index((0, 0))]
        for half in (0, 1):
            rows = slice(8 * half, 8 * half + 8)
            right = jnp.concatenate([o[rows] for o in own] + [load[rows], ones] + sides[half], axis=0)
            got = cell_sums(chosen_rows(home[rows]), right)
            sums[half] = got if half not in sums else sums[half] + got
    even_ref[...] = sums[0]
    odd_ref[...] = sums[1]


def setup_kernel(
    low_ref, mid_ref, high_ref, table_ref, place_ref, km_ref, even_ref, odd_ref,
    ke_ref, diag_ref, slot_ref,
):
    k_ref = Planes(km_ref, ke_ref)
    for plane in (-3, -2, -1, 8, 9, 10):
        stiff = masked(piece(low_ref, mid_ref, high_ref, 1, plane), present_flags(place_ref, plane))
        kind = piece(low_ref, mid_ref, high_ref, 2, plane)
        fill_stiffness(k_ref, table_ref, plane, stiff, kind)
    for plane in range(-2, 10):
        own = None
        total = None
        for j in range(13):
            term = k_ref[plane + DEPTH, j]
            own = term if own is None else own + term
        for sz in (-1, 0, 1):
            by_y = None
            for sy in (-1, 0, 1):
                part = k_ref[plane + 1 + DEPTH, STEP_OF[(1, sy, sz)]]
                part = part + k_ref[plane - 1 + DEPTH, STEP_OF[(1, -sy, -sz)]]
                if (0, sy, sz) in STEP_OF:
                    part = part + k_ref[plane + DEPTH, STEP_OF[(0, sy, sz)]]
                elif (0, -sy, -sz) in STEP_OF:
                    part = part + k_ref[plane + DEPTH, STEP_OF[(0, -sy, -sz)]]
                part = shift_y(part, sy)
                by_y = part if by_y is None else by_y + part
            by_y = shift_z(by_y, sz, 0.0)
            total = by_y if total is None else total + by_y
        diag_ref[plane + 2] = MASS_SHIFT + own + 0.5 * total
    middle = None
    for plane in range(8):
        for top in (0, 8):
            rows = slice(top, top + 8)
            got = cell_sums(
                chosen_rows(mid_ref[3, plane, rows]), 0.5 * diag_ref[plane + 2, rows]
            )
            middle = got if middle is None else middle + got
    spots = {shift: value[:16] for shift, value in shifted(high_ref[3, 0], -1.0).items()}
    row16 = sublanes((16, 256))
    nexts, up, down = [], [], []
    for j, (ox, oy, oz) in enumerate(HALF_STEPS):
        if ox == 1:
            across = shift_z(shift_y(k_ref[8 + DEPTH, j], oy), oz, 0.0)[:16]
            weight = -0.5 * (k_ref[7 + DEPTH, j, 0:16] + across)
            target = spots[(oy, oz)]
            if oy == 0:
                nexts.append((weight, target))
            elif oy == 1:
                nexts.append((jnp.where(row16 == 15, 0.0, weight), target))
                up.append((jnp.where(row16 == 15, weight, 0.0)[8:], target[8:]))
            else:
                nexts.append((jnp.where(row16 == 0, 0.0, weight), target))
                down.append((jnp.where(row16 == 0, weight, 0.0)[:8], target[:8]))
    nexts, up, down = by_label(nexts), by_label(up), by_label(down)
    sums = [even_ref[...], odd_ref[...]]
    for half in (0, 1):
        rows = slice(8 * half, 8 * half + 8)
        right = jnp.concatenate([o[rows] for o in nexts] + (down, up)[half], axis=0)
        sums.append(cell_sums(chosen_rows(mid_ref[3, 7, rows]), right))

    shape = (64, 8)
    total = jnp.sum(
        jnp.where(sublanes(shape) % 8 == lanes(shape), middle, 0.0), axis=1, keepdims=True
    )
    shape = (64, 3 * 128)
    total = jnp.where(
        jnp.logical_and(lanes(shape) < 128, lanes(shape) % 16 == sublanes(shape) // 8), total, 0.0
    )
    for which in range(4):
        width = sums[which].shape[1]
        shape = (64, width)
        kept = jnp.where(sublanes(shape) % 8 == lanes(shape) % 8, sums[which], 0.0)
        shape = (width, 3 * 128)
        group = sublanes(shape) // 8
        if which < 2:
            spot = jnp.where(group < 8, group, jnp.where(group < 10, 32 + group, group - 2))
        else:
            spot = jnp.where(group < 8, 24 + group, (8 if which == 2 else 24) + group)
        here = (lanes(shape) // 128) * 16 + lanes(shape) % 16
        total = total + pick(kept, jnp.where(here == spot, 1.0, 0.0).astype(BF16))
    shape = (64, 3 * 128)
    total = jnp.where(sublanes(shape) // 8 == (lanes(shape) % 128) // 16, total, 0.0)
    total = jnp.sum(total, axis=0, keepdims=True)
    rows = [total[:, 128 * r : 128 * r + 128] for r in range(3)]
    slots = jnp.concatenate(rows * 8, axis=0)
    for at in range(0, 768, 24):
        slot_ref[at : at + 24, :] = slots


def coarse_rows(values, chooser):
    spread = pick(values, chooser)
    shape = (256, BLOCK)
    kept = jnp.where(sublanes(shape) % 16 == lanes(shape) % 16, spread, 0.0)
    return jnp.sum(kept.reshape(16, 16, BLOCK), axis=1)


def as_columns(rows):
    count = len(rows)
    stacked = jnp.concatenate(rows + [jnp.zeros((1, BLOCK), F32)] * (8 - count), axis=0)
    turned = stacked.T
    return [turned[:, i : i + 1] for i in range(count)]


def coarse_solve(coarse_rhs, right_ref, left_ref, last_ref):
    now = [coarse_rhs[i : i + 1, :] for i in range(16)]
    begin = 0
    stages = []
    while len(now) > 2:
        count = len(now)
        odd = now[1::2]
        even = now[0::2]
        solved = []
        for q, column in enumerate(as_columns(odd)):
            product = jnp.sum(right_ref[begin + q] * column, axis=0, keepdims=True)
            solved.append(product[:, :BLOCK])
            even[q] = even[q] - product[:, BLOCK : 2 * BLOCK]
            if q + 1 < len(even):
                even[q + 1] = even[q + 1] - product[:, 2 * BLOCK :]
        stages.append((begin, solved))
        begin += count // 2
        now = even
    column = jnp.concatenate(as_columns(now), axis=0)
    both = jnp.sum(last_ref[...] * column, axis=0, keepdims=True)
    found = [both[:, :BLOCK], both[:, BLOCK:]]
    for begin, solved in reversed(stages):
        columns = as_columns(found)
        merged = []
        for q, value in enumerate(solved):
            value = value - jnp.sum(left_ref[begin + q, :BLOCK] * columns[q], axis=0, keepdims=True)
            if q + 1 < len(found):
                value = value - jnp.sum(
                    left_ref[begin + q, BLOCK:] * columns[q + 1], axis=0, keepdims=True
                )
            merged += [found[q], value]
        found = merged
    return jnp.concatenate(found, axis=0)


def split2(values):
    high = values.astype(BF16)
    return high, (values - high.astype(F32)).astype(BF16)


def left_stack(halves):
    high, low = halves
    return jnp.concatenate([high, high, low], axis=1)


def right_stack(halves):
    high, low = halves
    return jnp.concatenate([high, low, high], axis=0)


def invert(blocks, begin, scale_ref, x_ref, p_ref):
    shape = blocks[0].shape
    size = shape[0]
    eye = jnp.where(lanes(shape) == sublanes(shape), 1.0, 0.0).astype(F32)
    for q, block in enumerate(blocks):
        kept = eye * block
        across = 1.0 / jnp.sum(kept, axis=0, keepdims=True)
        down = 1.0 / jnp.sum(kept, axis=1, keepdims=True)
        c = 0.5 * scale_ref[begin]
        x_ref[q] = (2.0 * c * eye - (c * c) * (block * down)) * across
    for q, block in enumerate(blocks):
        p_ref[q] = dot(left_stack(split2(block)), right_stack(split2(x_ref[q])))

    def step(k, carry):
        c = scale_ref[k]
        for q in range(len(blocks)):
            x = x_ref[q]
            p = p_ref[q]
            halves = split2(p)
            both = jnp.concatenate([left_stack(halves), left_stack(split2(x))], axis=0)
            product = dot(both, right_stack(halves))
            p_ref[q] = (2.0 * c) * p - (c * c) * product[:size]
            x_ref[q] = (2.0 * c) * x - (c * c) * product[size:]
        return carry

    lax.fori_loop(begin + 1, len(SCALES) - 1, step, 0)
    values = [x_ref[q] for q in range(len(blocks))]
    rests = [eye - dot_high(s, x) for s, x in zip(blocks, values)]
    return [x + dot(x.astype(BF16), r.astype(BF16)) for x, r in zip(values, rests)]


def turned(values, split):
    shape = (BLOCK, BLOCK)
    eye = jnp.where(lanes(shape) == sublanes(shape), 1.0, 0.0).astype(BF16)
    return sum(dot(eye, part, ((1,), (1,))) for part in split(values))


def gather_lanes(values, spot):
    return jnp.take_along_axis(values, spot, axis=1, mode="promise_in_bounds")


def unpack_coarse(slots_ref, d_ref, b_ref, f_ref, n_ref):
    for top in (0, 8):
        shape = (8, BLOCK)
        device = sublanes(shape) + top
        ring = lanes(shape) % 16
        column = lanes(shape) // 16
        ahead = (ring - device + 16) % 16
        side = (ahead + 1) % 16
        home = jnp.minimum(ahead, 1) * 8 + column
        cross = jnp.minimum(side, 1) * 8 + column
        for s in range(16):
            at = 48 * s + 3 * top
            rows = [slots_ref[pl.ds(at + r, 8, stride=3), :] for r in range(3)]
            behind = pltpu.roll(slots_ref[pl.ds(48 * s, 16, stride=3), :], 1, axis=0)[top : top + 8]
            for label in range(LABELS):
                row = 16 * label + top
                got = gather_lanes(rows[0], home + 16 * label)
                same = got + gather_lanes(rows[0], 16 * column + label)
                back = gather_lanes(behind, 16 * column + 8 + label)
                got = jnp.where(ahead == 0, same, jnp.where(ahead == 1, got, 0.0))
                d_ref[s, row : row + 8, :] = jnp.where(ahead == 15, back, got)
                if s < 15:
                    got = jnp.where(
                        side < 2,
                        gather_lanes(rows[1], cross + 16 * label),
                        gather_lanes(rows[2], column + 16 * label),
                    )
                    b_ref[s, row : row + 8, :] = jnp.where(side < 3, got, 0.0)
            for place, target in ((8, f_ref), (9, n_ref)):
                got = jnp.where(ring == device, gather_lanes(rows[2], 16 * column + place), 0.0)
                total = jnp.sum(got, axis=0, keepdims=True)
                if top > 0:
                    total = target[s : s + 1, :] + total
                target[s : s + 1, :] = total


def first_step(d_ref, n_ref):
    shape = (BLOCK, BLOCK)
    eye = lanes(shape) == sublanes(shape)
    diagonal = jnp.concatenate(
        [jnp.sum(jnp.where(eye, d_ref[s], 0.0), axis=0, keepdims=True) for s in range(16)], axis=0
    )
    low = jnp.min((0.5 * MASS_SHIFT) * n_ref[...] / diagonal)
    return sum(jnp.where(low >= bound, 1, 0).astype(jnp.int32) for bound in LOWS[1:-2])


def factor_kernel(
    slots_ref, scale_ref, right_ref, left_ref, last_ref, y_ref, d_ref, b_ref, x_ref, p_ref,
    xl_ref, pl_ref, f_ref, n_ref,
):
    unpack_coarse(slots_ref, d_ref, b_ref, f_ref, n_ref)
    b_ref[15] = jnp.zeros((BLOCK, BLOCK), F32)
    first = first_step(d_ref, n_ref)
    begin = 0
    stride = 1
    while stride < 8:
        count = 8 // stride
        odd = [(2 * q + 1) * stride for q in range(count)]
        inverses = invert([d_ref[i] for i in odd], first, scale_ref, x_ref, p_ref)
        ups = [
            dot_high(inverse, b_ref[i - stride], ((1,), (1,))) for i, inverse in zip(odd, inverses)
        ]
        downs = [dot_high(inverse, b_ref[i]) for i, inverse in zip(odd, inverses)]
        products = [jnp.concatenate(pair, axis=1) for pair in zip(ups, downs)]
        for q in range(count):
            right_ref[begin + q, :, :BLOCK] = inverses[q]
            right_ref[begin + q, :, BLOCK:] = products[q]
        grams = [dot_high(b_ref[i - stride], product) for i, product in zip(odd, products)]
        for q in range(count):
            left_ref[begin + q, :BLOCK, :] = turned(ups[q], split2)
            left_ref[begin + q, BLOCK:, :] = turned(downs[q], split2)
        afters = [
            dot_high(left_ref[begin + q, BLOCK:, :], b_ref[i])
            for q, i in enumerate(odd)
            if i + stride < 16
        ]
        for q, i in enumerate(odd):
            change = grams[q][:, :BLOCK]
            if q > 0:
                change = change + afters[q - 1]
            d_ref[i - stride] = d_ref[i - stride] - change
            b_ref[i - stride] = -grams[q][:, BLOCK:]
        begin += count
        stride *= 2
    pair = jnp.concatenate(
        [
            jnp.concatenate([d_ref[0], b_ref[0]], axis=1),
            jnp.concatenate([turned(b_ref[0], split3), d_ref[8]], axis=1),
        ],
        axis=0,
    )
    (last,) = invert([pair], first, scale_ref, xl_ref, pl_ref)
    last_ref[...] = last
    y_ref[...] = coarse_solve(f_ref[...], right_ref, left_ref, last_ref)


def spread_field(y_ref, place_ref, label_of, plane):
    axial = place_ref[0]
    if plane < 0:
        axial = jnp.maximum(axial - 1, 0)
    elif plane > 7:
        axial = jnp.minimum(axial + 1, 15)
    line = jnp.broadcast_to(y_ref[pl.ds(axial, 1), :], (8, BLOCK))
    ring = sublanes((ROWS, 256))
    move = jnp.where(ring < 16, 0, jnp.where(ring < 16 + EDGE, 1, 15))
    spot = label_of(plane).astype(jnp.int32) * 16 + (place_ref[1] + move) % 16
    parts = []
    for top in range(0, ROWS, 8):
        parts.append(
            jnp.concatenate(
                [
                    jnp.take_along_axis(
                        line,
                        spot[top : top + 8, left : left + 128],
                        axis=1,
                        mode="promise_in_bounds",
                    )
                    for left in (0, 128)
                ],
                axis=1,
            )
        )
    return masked(jnp.concatenate(parts, axis=0), present_flags(place_ref, plane))


def fold(values):
    half = values[:8] + values[8:]
    return half[:, :128] + half[:, 128:]


def slot_row(totals):
    count = len(totals)
    stacked = jnp.concatenate(totals, axis=0)
    shape = (8 * count, 128)
    sums = jnp.sum(stacked, axis=1, keepdims=True)
    kept = jnp.where(sublanes(shape) // 8 == lanes(shape), sums, 0.0)
    return jnp.sum(kept, axis=0, keepdims=True)


class Totals:
    def __init__(self, count):
        self.values = [None] * count

    def add(self, at, term):
        self.values[at] = term if self.values[at] is None else self.values[at] + term

    def by_label(self, labels, field):
        for k in range(LABELS):
            self.add(k, fold(jnp.where(labels == float(k), field, 0.0)))


def start_kernel(
    low_ref, mid_ref, high_ref, km_ref, ke_ref, diag_ref, y_ref, place_ref,
    x_out, r_out, image_ref, slot_ref, v_ref, w_ref,
):
    k_ref = Planes(km_ref, ke_ref)
    def label_of(plane):
        return piece(low_ref, mid_ref, high_ref, 3, plane)

    for plane in range(-3, 11):
        v_ref[plane + 3] = spread_field(y_ref, place_ref, label_of, plane)

    def put_residual(plane, image):
        load = piece(low_ref, mid_ref, high_ref, 0, plane)
        w_ref[plane + 2] = masked(load - image, present_flags(place_ref, plane))

    stencil(lambda plane: v_ref[plane + 3], k_ref, diag_ref, -2, 10, put_residual)
    totals = Totals(9)

    def put_image(plane, image):
        image_ref[plane + 1] = image
        if 0 <= plane < 8:
            totals.by_label(mid_ref[3, plane, 0:16], image[:16])
            own = w_ref[plane + 2, 0:16]
            totals.add(8, fold(own * own))

    stencil(lambda plane: w_ref[plane + 2], k_ref, diag_ref, -1, 9, put_image)
    for plane in range(8):
        x_out[plane] = v_ref[plane + 3, 0:16]
        r_out[plane] = w_ref[plane + 2, 0:16]
    slot_ref[...] = jnp.broadcast_to(slot_row(totals.values), (256, 128))


def label_chooser():
    shape = (128, BLOCK)
    return jnp.where(sublanes(shape) == lanes(shape) // 16, 1.0, 0.0).astype(BF16)


def first_kernel(
    got_ref, right_ref, left_ref, last_ref, low_ref, mid_ref, high_ref, km_ref, ke_ref, diag_ref, image_ref,
    r_ref, place_ref, w_out, d_out, aw_out, slot_ref, y_ref, v_ref, w_ref,
):
    k_ref = Planes(km_ref, ke_ref)
    got = got_ref[...]
    coarse_rhs = coarse_rows(got, label_chooser())
    y_ref[...] = coarse_solve(coarse_rhs, right_ref, left_ref, last_ref)

    def label_of(plane):
        return piece(low_ref, mid_ref, high_ref, 3, plane)

    for plane in range(-2, 10):
        v_ref[plane + 2] = spread_field(y_ref, place_ref, label_of, plane)
    totals = Totals(12)

    def put_direction_image(plane, image):
        w_ref[plane + 1] = masked(image_ref[plane + 1] - image, present_flags(place_ref, plane))

    stencil(lambda plane: v_ref[plane + 2], k_ref, diag_ref, -1, 9, put_direction_image)

    def put_second(plane, image):
        own = w_ref[plane + 1, 0:16]
        image = image[:16]
        residual = r_ref[plane]
        direction = residual - v_ref[plane + 2, 0:16]
        w_out[plane] = own
        d_out[plane] = direction
        aw_out[plane] = image
        totals.by_label(mid_ref[3, plane, 0:16], image)
        totals.add(8, fold(direction * own))
        totals.add(9, fold(own * own))
        totals.add(10, fold(residual * own))
        totals.add(11, fold(own * image))

    stencil(lambda plane: w_ref[plane + 1], k_ref, diag_ref, 0, 8, put_second)
    square = jnp.sum(got, axis=0, keepdims=True) * (1.0 / 256.0)
    shape = (1, 128)
    square = jnp.sum(jnp.where(lanes(shape) == 8, square, 0.0), axis=1, keepdims=True)
    row = slot_row(totals.values) + jnp.where(lanes(shape) == 12, square, 0.0)
    slot_ref[...] = jnp.broadcast_to(row, (256, 128))


def last_kernel(
    got_ref, right_ref, left_ref, last_ref, low_ref, mid_ref, high_ref, km_ref, ke_ref, diag_ref,
    x_ref, r_ref, w_ref, d_ref, aw_ref, place_ref, x_out, r_out, y_ref, v_ref,
):
    k_ref = Planes(km_ref, ke_ref)
    got = got_ref[...]
    coarse_rhs = coarse_rows(got, label_chooser())
    solved = coarse_solve(coarse_rhs, right_ref, left_ref, last_ref)
    y_ref[...] = solved
    row = jnp.sum(got, axis=0, keepdims=True)

    def scalar(at):
        return jnp.sum(jnp.where(lanes((1, 128)) == at, row, 0.0), axis=1, keepdims=True)

    dw, ww, rw, waw, rr = (scalar(at) for at in (8, 9, 10, 11, 12))
    hq = jnp.sum(jnp.sum(coarse_rhs * solved, axis=1, keepdims=True), axis=0, keepdims=True)
    alpha = rr / dw
    rr_next = rr - 2.0 * alpha * rw + alpha * alpha * ww
    beta = rr_next / rr
    gain = 1.0 + beta
    curvature = gain * gain * dw - 2.0 * gain * alpha * ww + alpha * alpha * (waw - hq)
    alpha_next = rr_next / curvature

    def label_of(plane):
        return piece(low_ref, mid_ref, high_ref, 3, plane)

    for plane in range(-1, 9):
        v_ref[plane + 1] = spread_field(y_ref, place_ref, label_of, plane)

    def put(plane, image):
        w = w_ref[plane]
        d = d_ref[plane]
        u = aw_ref[plane] - image[:16]
        d_next = gain * d - alpha * (w - v_ref[plane + 1, 0:16])
        w_next = gain * w - alpha * u
        x_out[plane] = x_ref[plane] + alpha * d + alpha_next * d_next
        r_out[plane] = r_ref[plane] - alpha * w - alpha_next * w_next

    stencil(lambda plane: v_ref[plane + 1], k_ref, diag_ref, 0, 8, put)


VMEM = pl.BlockSpec(memory_space=pltpu.VMEM)
SMEM = pl.BlockSpec(memory_space=pltpu.SMEM)


def shape_of(*dims):
    return jax.ShapeDtypeStruct(dims, F32)


def call(kernel, name, outs, scratch, in_specs, mib, cost=None):
    return pl.pallas_call(
        kernel,
        name=name,
        out_shape=outs,
        in_specs=in_specs,
        out_specs=tuple(VMEM for _ in outs),
        scratch_shapes=scratch,
        cost_estimate=cost,
        compiler_params=pltpu.CompilerParams(vmem_limit_bytes=mib * 1024 * 1024),
    )


def ring_pairs(peers):
    up = [(i, (i + 1) % peers) for i in range(peers)]
    return up, [(j, i) for i, j in up]


def exchange_all(slots):
    width = slots.shape[0] // 256
    return lax.all_to_all(slots.reshape(256, width * 128), AXIAL_CIRC, 0, 0, tiled=True).reshape(
        256 * width, 128
    )


def exchange(slots, count):
    return lax.all_to_all(slots.reshape(256, count, 128), AXIAL_CIRC, 0, 0, tiled=True).reshape(
        256 * count, 128
    )


def shards(right_side, stiffness, material, groups):
    place = jnp.stack([lax.axis_index(AXIAL), lax.axis_index(CIRC)]).astype(jnp.int32)

    def fields(rows):
        parts = (right_side, stiffness, material, groups)
        return jnp.stack([part[:, rows].astype(F32) for part in parts])

    up, down = ring_pairs(16)
    before = lax.ppermute(fields(slice(16 - EDGE, 16)), CIRC, up)
    after = lax.ppermute(fields(slice(0, EDGE)), CIRC, down)
    middle = jnp.concatenate([fields(slice(0, 16)), after, before], axis=2)
    low = lax.ppermute(middle[:, 8 - DEPTH :], AXIAL, up)
    high = lax.ppermute(middle[:, :DEPTH], AXIAL, down)
    table = np.zeros((16, 128), np.float32)
    table[:13, :CLASSES] = coefficient_table().T
    ext = (ROWS, 256)
    table = jnp.asarray(table)
    k_mid, even, odd = call(
        inner_kernel,
        "inner",
        (shape_of(8, 13, *ext), shape_of(64, 80), shape_of(64, 144)),
        [pltpu.VMEM((8, 9, 16, 256), F32)],
        [VMEM, VMEM],
        20,
        pl.CostEstimate(flops=40_000_000, transcendentals=0, bytes_accessed=4_000_000),
    )(middle, table)
    k_end, diag, slots = call(
        setup_kernel,
        "setup",
        (shape_of(6, 13, *ext), shape_of(12, *ext), shape_of(768, 128)),
        [],
        [VMEM, VMEM, VMEM, VMEM, SMEM, VMEM, VMEM, VMEM],
        20,
    )(low, middle, high, table, place, k_mid, even, odd)
    gathered = exchange_all(slots)
    square = (BLOCK, BLOCK)
    double = (2 * BLOCK, 2 * BLOCK)
    right, left, last, y = call(
        factor_kernel,
        "factor",
        (shape_of(14, BLOCK, 3 * BLOCK), shape_of(14, 2 * BLOCK, BLOCK), shape_of(*double), shape_of(16, BLOCK)),
        [
            pltpu.VMEM((16, *square), F32),
            pltpu.VMEM((16, *square), F32),
            pltpu.VMEM((8, *square), F32),
            pltpu.VMEM((8, *square), F32),
            pltpu.VMEM((1, *double), F32),
            pltpu.VMEM((1, *double), F32),
            pltpu.VMEM((16, BLOCK), F32),
            pltpu.VMEM((16, BLOCK), F32),
        ],
        [VMEM, SMEM],
        24,
    )(gathered, jnp.asarray(np.array(SCALES, np.float32)))
    own = (8, 16, 256)
    x0, r0, image, slots = call(
        start_kernel,
        "start",
        (shape_of(*own), shape_of(*own), shape_of(10, *ext), shape_of(256, 128)),
        [pltpu.VMEM((14, *ext), F32), pltpu.VMEM((12, *ext), F32)],
        [VMEM] * 7 + [SMEM],
        24,
    )(low, middle, high, k_mid, k_end, diag, y, place)
    gathered = exchange(slots, 1)
    w0, d0, aw0, slots = call(
        first_kernel,
        "first",
        (shape_of(*own), shape_of(*own), shape_of(*own), shape_of(256, 128)),
        [pltpu.VMEM((16, BLOCK), F32), pltpu.VMEM((12, *ext), F32), pltpu.VMEM((10, *ext), F32)],
        [VMEM] * 12 + [SMEM],
        24,
    )(gathered, right, left, last, low, middle, high, k_mid, k_end, diag, image, r0, place)
    gathered = exchange(slots, 1)
    return call(
        last_kernel,
        "last",
        (shape_of(*own), shape_of(*own)),
        [pltpu.VMEM((16, BLOCK), F32), pltpu.VMEM((10, *ext), F32)],
        [VMEM] * 15 + [SMEM],
        24,
    )(gathered, right, left, last, low, middle, high, k_mid, k_end, diag, x0, r0, w0, d0, aw0, place)


def solution(mesh):
    split = Mesh(mesh.devices.reshape(8, 2, 4, 4), ("axial_0", "axial_1", "circ_0", "circ_1"))
    placed = P(AXIAL, CIRC, None)
    return jax.shard_map(
        shards,
        mesh=split,
        in_specs=(placed,) * 4,
        out_specs=(placed, placed),
        check_vma=False,
    )
```

```python
import math

import jax
import jax.numpy as jnp
import numpy as np
from jax import lax
from jax.experimental import pallas as pl
from jax.experimental.pallas import tpu as pltpu
from jax.sharding import Mesh
from jax.sharding import PartitionSpec as P

LABELS = 8
CLASSES = 16
CIRC = ("circ_0", "circ_1")
AXIAL = ("axial_0", "axial_1")
AXIAL_CIRC = ("axial_0", "axial_1", "circ_0", "circ_1")
MASS_SHIFT = 0.02
HIGH = lax.Precision.HIGHEST
HALF_STEPS = (
    (0, 0, 1),
    (0, 1, -1),
    (0, 1, 0),
    (0, 1, 1),
    (1, -1, -1),
    (1, -1, 0),
    (1, -1, 1),
    (1, 0, -1),
    (1, 0, 0),
    (1, 0, 1),
    (1, 1, -1),
    (1, 1, 0),
    (1, 1, 1),
)
STEP_OF = {step: place for place, step in enumerate(HALF_STEPS)}
SHIFTS = [(sy, sz) for sy in (-1, 0, 1) for sz in (-1, 0, 1)]
ROWS = 24
EDGE = 4
DEPTH = 3
BLOCK = 128
F32 = jnp.float32
BF16 = jnp.bfloat16


def coefficient_table():
    rows_out = []
    for material_id in range(CLASSES):
        fiber_angle = math.pi * (material_id % 8) / 8.0
        if material_id < 8:
            fiber_dir = (math.cos(fiber_angle), math.sin(fiber_angle), 0.0)
            strength, anisotropy = (1.0, 6.0)
        else:
            fiber_dir = (0.6 * math.cos(fiber_angle), 0.6 * math.sin(fiber_angle), 0.8)
            strength, anisotropy = (0.35, 2.0)
        line_values = []
        for offset in HALF_STEPS:
            length_sq = float(offset[0] * offset[0] + offset[1] * offset[1] + offset[2] * offset[2])
            along_fiber = (
                fiber_dir[0] * offset[0] + fiber_dir[1] * offset[1] + fiber_dir[2] * offset[2]
            )
            line_values.append(
                strength * (0.15 + anisotropy * along_fiber * along_fiber / length_sq) / length_sq
            )
        rows_out.append(line_values)
    return np.array(rows_out, dtype=np.float32)


def inverse_scales():
    table = coefficient_table().astype(np.float64)
    widest = MASS_SHIFT + 0.3 * (table.sum(axis=1).max() + table.max(axis=0).sum())
    low = 0.5 * MASS_SHIFT / widest
    scales, lows = [], []
    while 1.0 - low > 2e-7:
        scales.append(2.0 / (1.0 + low))
        lows.append(low)
        low = 4.0 * low / (1.0 + low) ** 2
    return scales, lows


SCALES, LOWS = inverse_scales()


def lanes(shape):
    return lax.broadcasted_iota(jnp.int32, shape, len(shape) - 1)


def sublanes(shape):
    return lax.broadcasted_iota(jnp.int32, shape, len(shape) - 2)


def shift_z(values, move, fill):
    if move == 0:
        return values
    length = values.shape[-1]
    turned = pltpu.roll(values, (-move) % length, axis=1)
    edge = length - 1 if move > 0 else 0
    return jnp.where(lanes(values.shape) == edge, fill, turned)


def shift_y(values, move):
    if move == 0:
        return values
    return pltpu.roll(values, (-move) % values.shape[0], axis=0)


def shifted(values, fill):
    by_z = {sz: shift_z(values, sz, fill) for sz in (-1, 0, 1)}
    return {(sy, sz): shift_y(by_z[sz], sy) for sy, sz in SHIFTS}


def present_flags(place_ref, plane):
    if plane < 0:
        return place_ref[0] > 0
    if plane > 7:
        return place_ref[0] < 15
    return None


def masked(values, flag):
    if flag is None:
        return values
    return values * jnp.where(flag, 1.0, 0.0).astype(F32)


def stencil(v_at, k_ref, diag_ref, start, stop, emit):
    wide = {}
    made = {}

    def prepare(plane):
        values = v_at(plane)
        wide[plane] = shifted(values, 0.0)
        made[plane] = [k_ref[plane + DEPTH, j] * values for j in range(13)]

    prepare(start - 1)
    prepare(start)
    for plane in range(start, stop):
        prepare(plane + 1)
        total = None
        for j, (ox, oy, oz) in enumerate(HALF_STEPS):
            pair = wide[plane + ox][(oy, oz)] + wide[plane - ox][(-oy, -oz)]
            term = k_ref[plane + DEPTH, j] * pair
            total = term if total is None else total + term
        for sz in (-1, 0, 1):
            by_y = None
            for sy in (-1, 0, 1):
                part = made[plane + 1][STEP_OF[(1, sy, sz)]] + made[plane - 1][STEP_OF[(1, -sy, -sz)]]
                if (0, sy, sz) in STEP_OF:
                    part = part + made[plane][STEP_OF[(0, sy, sz)]]
                elif (0, -sy, -sz) in STEP_OF:
                    part = part + made[plane][STEP_OF[(0, -sy, -sz)]]
                part = shift_y(part, sy)
                by_y = part if by_y is None else by_y + part
            total = total + shift_z(by_y, sz, 0.0)
        emit(plane, diag_ref[plane + 2] * wide[plane][(0, 0)] - 0.5 * total)
        del wide[plane - 1], made[plane - 1]


def piece(low_ref, mid_ref, high_ref, field, plane):
    if plane < 0:
        return low_ref[field, plane + DEPTH]
    if plane > 7:
        return high_ref[field, plane - 8]
    return mid_ref[field, plane]


def split3(values):
    high = values.astype(BF16)
    rest = values - high.astype(F32)
    mid = rest.astype(BF16)
    low = (rest - mid.astype(F32)).astype(BF16)
    return high, mid, low


def dot(a, b, dims=((1,), (0,))):
    return lax.dot_general(a, b, (dims, ((), ())), preferred_element_type=F32)


def dot_high(a, b, dims=((1,), (0,))):
    return lax.dot_general(
        a, b, (dims, ((), ())), precision=HIGH, preferred_element_type=F32
    )


def pick(values, chooser):
    return sum(dot(part, chooser) for part in split3(values))


class Planes:
    def __init__(self, mid_ref, end_ref):
        self.mid_ref = mid_ref
        self.end_ref = end_ref

    def place(self, key):
        plane = key[0] - DEPTH
        if 0 <= plane < 8:
            return self.mid_ref, (plane, *key[1:])
        return self.end_ref, ((plane + DEPTH if plane < 0 else plane - 5), *key[1:])

    def __getitem__(self, key):
        ref, at = self.place(key)
        return ref[at]

    def __setitem__(self, key, values):
        ref, at = self.place(key)
        ref[at] = values


def fill_stiffness(k_ref, table_ref, plane, stiff, kind):
    kind = kind.astype(jnp.int32)
    for j in range(13):
        row = jnp.broadcast_to(table_ref[j : j + 1, :], (8, 128))
        parts = []
        for top in range(0, ROWS, 8):
            line = [
                gather_lanes(row, kind[top : top + 8, left : left + 128]) for left in (0, 128)
            ]
            parts.append(jnp.concatenate(line, axis=1))
        k_ref[plane + DEPTH, j] = stiff * jnp.concatenate(parts, axis=0)


def by_label(pairs):
    out = []
    for label in range(LABELS):
        total = None
        for weight, target in pairs:
            term = jnp.where(target == float(label), weight, 0.0)
            total = term if total is None else total + term
        out.append(total)
    return out


def chosen_rows(home):
    return jnp.concatenate(
        [jnp.where(home == float(k), 1.0, 0.0) for k in range(LABELS)], axis=0
    ).astype(BF16)


def cell_sums(chosen, right):
    return sum(dot(chosen, part, ((1,), (1,))) for part in split3(right))


def inner_kernel(mid_ref, table_ref, km_ref, even_ref, odd_ref, label_ref):
    k_ref = Planes(km_ref, None)
    for plane in range(8):
        fill_stiffness(k_ref, table_ref, plane, mid_ref[1, plane], mid_ref[2, plane])
        spots = shifted(mid_ref[3, plane], -1.0)
        for place, shift in enumerate(SHIFTS):
            label_ref[plane, place] = spots[shift][:16]
    row16 = sublanes((16, 256))
    ones = jnp.ones((8, 256), F32)
    sums = {}
    for plane in range(8):
        own, up = [], []
        for j, (ox, oy, oz) in enumerate(HALF_STEPS):
            if ox == 0 or plane < 7:
                across = shift_z(shift_y(k_ref[plane + ox + DEPTH, j], oy), oz, 0.0)[:16]
                weight = -0.5 * (k_ref[plane + DEPTH, j, 0:16] + across)
                target = label_ref[plane + ox, SHIFTS.index((oy, oz))]
                if oy == 0:
                    own.append((weight, target))
                else:
                    edge = 15 if oy == 1 else 0
                    own.append((jnp.where(row16 == edge, 0.0, weight), target))
                    if oy == 1:
                        up.append((jnp.where(row16 == 15, weight, 0.0)[8:], target[8:]))
            if oy == -1 and plane > 0:
                back = shift_z(shift_y(k_ref[plane - 1 + DEPTH, j], -oy), -oz, 0.0)[8:16]
                back = -0.5 * (k_ref[plane + DEPTH, j, 8:16] + back)
                source = label_ref[plane - 1, SHIFTS.index((-oy, -oz)), 8:16]
                up.append((jnp.where(row16[8:] == 15, back, 0.0), source))
        own = by_label(own)
        sides = ([], by_label(up))
        load = mid_ref[0, plane, 0:16]
        home = label_ref[plane, SHIFTS.index((0, 0))]
        for half in (0, 1):
            rows = slice(8 * half, 8 * half + 8)
            right = jnp.concatenate([o[rows] for o in own] + [load[rows], ones] + sides[half], axis=0)
            got = cell_sums(chosen_rows(home[rows]), right)
            sums[half] = got if half not in sums else sums[half] + got
    even_ref[...] = sums[0]
    odd_ref[...] = sums[1]


def setup_kernel(
    low_ref, mid_ref, high_ref, table_ref, place_ref, km_ref, even_ref, odd_ref,
    ke_ref, diag_ref, slot_ref,
):
    k_ref = Planes(km_ref, ke_ref)
    for plane in (-3, -2, -1, 8, 9, 10):
        stiff = masked(piece(low_ref, mid_ref, high_ref, 1, plane), present_flags(place_ref, plane))
        kind = piece(low_ref, mid_ref, high_ref, 2, plane)
        fill_stiffness(k_ref, table_ref, plane, stiff, kind)
    for plane in range(-2, 10):
        own = None
        total = None
        for j in range(13):
            term = k_ref[plane + DEPTH, j]
            own = term if own is None else own + term
        for sz in (-1, 0, 1):
            by_y = None
            for sy in (-1, 0, 1):
                part = k_ref[plane + 1 + DEPTH, STEP_OF[(1, sy, sz)]]
                part = part + k_ref[plane - 1 + DEPTH, STEP_OF[(1, -sy, -sz)]]
                if (0, sy, sz) in STEP_OF:
                    part = part + k_ref[plane + DEPTH, STEP_OF[(0, sy, sz)]]
                elif (0, -sy, -sz) in STEP_OF:
                    part = part + k_ref[plane + DEPTH, STEP_OF[(0, -sy, -sz)]]
                part = shift_y(part, sy)
                by_y = part if by_y is None else by_y + part
            by_y = shift_z(by_y, sz, 0.0)
            total = by_y if total is None else total + by_y
        diag_ref[plane + 2] = MASS_SHIFT + own + 0.5 * total
    middle = None
    for plane in range(8):
        for top in (0, 8):
            rows = slice(top, top + 8)
            got = cell_sums(
                chosen_rows(mid_ref[3, plane, rows]), 0.5 * diag_ref[plane + 2, rows]
            )
            middle = got if middle is None else middle + got
    spots = {shift: value[:16] for shift, value in shifted(high_ref[3, 0], -1.0).items()}
    row16 = sublanes((16, 256))
    nexts, up, down = [], [], []
    for j, (ox, oy, oz) in enumerate(HALF_STEPS):
        if ox == 1:
            across = shift_z(shift_y(k_ref[8 + DEPTH, j], oy), oz, 0.0)[:16]
            weight = -0.5 * (k_ref[7 + DEPTH, j, 0:16] + across)
            target = spots[(oy, oz)]
            if oy == 0:
                nexts.append((weight, target))
            elif oy == 1:
                nexts.append((jnp.where(row16 == 15, 0.0, weight), target))
                up.append((jnp.where(row16 == 15, weight, 0.0)[8:], target[8:]))
            else:
                nexts.append((jnp.where(row16 == 0, 0.0, weight), target))
                down.append((jnp.where(row16 == 0, weight, 0.0)[:8], target[:8]))
    nexts, up, down = by_label(nexts), by_label(up), by_label(down)
    sums = [even_ref[...], odd_ref[...]]
    for half in (0, 1):
        rows = slice(8 * half, 8 * half + 8)
        right = jnp.concatenate([o[rows] for o in nexts] + (down, up)[half], axis=0)
        sums.append(cell_sums(chosen_rows(mid_ref[3, 7, rows]), right))

    shape = (64, 8)
    total = jnp.sum(
        jnp.where(sublanes(shape) % 8 == lanes(shape), middle, 0.0), axis=1, keepdims=True
    )
    shape = (64, 3 * 128)
    total = jnp.where(
        jnp.logical_and(lanes(shape) < 128, lanes(shape) % 16 == sublanes(shape) // 8), total, 0.0
    )
    for which in range(4):
        width = sums[which].shape[1]
        shape = (64, width)
        kept = jnp.where(sublanes(shape) % 8 == lanes(shape) % 8, sums[which], 0.0)
        shape = (width, 3 * 128)
        group = sublanes(shape) // 8
        if which < 2:
            spot = jnp.where(group < 8, group, jnp.where(group < 10, 32 + group, group - 2))
        else:
            spot = jnp.where(group < 8, 24 + group, (8 if which == 2 else 24) + group)
        here = (lanes(shape) // 128) * 16 + lanes(shape) % 16
        total = total + pick(kept, jnp.where(here == spot, 1.0, 0.0).astype(BF16))
    shape = (64, 3 * 128)
    total = jnp.where(sublanes(shape) // 8 == (lanes(shape) % 128) // 16, total, 0.0)
    total = jnp.sum(total, axis=0, keepdims=True)
    rows = [total[:, 128 * r : 128 * r + 128] for r in range(3)]
    slots = jnp.concatenate(rows * 8, axis=0)
    for at in range(0, 768, 24):
        slot_ref[at : at + 24, :] = slots


def coarse_rows(values, chooser):
    spread = pick(values, chooser)
    shape = (256, BLOCK)
    kept = jnp.where(sublanes(shape) % 16 == lanes(shape) % 16, spread, 0.0)
    return jnp.sum(kept.reshape(16, 16, BLOCK), axis=1)


def as_columns(rows):
    count = len(rows)
    stacked = jnp.concatenate(rows + [jnp.zeros((1, BLOCK), F32)] * (8 - count), axis=0)
    turned = stacked.T
    return [turned[:, i : i + 1] for i in range(count)]


def coarse_solve(coarse_rhs, right_ref, left_ref, last_ref):
    now = [coarse_rhs[i : i + 1, :] for i in range(16)]
    begin = 0
    stages = []
    while len(now) > 2:
        count = len(now)
        odd = now[1::2]
        even = now[0::2]
        solved = []
        for q, column in enumerate(as_columns(odd)):
            product = jnp.sum(right_ref[begin + q] * column, axis=0, keepdims=True)
            solved.append(product[:, :BLOCK])
            even[q] = even[q] - product[:, BLOCK : 2 * BLOCK]
            if q + 1 < len(even):
                even[q + 1] = even[q + 1] - product[:, 2 * BLOCK :]
        stages.append((begin, solved))
        begin += count // 2
        now = even
    column = jnp.concatenate(as_columns(now), axis=0)
    both = jnp.sum(last_ref[...] * column, axis=0, keepdims=True)
    found = [both[:, :BLOCK], both[:, BLOCK:]]
    for begin, solved in reversed(stages):
        columns = as_columns(found)
        merged = []
        for q, value in enumerate(solved):
            value = value - jnp.sum(left_ref[begin + q, :BLOCK] * columns[q], axis=0, keepdims=True)
            if q + 1 < len(found):
                value = value - jnp.sum(
                    left_ref[begin + q, BLOCK:] * columns[q + 1], axis=0, keepdims=True
                )
            merged += [found[q], value]
        found = merged
    return jnp.concatenate(found, axis=0)


def split2(values):
    high = values.astype(BF16)
    return high, (values - high.astype(F32)).astype(BF16)


def left_stack(halves):
    high, low = halves
    return jnp.concatenate([high, high, low], axis=1)


def right_stack(halves):
    high, low = halves
    return jnp.concatenate([high, low, high], axis=0)


def invert(blocks, begin, scale_ref, x_ref, p_ref):
    shape = blocks[0].shape
    size = shape[0]
    eye = jnp.where(lanes(shape) == sublanes(shape), 1.0, 0.0).astype(F32)
    for q, block in enumerate(blocks):
        kept = eye * block
        across = 1.0 / jnp.sum(kept, axis=0, keepdims=True)
        down = 1.0 / jnp.sum(kept, axis=1, keepdims=True)
        c = 0.5 * scale_ref[begin]
        x_ref[q] = (2.0 * c * eye - (c * c) * (block * down)) * across
    for q, block in enumerate(blocks):
        p_ref[q] = dot(left_stack(split2(block)), right_stack(split2(x_ref[q])))

    def step(k, carry):
        c = scale_ref[k]
        for q in range(len(blocks)):
            x = x_ref[q]
            p = p_ref[q]
            halves = split2(p)
            both = jnp.concatenate([left_stack(halves), left_stack(split2(x))], axis=0)
            product = dot(both, right_stack(halves))
            p_ref[q] = (2.0 * c) * p - (c * c) * product[:size]
            x_ref[q] = (2.0 * c) * x - (c * c) * product[size:]
        return carry

    lax.fori_loop(begin + 1, len(SCALES) - 2, step, 0)
    values = [x_ref[q] for q in range(len(blocks))]
    rests = [
        eye - dot(left_stack(split2(s)), right_stack(split2(x))) for s, x in zip(blocks, values)
    ]
    values = [x + dot(x.astype(BF16), r.astype(BF16)) for x, r in zip(values, rests)]
    rests = [eye - dot_high(s, x) for s, x in zip(blocks, values)]
    return [x + dot(x.astype(BF16), r.astype(BF16)) for x, r in zip(values, rests)]


def turned(values):
    shape = (BLOCK, BLOCK)
    eye = jnp.where(lanes(shape) == sublanes(shape), 1.0, 0.0).astype(BF16)
    return sum(dot(eye, part, ((1,), (1,))) for part in split3(values))


def gather_lanes(values, spot):
    return jnp.take_along_axis(values, spot, axis=1, mode="promise_in_bounds")


def unpack_coarse(slots_ref, d_ref, b_ref, f_ref, n_ref):
    for top in (0, 8):
        shape = (8, BLOCK)
        device = sublanes(shape) + top
        ring = lanes(shape) % 16
        column = lanes(shape) // 16
        ahead = (ring - device + 16) % 16
        side = (ahead + 1) % 16
        home = jnp.minimum(ahead, 1) * 8 + column
        cross = jnp.minimum(side, 1) * 8 + column
        for s in range(16):
            at = 48 * s + 3 * top
            rows = [slots_ref[pl.ds(at + r, 8, stride=3), :] for r in range(3)]
            for label in range(LABELS):
                row = 16 * label + top
                got = gather_lanes(rows[0], home + 16 * label)
                d_ref[s, row : row + 8, :] = jnp.where(ahead < 2, got, 0.0)
                if s < 15:
                    got = jnp.where(
                        side < 2,
                        gather_lanes(rows[1], cross + 16 * label),
                        gather_lanes(rows[2], column + 16 * label),
                    )
                    b_ref[s, row : row + 8, :] = jnp.where(side < 3, got, 0.0)
            for place, target in ((8, f_ref), (9, n_ref)):
                got = jnp.where(ring == device, gather_lanes(rows[2], 16 * column + place), 0.0)
                total = jnp.sum(got, axis=0, keepdims=True)
                if top > 0:
                    total = target[s : s + 1, :] + total
                target[s : s + 1, :] = total


def first_step(d_ref, n_ref):
    shape = (BLOCK, BLOCK)
    eye = lanes(shape) == sublanes(shape)
    diagonal = jnp.concatenate(
        [jnp.sum(jnp.where(eye, d_ref[s], 0.0), axis=0, keepdims=True) for s in range(16)], axis=0
    )
    low = jnp.min((0.5 * MASS_SHIFT) * n_ref[...] / diagonal)
    return sum(jnp.where(low >= bound, 1, 0).astype(jnp.int32) for bound in LOWS[1:-2])


def factor_kernel(
    slots_ref, scale_ref, right_ref, left_ref, last_ref, y_ref, d_ref, b_ref, x_ref, p_ref,
    xl_ref, pl_ref, f_ref, n_ref,
):
    unpack_coarse(slots_ref, d_ref, b_ref, f_ref, n_ref)
    b_ref[15] = jnp.zeros((BLOCK, BLOCK), F32)
    for i in range(16):
        d_ref[i] = d_ref[i] + turned(d_ref[i])
    first = first_step(d_ref, n_ref)
    begin = 0
    stride = 1
    while stride < 8:
        count = 8 // stride
        odd = [(2 * q + 1) * stride for q in range(count)]
        inverses = invert([d_ref[i] for i in odd], first, scale_ref, x_ref, p_ref)
        ups = [
            dot_high(inverse, b_ref[i - stride], ((1,), (1,))) for i, inverse in zip(odd, inverses)
        ]
        downs = [dot_high(inverse, b_ref[i]) for i, inverse in zip(odd, inverses)]
        products = [jnp.concatenate(pair, axis=1) for pair in zip(ups, downs)]
        for q in range(count):
            right_ref[begin + q, :, :BLOCK] = inverses[q]
            right_ref[begin + q, :, BLOCK:] = products[q]
        grams = [dot_high(b_ref[i - stride], product) for i, product in zip(odd, products)]
        for q in range(count):
            left_ref[begin + q, :BLOCK, :] = ups[q].T
            left_ref[begin + q, BLOCK:, :] = downs[q].T
        afters = [
            dot_high(left_ref[begin + q, BLOCK:, :], b_ref[i])
            for q, i in enumerate(odd)
            if i + stride < 16
        ]
        for q, i in enumerate(odd):
            change = grams[q][:, :BLOCK]
            if q > 0:
                change = change + afters[q - 1]
            d_ref[i - stride] = d_ref[i - stride] - change
            b_ref[i - stride] = -grams[q][:, BLOCK:]
        begin += count
        stride *= 2
    pair = jnp.concatenate(
        [
            jnp.concatenate([d_ref[0], b_ref[0]], axis=1),
            jnp.concatenate([turned(b_ref[0]), d_ref[8]], axis=1),
        ],
        axis=0,
    )
    (last,) = invert([pair], first, scale_ref, xl_ref, pl_ref)
    last_ref[...] = last
    y_ref[...] = coarse_solve(f_ref[...], right_ref, left_ref, last_ref)


def spread_field(y_ref, place_ref, label_of, plane):
    axial = place_ref[0]
    if plane < 0:
        axial = jnp.maximum(axial - 1, 0)
    elif plane > 7:
        axial = jnp.minimum(axial + 1, 15)
    line = jnp.broadcast_to(y_ref[pl.ds(axial, 1), :], (8, BLOCK))
    ring = sublanes((ROWS, 256))
    move = jnp.where(ring < 16, 0, jnp.where(ring < 16 + EDGE, 1, 15))
    spot = label_of(plane).astype(jnp.int32) * 16 + (place_ref[1] + move) % 16
    parts = []
    for top in range(0, ROWS, 8):
        parts.append(
            jnp.concatenate(
                [
                    jnp.take_along_axis(
                        line,
                        spot[top : top + 8, left : left + 128],
                        axis=1,
                        mode="promise_in_bounds",
                    )
                    for left in (0, 128)
                ],
                axis=1,
            )
        )
    return masked(jnp.concatenate(parts, axis=0), present_flags(place_ref, plane))


def fold(values):
    half = values[:8] + values[8:]
    return half[:, :128] + half[:, 128:]


def slot_row(totals):
    count = len(totals)
    stacked = jnp.concatenate(totals, axis=0)
    shape = (8 * count, 128)
    sums = jnp.sum(stacked, axis=1, keepdims=True)
    kept = jnp.where(sublanes(shape) // 8 == lanes(shape), sums, 0.0)
    return jnp.sum(kept, axis=0, keepdims=True)


class Totals:
    def __init__(self, count):
        self.values = [None] * count

    def add(self, at, term):
        self.values[at] = term if self.values[at] is None else self.values[at] + term

    def by_label(self, labels, field):
        for k in range(LABELS):
            self.add(k, fold(jnp.where(labels == float(k), field, 0.0)))


def start_kernel(
    low_ref, mid_ref, high_ref, km_ref, ke_ref, diag_ref, y_ref, place_ref,
    x_out, r_out, image_ref, slot_ref, v_ref, w_ref,
):
    k_ref = Planes(km_ref, ke_ref)
    def label_of(plane):
        return piece(low_ref, mid_ref, high_ref, 3, plane)

    for plane in range(-3, 11):
        v_ref[plane + 3] = spread_field(y_ref, place_ref, label_of, plane)

    def put_residual(plane, image):
        load = piece(low_ref, mid_ref, high_ref, 0, plane)
        w_ref[plane + 2] = masked(load - image, present_flags(place_ref, plane))

    stencil(lambda plane: v_ref[plane + 3], k_ref, diag_ref, -2, 10, put_residual)
    totals = Totals(9)

    def put_image(plane, image):
        image_ref[plane + 1] = image
        if 0 <= plane < 8:
            totals.by_label(mid_ref[3, plane, 0:16], image[:16])
            own = w_ref[plane + 2, 0:16]
            totals.add(8, fold(own * own))

    stencil(lambda plane: w_ref[plane + 2], k_ref, diag_ref, -1, 9, put_image)
    for plane in range(8):
        x_out[plane] = v_ref[plane + 3, 0:16]
        r_out[plane] = w_ref[plane + 2, 0:16]
    slot_ref[...] = jnp.broadcast_to(slot_row(totals.values), (256, 128))


def label_chooser():
    shape = (128, BLOCK)
    return jnp.where(sublanes(shape) == lanes(shape) // 16, 1.0, 0.0).astype(BF16)


def first_kernel(
    got_ref, right_ref, left_ref, last_ref, low_ref, mid_ref, high_ref, km_ref, ke_ref, diag_ref, image_ref,
    r_ref, place_ref, w_out, d_out, aw_out, slot_ref, y_ref, v_ref, w_ref,
):
    k_ref = Planes(km_ref, ke_ref)
    got = got_ref[...]
    coarse_rhs = coarse_rows(got, label_chooser())
    y_ref[...] = coarse_solve(coarse_rhs, right_ref, left_ref, last_ref)

    def label_of(plane):
        return piece(low_ref, mid_ref, high_ref, 3, plane)

    for plane in range(-2, 10):
        v_ref[plane + 2] = spread_field(y_ref, place_ref, label_of, plane)
    totals = Totals(12)

    def put_direction_image(plane, image):
        w_ref[plane + 1] = masked(image_ref[plane + 1] - image, present_flags(place_ref, plane))

    stencil(lambda plane: v_ref[plane + 2], k_ref, diag_ref, -1, 9, put_direction_image)

    def put_second(plane, image):
        own = w_ref[plane + 1, 0:16]
        image = image[:16]
        residual = r_ref[plane]
        direction = residual - v_ref[plane + 2, 0:16]
        w_out[plane] = own
        d_out[plane] = direction
        aw_out[plane] = image
        totals.by_label(mid_ref[3, plane, 0:16], image)
        totals.add(8, fold(direction * own))
        totals.add(9, fold(own * own))
        totals.add(10, fold(residual * own))
        totals.add(11, fold(own * image))

    stencil(lambda plane: w_ref[plane + 1], k_ref, diag_ref, 0, 8, put_second)
    square = jnp.sum(got, axis=0, keepdims=True) * (1.0 / 256.0)
    shape = (1, 128)
    square = jnp.sum(jnp.where(lanes(shape) == 8, square, 0.0), axis=1, keepdims=True)
    row = slot_row(totals.values) + jnp.where(lanes(shape) == 12, square, 0.0)
    slot_ref[...] = jnp.broadcast_to(row, (256, 128))


def last_kernel(
    got_ref, right_ref, left_ref, last_ref, low_ref, mid_ref, high_ref, km_ref, ke_ref, diag_ref,
    x_ref, r_ref, w_ref, d_ref, aw_ref, place_ref, x_out, r_out, y_ref, v_ref,
):
    k_ref = Planes(km_ref, ke_ref)
    got = got_ref[...]
    coarse_rhs = coarse_rows(got, label_chooser())
    solved = coarse_solve(coarse_rhs, right_ref, left_ref, last_ref)
    y_ref[...] = solved
    row = jnp.sum(got, axis=0, keepdims=True)

    def scalar(at):
        return jnp.sum(jnp.where(lanes((1, 128)) == at, row, 0.0), axis=1, keepdims=True)

    dw, ww, rw, waw, rr = (scalar(at) for at in (8, 9, 10, 11, 12))
    hq = jnp.sum(jnp.sum(coarse_rhs * solved, axis=1, keepdims=True), axis=0, keepdims=True)
    alpha = rr / dw
    rr_next = rr - 2.0 * alpha * rw + alpha * alpha * ww
    beta = rr_next / rr
    gain = 1.0 + beta
    curvature = gain * gain * dw - 2.0 * gain * alpha * ww + alpha * alpha * (waw - hq)
    alpha_next = rr_next / curvature

    def label_of(plane):
        return piece(low_ref, mid_ref, high_ref, 3, plane)

    for plane in range(-1, 9):
        v_ref[plane + 1] = spread_field(y_ref, place_ref, label_of, plane)

    def put(plane, image):
        w = w_ref[plane]
        d = d_ref[plane]
        u = aw_ref[plane] - image[:16]
        d_next = gain * d - alpha * (w - v_ref[plane + 1, 0:16])
        w_next = gain * w - alpha * u
        x_out[plane] = x_ref[plane] + alpha * d + alpha_next * d_next
        r_out[plane] = r_ref[plane] - alpha * w - alpha_next * w_next

    stencil(lambda plane: v_ref[plane + 1], k_ref, diag_ref, 0, 8, put)


VMEM = pl.BlockSpec(memory_space=pltpu.VMEM)
SMEM = pl.BlockSpec(memory_space=pltpu.SMEM)


def shape_of(*dims):
    return jax.ShapeDtypeStruct(dims, F32)


def call(kernel, name, outs, scratch, in_specs, mib, cost=None):
    return pl.pallas_call(
        kernel,
        name=name,
        out_shape=outs,
        in_specs=in_specs,
        out_specs=tuple(VMEM for _ in outs),
        scratch_shapes=scratch,
        cost_estimate=cost,
        compiler_params=pltpu.CompilerParams(vmem_limit_bytes=mib * 1024 * 1024),
    )


def ring_pairs(peers):
    up = [(i, (i + 1) % peers) for i in range(peers)]
    return up, [(j, i) for i, j in up]


def exchange_all(slots):
    width = slots.shape[0] // 256
    return lax.all_to_all(slots.reshape(256, width * 128), AXIAL_CIRC, 0, 0, tiled=True).reshape(
        256 * width, 128
    )


def exchange(slots, count):
    return lax.all_to_all(slots.reshape(256, count, 128), AXIAL_CIRC, 0, 0, tiled=True).reshape(
        256 * count, 128
    )


def shards(right_side, stiffness, material, groups):
    place = jnp.stack([lax.axis_index(AXIAL), lax.axis_index(CIRC)]).astype(jnp.int32)

    def fields(rows):
        parts = (right_side, stiffness, material, groups)
        return jnp.stack([part[:, rows].astype(F32) for part in parts])

    up, down = ring_pairs(16)
    before = lax.ppermute(fields(slice(16 - EDGE, 16)), CIRC, up)
    after = lax.ppermute(fields(slice(0, EDGE)), CIRC, down)
    middle = jnp.concatenate([fields(slice(0, 16)), after, before], axis=2)
    low = lax.ppermute(middle[:, 8 - DEPTH :], AXIAL, up)
    high = lax.ppermute(middle[:, :DEPTH], AXIAL, down)
    table = np.zeros((16, 128), np.float32)
    table[:13, :CLASSES] = coefficient_table().T
    ext = (ROWS, 256)
    table = jnp.asarray(table)
    k_mid, even, odd = call(
        inner_kernel,
        "inner",
        (shape_of(8, 13, *ext), shape_of(64, 80), shape_of(64, 144)),
        [pltpu.VMEM((8, 9, 16, 256), F32)],
        [VMEM, VMEM],
        20,
        pl.CostEstimate(flops=40_000_000, transcendentals=0, bytes_accessed=4_000_000),
    )(middle, table)
    k_end, diag, slots = call(
        setup_kernel,
        "setup",
        (shape_of(6, 13, *ext), shape_of(12, *ext), shape_of(768, 128)),
        [],
        [VMEM, VMEM, VMEM, VMEM, SMEM, VMEM, VMEM, VMEM],
        20,
    )(low, middle, high, table, place, k_mid, even, odd)
    gathered = exchange_all(slots)
    square = (BLOCK, BLOCK)
    double = (2 * BLOCK, 2 * BLOCK)
    right, left, last, y = call(
        factor_kernel,
        "factor",
        (shape_of(14, BLOCK, 3 * BLOCK), shape_of(14, 2 * BLOCK, BLOCK), shape_of(*double), shape_of(16, BLOCK)),
        [
            pltpu.VMEM((16, *square), F32),
            pltpu.VMEM((16, *square), F32),
            pltpu.VMEM((8, *square), F32),
            pltpu.VMEM((8, *square), F32),
            pltpu.VMEM((1, *double), F32),
            pltpu.VMEM((1, *double), F32),
            pltpu.VMEM((16, BLOCK), F32),
            pltpu.VMEM((16, BLOCK), F32),
        ],
        [VMEM, SMEM],
        24,
    )(gathered, jnp.asarray(np.array(SCALES, np.float32)))
    own = (8, 16, 256)
    x0, r0, image, slots = call(
        start_kernel,
        "start",
        (shape_of(*own), shape_of(*own), shape_of(10, *ext), shape_of(256, 128)),
        [pltpu.VMEM((14, *ext), F32), pltpu.VMEM((12, *ext), F32)],
        [VMEM] * 7 + [SMEM],
        24,
    )(low, middle, high, k_mid, k_end, diag, y, place)
    gathered = exchange(slots, 1)
    w0, d0, aw0, slots = call(
        first_kernel,
        "first",
        (shape_of(*own), shape_of(*own), shape_of(*own), shape_of(256, 128)),
        [pltpu.VMEM((16, BLOCK), F32), pltpu.VMEM((12, *ext), F32), pltpu.VMEM((10, *ext), F32)],
        [VMEM] * 12 + [SMEM],
        24,
    )(gathered, right, left, last, low, middle, high, k_mid, k_end, diag, image, r0, place)
    gathered = exchange(slots, 1)
    return call(
        last_kernel,
        "last",
        (shape_of(*own), shape_of(*own)),
        [pltpu.VMEM((16, BLOCK), F32), pltpu.VMEM((10, *ext), F32)],
        [VMEM] * 15 + [SMEM],
        24,
    )(gathered, right, left, last, low, middle, high, k_mid, k_end, diag, x0, r0, w0, d0, aw0, place)


def solution(mesh):
    split = Mesh(mesh.devices.reshape(8, 2, 4, 4), ("axial_0", "axial_1", "circ_0", "circ_1"))
    placed = P(AXIAL, CIRC, None)
    return jax.shard_map(
        shards,
        mesh=split,
        in_specs=(placed,) * 4,
        out_specs=(placed, placed),
        check_vma=False,
    )
```

```python
import math

import jax
import jax.numpy as jnp
import numpy as np
from jax import lax
from jax.experimental import pallas as pl
from jax.experimental.pallas import tpu as pltpu
from jax.sharding import Mesh
from jax.sharding import PartitionSpec as P

LABELS = 8
CLASSES = 16
CIRC = ("circ_0", "circ_1")
AXIAL = ("axial_0", "axial_1")
AXIAL_CIRC = ("axial_0", "axial_1", "circ_0", "circ_1")
MASS_SHIFT = 0.02
HIGH = lax.Precision.HIGHEST
HALF_STEPS = (
    (0, 0, 1),
    (0, 1, -1),
    (0, 1, 0),
    (0, 1, 1),
    (1, -1, -1),
    (1, -1, 0),
    (1, -1, 1),
    (1, 0, -1),
    (1, 0, 0),
    (1, 0, 1),
    (1, 1, -1),
    (1, 1, 0),
    (1, 1, 1),
)
STEP_OF = {step: place for place, step in enumerate(HALF_STEPS)}
SHIFTS = [(sy, sz) for sy in (-1, 0, 1) for sz in (-1, 0, 1)]
ROWS = 24
EDGE = 4
DEPTH = 3
BLOCK = 128
F32 = jnp.float32
BF16 = jnp.bfloat16


def coefficient_table():
    rows_out = []
    for material_id in range(CLASSES):
        fiber_angle = math.pi * (material_id % 8) / 8.0
        if material_id < 8:
            fiber_dir = (math.cos(fiber_angle), math.sin(fiber_angle), 0.0)
            strength, anisotropy = (1.0, 6.0)
        else:
            fiber_dir = (0.6 * math.cos(fiber_angle), 0.6 * math.sin(fiber_angle), 0.8)
            strength, anisotropy = (0.35, 2.0)
        line_values = []
        for offset in HALF_STEPS:
            length_sq = float(offset[0] * offset[0] + offset[1] * offset[1] + offset[2] * offset[2])
            along_fiber = (
                fiber_dir[0] * offset[0] + fiber_dir[1] * offset[1] + fiber_dir[2] * offset[2]
            )
            line_values.append(
                strength * (0.15 + anisotropy * along_fiber * along_fiber / length_sq) / length_sq
            )
        rows_out.append(line_values)
    return np.array(rows_out, dtype=np.float32)


def inverse_scales():
    table = coefficient_table().astype(np.float64)
    widest = MASS_SHIFT + 0.3 * (table.sum(axis=1).max() + table.max(axis=0).sum())
    low = 0.5 * MASS_SHIFT / widest
    scales, lows = [], []
    while 1.0 - low > 2e-7:
        scales.append(2.0 / (1.0 + low))
        lows.append(low)
        low = 4.0 * low / (1.0 + low) ** 2
    return scales, lows


SCALES, LOWS = inverse_scales()


def lanes(shape):
    return lax.broadcasted_iota(jnp.int32, shape, len(shape) - 1)


def sublanes(shape):
    return lax.broadcasted_iota(jnp.int32, shape, len(shape) - 2)


def shift_z(values, move, fill):
    if move == 0:
        return values
    length = values.shape[-1]
    turned = pltpu.roll(values, (-move) % length, axis=1)
    edge = length - 1 if move > 0 else 0
    return jnp.where(lanes(values.shape) == edge, fill, turned)


def shift_y(values, move):
    if move == 0:
        return values
    return pltpu.roll(values, (-move) % values.shape[0], axis=0)


def shifted(values, fill):
    by_z = {sz: shift_z(values, sz, fill) for sz in (-1, 0, 1)}
    return {(sy, sz): shift_y(by_z[sz], sy) for sy, sz in SHIFTS}


def present_flags(place_ref, plane):
    if plane < 0:
        return place_ref[0] > 0
    if plane > 7:
        return place_ref[0] < 15
    return None


def masked(values, flag):
    if flag is None:
        return values
    return values * jnp.where(flag, 1.0, 0.0).astype(F32)


def stencil(v_at, k_ref, diag_ref, start, stop, emit):
    wide = {}
    made = {}

    def prepare(plane):
        values = v_at(plane)
        wide[plane] = shifted(values, 0.0)
        made[plane] = [k_ref[plane + DEPTH, j] * values for j in range(13)]

    prepare(start - 1)
    prepare(start)
    for plane in range(start, stop):
        prepare(plane + 1)
        total = None
        for j, (ox, oy, oz) in enumerate(HALF_STEPS):
            pair = wide[plane + ox][(oy, oz)] + wide[plane - ox][(-oy, -oz)]
            term = k_ref[plane + DEPTH, j] * pair
            total = term if total is None else total + term
        for sz in (-1, 0, 1):
            by_y = None
            for sy in (-1, 0, 1):
                part = made[plane + 1][STEP_OF[(1, sy, sz)]] + made[plane - 1][STEP_OF[(1, -sy, -sz)]]
                if (0, sy, sz) in STEP_OF:
                    part = part + made[plane][STEP_OF[(0, sy, sz)]]
                elif (0, -sy, -sz) in STEP_OF:
                    part = part + made[plane][STEP_OF[(0, -sy, -sz)]]
                part = shift_y(part, sy)
                by_y = part if by_y is None else by_y + part
            total = total + shift_z(by_y, sz, 0.0)
        emit(plane, diag_ref[plane + 2] * wide[plane][(0, 0)] - 0.5 * total)
        del wide[plane - 1], made[plane - 1]


def piece(low_ref, mid_ref, high_ref, field, plane):
    if plane < 0:
        return low_ref[field, plane + DEPTH]
    if plane > 7:
        return high_ref[field, plane - 8]
    return mid_ref[field, plane]


def split3(values):
    high = values.astype(BF16)
    rest = values - high.astype(F32)
    mid = rest.astype(BF16)
    low = (rest - mid.astype(F32)).astype(BF16)
    return high, mid, low


def dot(a, b, dims=((1,), (0,))):
    return lax.dot_general(a, b, (dims, ((), ())), preferred_element_type=F32)


def dot_high(a, b, dims=((1,), (0,))):
    return lax.dot_general(
        a, b, (dims, ((), ())), precision=HIGH, preferred_element_type=F32
    )


def pick(values, chooser):
    return sum(dot(part, chooser) for part in split3(values))


class Planes:
    def __init__(self, mid_ref, end_ref):
        self.mid_ref = mid_ref
        self.end_ref = end_ref

    def place(self, key):
        plane = key[0] - DEPTH
        if 0 <= plane < 8:
            return self.mid_ref, (plane, *key[1:])
        return self.end_ref, ((plane + DEPTH if plane < 0 else plane - 5), *key[1:])

    def __getitem__(self, key):
        ref, at = self.place(key)
        return ref[at]

    def __setitem__(self, key, values):
        ref, at = self.place(key)
        ref[at] = values


def fill_stiffness(k_ref, table_ref, plane, stiff, kind):
    kind = kind.astype(jnp.int32)
    for j in range(13):
        row = jnp.broadcast_to(table_ref[j : j + 1, :], (8, 128))
        parts = []
        for top in range(0, ROWS, 8):
            line = [
                gather_lanes(row, kind[top : top + 8, left : left + 128]) for left in (0, 128)
            ]
            parts.append(jnp.concatenate(line, axis=1))
        k_ref[plane + DEPTH, j] = stiff * jnp.concatenate(parts, axis=0)


def by_label(pairs):
    out = []
    for label in range(LABELS):
        total = None
        for weight, target in pairs:
            term = jnp.where(target == float(label), weight, 0.0)
            total = term if total is None else total + term
        out.append(total)
    return out


def chosen_rows(home):
    return jnp.concatenate(
        [jnp.where(home == float(k), 1.0, 0.0) for k in range(LABELS)], axis=0
    ).astype(BF16)


def cell_sums(chosen, right):
    return sum(dot(chosen, part, ((1,), (1,))) for part in split3(right))


def inner_kernel(mid_ref, table_ref, km_ref, even_ref, odd_ref, label_ref):
    k_ref = Planes(km_ref, None)
    for plane in range(8):
        fill_stiffness(k_ref, table_ref, plane, mid_ref[1, plane], mid_ref[2, plane])
        spots = shifted(mid_ref[3, plane], -1.0)
        for place, shift in enumerate(SHIFTS):
            label_ref[plane, place] = spots[shift][:16]
    row16 = sublanes((16, 256))
    ones = jnp.ones((8, 256), F32)
    sums = {}
    for plane in range(8):
        own, up = [], []
        for j, (ox, oy, oz) in enumerate(HALF_STEPS):
            if ox == 0 or plane < 7:
                across = shift_z(shift_y(k_ref[plane + ox + DEPTH, j], oy), oz, 0.0)[:16]
                weight = -0.5 * (k_ref[plane + DEPTH, j, 0:16] + across)
                target = label_ref[plane + ox, SHIFTS.index((oy, oz))]
                if oy == 0:
                    own.append((weight, target))
                else:
                    edge = 15 if oy == 1 else 0
                    own.append((jnp.where(row16 == edge, 0.0, weight), target))
                    if oy == 1:
                        up.append((jnp.where(row16 == 15, weight, 0.0)[8:], target[8:]))
            if oy == -1 and plane > 0:
                back = shift_z(shift_y(k_ref[plane - 1 + DEPTH, j], -oy), -oz, 0.0)[8:16]
                back = -0.5 * (k_ref[plane + DEPTH, j, 8:16] + back)
                source = label_ref[plane - 1, SHIFTS.index((-oy, -oz)), 8:16]
                up.append((jnp.where(row16[8:] == 15, back, 0.0), source))
        own = by_label(own)
        sides = ([], by_label(up))
        load = mid_ref[0, plane, 0:16]
        home = label_ref[plane, SHIFTS.index((0, 0))]
        for half in (0, 1):
            rows = slice(8 * half, 8 * half + 8)
            right = jnp.concatenate([o[rows] for o in own] + [load[rows], ones] + sides[half], axis=0)
            got = cell_sums(chosen_rows(home[rows]), right)
            sums[half] = got if half not in sums else sums[half] + got
    even_ref[...] = sums[0]
    odd_ref[...] = sums[1]


def setup_kernel(
    low_ref, mid_ref, high_ref, table_ref, place_ref, km_ref, even_ref, odd_ref,
    ke_ref, diag_ref, slot_ref,
):
    k_ref = Planes(km_ref, ke_ref)
    for plane in (-3, -2, -1, 8, 9, 10):
        stiff = masked(piece(low_ref, mid_ref, high_ref, 1, plane), present_flags(place_ref, plane))
        kind = piece(low_ref, mid_ref, high_ref, 2, plane)
        fill_stiffness(k_ref, table_ref, plane, stiff, kind)
    for plane in range(-2, 10):
        own = None
        total = None
        for j in range(13):
            term = k_ref[plane + DEPTH, j]
            own = term if own is None else own + term
        for sz in (-1, 0, 1):
            by_y = None
            for sy in (-1, 0, 1):
                part = k_ref[plane + 1 + DEPTH, STEP_OF[(1, sy, sz)]]
                part = part + k_ref[plane - 1 + DEPTH, STEP_OF[(1, -sy, -sz)]]
                if (0, sy, sz) in STEP_OF:
                    part = part + k_ref[plane + DEPTH, STEP_OF[(0, sy, sz)]]
                elif (0, -sy, -sz) in STEP_OF:
                    part = part + k_ref[plane + DEPTH, STEP_OF[(0, -sy, -sz)]]
                part = shift_y(part, sy)
                by_y = part if by_y is None else by_y + part
            by_y = shift_z(by_y, sz, 0.0)
            total = by_y if total is None else total + by_y
        diag_ref[plane + 2] = MASS_SHIFT + own + 0.5 * total
    middle = None
    for plane in range(8):
        for top in (0, 8):
            rows = slice(top, top + 8)
            got = cell_sums(
                chosen_rows(mid_ref[3, plane, rows]), 0.5 * diag_ref[plane + 2, rows]
            )
            middle = got if middle is None else middle + got
    spots = {shift: value[:16] for shift, value in shifted(high_ref[3, 0], -1.0).items()}
    row16 = sublanes((16, 256))
    nexts, up, down = [], [], []
    for j, (ox, oy, oz) in enumerate(HALF_STEPS):
        if ox == 1:
            across = shift_z(shift_y(k_ref[8 + DEPTH, j], oy), oz, 0.0)[:16]
            weight = -0.5 * (k_ref[7 + DEPTH, j, 0:16] + across)
            target = spots[(oy, oz)]
            if oy == 0:
                nexts.append((weight, target))
            elif oy == 1:
                nexts.append((jnp.where(row16 == 15, 0.0, weight), target))
                up.append((jnp.where(row16 == 15, weight, 0.0)[8:], target[8:]))
            else:
                nexts.append((jnp.where(row16 == 0, 0.0, weight), target))
                down.append((jnp.where(row16 == 0, weight, 0.0)[:8], target[:8]))
    nexts, up, down = by_label(nexts), by_label(up), by_label(down)
    sums = [even_ref[...], odd_ref[...]]
    for half in (0, 1):
        rows = slice(8 * half, 8 * half + 8)
        right = jnp.concatenate([o[rows] for o in nexts] + (down, up)[half], axis=0)
        sums.append(cell_sums(chosen_rows(mid_ref[3, 7, rows]), right))

    shape = (64, 8)
    total = jnp.sum(
        jnp.where(sublanes(shape) % 8 == lanes(shape), middle, 0.0), axis=1, keepdims=True
    )
    shape = (64, 3 * 128)
    total = jnp.where(
        jnp.logical_and(lanes(shape) < 128, lanes(shape) % 16 == sublanes(shape) // 8), total, 0.0
    )
    for which in range(4):
        width = sums[which].shape[1]
        shape = (64, width)
        kept = jnp.where(sublanes(shape) % 8 == lanes(shape) % 8, sums[which], 0.0)
        shape = (width, 3 * 128)
        group = sublanes(shape) // 8
        if which < 2:
            spot = jnp.where(group < 8, group, jnp.where(group < 10, 32 + group, group - 2))
        else:
            spot = jnp.where(group < 8, 24 + group, (8 if which == 2 else 24) + group)
        here = (lanes(shape) // 128) * 16 + lanes(shape) % 16
        total = total + pick(kept, jnp.where(here == spot, 1.0, 0.0).astype(BF16))
    shape = (64, 3 * 128)
    total = jnp.where(sublanes(shape) // 8 == (lanes(shape) % 128) // 16, total, 0.0)
    total = jnp.sum(total, axis=0, keepdims=True)
    rows = [total[:, 128 * r : 128 * r + 128] for r in range(3)]
    slots = jnp.concatenate(rows * 8, axis=0)
    for at in range(0, 768, 24):
        slot_ref[at : at + 24, :] = slots


def coarse_rows(values, chooser):
    spread = pick(values, chooser)
    shape = (256, BLOCK)
    kept = jnp.where(sublanes(shape) % 16 == lanes(shape) % 16, spread, 0.0)
    return jnp.sum(kept.reshape(16, 16, BLOCK), axis=1)


def as_columns(rows):
    count = len(rows)
    stacked = jnp.concatenate(rows + [jnp.zeros((1, BLOCK), F32)] * (8 - count), axis=0)
    turned = stacked.T
    return [turned[:, i : i + 1] for i in range(count)]


def coarse_solve(coarse_rhs, right_ref, left_ref, last_ref):
    now = [coarse_rhs[i : i + 1, :] for i in range(16)]
    begin = 0
    stages = []
    while len(now) > 2:
        count = len(now)
        odd = now[1::2]
        even = now[0::2]
        solved = []
        for q, column in enumerate(as_columns(odd)):
            product = jnp.sum(right_ref[begin + q] * column, axis=0, keepdims=True)
            solved.append(product[:, :BLOCK])
            even[q] = even[q] - product[:, BLOCK : 2 * BLOCK]
            if q + 1 < len(even):
                even[q + 1] = even[q + 1] - product[:, 2 * BLOCK :]
        stages.append((begin, solved))
        begin += count // 2
        now = even
    column = jnp.concatenate(as_columns(now), axis=0)
    both = jnp.sum(last_ref[...] * column, axis=0, keepdims=True)
    found = [both[:, :BLOCK], both[:, BLOCK:]]
    for begin, solved in reversed(stages):
        columns = as_columns(found)
        merged = []
        for q, value in enumerate(solved):
            value = value - jnp.sum(left_ref[begin + q, :BLOCK] * columns[q], axis=0, keepdims=True)
            if q + 1 < len(found):
                value = value - jnp.sum(
                    left_ref[begin + q, BLOCK:] * columns[q + 1], axis=0, keepdims=True
                )
            merged += [found[q], value]
        found = merged
    return jnp.concatenate(found, axis=0)


def split2(values):
    high = values.astype(BF16)
    return high, (values - high.astype(F32)).astype(BF16)


def left_stack(halves):
    high, low = halves
    return jnp.concatenate([high, high, low], axis=1)


def right_stack(halves):
    high, low = halves
    return jnp.concatenate([high, low, high], axis=0)


def invert(blocks, begin, scale_ref, x_ref, p_ref):
    shape = blocks[0].shape
    size = shape[0]
    eye = jnp.where(lanes(shape) == sublanes(shape), 1.0, 0.0).astype(F32)
    for q, block in enumerate(blocks):
        kept = eye * block
        across = 1.0 / jnp.sum(kept, axis=0, keepdims=True)
        down = 1.0 / jnp.sum(kept, axis=1, keepdims=True)
        c = 0.5 * scale_ref[begin]
        x_ref[q] = (2.0 * c * eye - (c * c) * (block * down)) * across
    for q, block in enumerate(blocks):
        p_ref[q] = dot(left_stack(split2(block)), right_stack(split2(x_ref[q])))

    def step(k, carry):
        c = scale_ref[k]
        for q in range(len(blocks)):
            x = x_ref[q]
            p = p_ref[q]
            halves = split2(p)
            both = jnp.concatenate([left_stack(halves), left_stack(split2(x))], axis=0)
            product = dot(both, right_stack(halves))
            p_ref[q] = (2.0 * c) * p - (c * c) * product[:size]
            x_ref[q] = (2.0 * c) * x - (c * c) * product[size:]
        return carry

    lax.fori_loop(begin + 1, len(SCALES) - 2, step, 0)
    values = [x_ref[q] for q in range(len(blocks))]
    rests = [
        eye - dot(left_stack(split2(s)), right_stack(split2(x))) for s, x in zip(blocks, values)
    ]
    values = [x + dot(x.astype(BF16), r.astype(BF16)) for x, r in zip(values, rests)]
    rests = [eye - dot_high(s, x) for s, x in zip(blocks, values)]
    return [x + dot(x.astype(BF16), r.astype(BF16)) for x, r in zip(values, rests)]


def turned(values):
    shape = (BLOCK, BLOCK)
    eye = jnp.where(lanes(shape) == sublanes(shape), 1.0, 0.0).astype(BF16)
    return sum(dot(eye, part, ((1,), (1,))) for part in split3(values))


def gather_lanes(values, spot):
    return jnp.take_along_axis(values, spot, axis=1, mode="promise_in_bounds")


def unpack_coarse(slots_ref, d_ref, b_ref, f_ref, n_ref):
    for top in (0, 8):
        shape = (8, BLOCK)
        device = sublanes(shape) + top
        ring = lanes(shape) % 16
        column = lanes(shape) // 16
        ahead = (ring - device + 16) % 16
        side = (ahead + 1) % 16
        home = jnp.minimum(ahead, 1) * 8 + column
        cross = jnp.minimum(side, 1) * 8 + column
        for s in range(16):
            at = 48 * s + 3 * top
            rows = [slots_ref[pl.ds(at + r, 8, stride=3), :] for r in range(3)]
            for label in range(LABELS):
                row = 16 * label + top
                got = gather_lanes(rows[0], home + 16 * label)
                d_ref[s, row : row + 8, :] = jnp.where(ahead < 2, got, 0.0)
                if s < 15:
                    got = jnp.where(
                        side < 2,
                        gather_lanes(rows[1], cross + 16 * label),
                        gather_lanes(rows[2], column + 16 * label),
                    )
                    b_ref[s, row : row + 8, :] = jnp.where(side < 3, got, 0.0)
            for place, target in ((8, f_ref), (9, n_ref)):
                got = jnp.where(ring == device, gather_lanes(rows[2], 16 * column + place), 0.0)
                total = jnp.sum(got, axis=0, keepdims=True)
                if top > 0:
                    total = target[s : s + 1, :] + total
                target[s : s + 1, :] = total


def first_step(d_ref, n_ref):
    shape = (BLOCK, BLOCK)
    eye = lanes(shape) == sublanes(shape)
    diagonal = jnp.concatenate(
        [jnp.sum(jnp.where(eye, d_ref[s], 0.0), axis=0, keepdims=True) for s in range(16)], axis=0
    )
    low = jnp.min((0.5 * MASS_SHIFT) * n_ref[...] / diagonal)
    return sum(jnp.where(low >= bound, 1, 0).astype(jnp.int32) for bound in LOWS[1:-2])


def factor_kernel(
    slots_ref, scale_ref, right_ref, left_ref, last_ref, y_ref, d_ref, b_ref, x_ref, p_ref,
    xl_ref, pl_ref, f_ref, n_ref,
):
    unpack_coarse(slots_ref, d_ref, b_ref, f_ref, n_ref)
    b_ref[15] = jnp.zeros((BLOCK, BLOCK), F32)
    for i in range(16):
        d_ref[i] = d_ref[i] + turned(d_ref[i])
    first = first_step(d_ref, n_ref)
    begin = 0
    stride = 1
    while stride < 8:
        count = 8 // stride
        odd = [(2 * q + 1) * stride for q in range(count)]
        inverses = invert([d_ref[i] for i in odd], first, scale_ref, x_ref, p_ref)
        ups = [
            dot_high(inverse, b_ref[i - stride].T) for i, inverse in zip(odd, inverses)
        ]
        downs = [dot_high(inverse, b_ref[i]) for i, inverse in zip(odd, inverses)]
        products = [jnp.concatenate(pair, axis=1) for pair in zip(ups, downs)]
        for q in range(count):
            right_ref[begin + q, :, :BLOCK] = inverses[q]
            right_ref[begin + q, :, BLOCK:] = products[q]
        grams = [dot_high(b_ref[i - stride], product) for i, product in zip(odd, products)]
        for q in range(count):
            left_ref[begin + q, :BLOCK, :] = ups[q].T
            left_ref[begin + q, BLOCK:, :] = downs[q].T
        afters = [
            dot_high(left_ref[begin + q, BLOCK:, :], b_ref[i])
            for q, i in enumerate(odd)
            if i + stride < 16
        ]
        for q, i in enumerate(odd):
            change = grams[q][:, :BLOCK]
            if q > 0:
                change = change + afters[q - 1]
            d_ref[i - stride] = d_ref[i - stride] - change
            b_ref[i - stride] = -grams[q][:, BLOCK:]
        begin += count
        stride *= 2
    pair = jnp.concatenate(
        [
            jnp.concatenate([d_ref[0], b_ref[0]], axis=1),
            jnp.concatenate([b_ref[0].T, d_ref[8]], axis=1),
        ],
        axis=0,
    )
    (last,) = invert([pair], first, scale_ref, xl_ref, pl_ref)
    last_ref[...] = last
    y_ref[...] = coarse_solve(f_ref[...], right_ref, left_ref, last_ref)


def spread_field(y_ref, place_ref, label_of, plane):
    axial = place_ref[0]
    if plane < 0:
        axial = jnp.maximum(axial - 1, 0)
    elif plane > 7:
        axial = jnp.minimum(axial + 1, 15)
    line = jnp.broadcast_to(y_ref[pl.ds(axial, 1), :], (8, BLOCK))
    ring = sublanes((ROWS, 256))
    move = jnp.where(ring < 16, 0, jnp.where(ring < 16 + EDGE, 1, 15))
    spot = label_of(plane).astype(jnp.int32) * 16 + (place_ref[1] + move) % 16
    parts = []
    for top in range(0, ROWS, 8):
        parts.append(
            jnp.concatenate(
                [
                    jnp.take_along_axis(
                        line,
                        spot[top : top + 8, left : left + 128],
                        axis=1,
                        mode="promise_in_bounds",
                    )
                    for left in (0, 128)
                ],
                axis=1,
            )
        )
    return masked(jnp.concatenate(parts, axis=0), present_flags(place_ref, plane))


def fold(values):
    half = values[:8] + values[8:]
    return half[:, :128] + half[:, 128:]


def slot_row(totals):
    count = len(totals)
    stacked = jnp.concatenate(totals, axis=0)
    shape = (8 * count, 128)
    sums = jnp.sum(stacked, axis=1, keepdims=True)
    kept = jnp.where(sublanes(shape) // 8 == lanes(shape), sums, 0.0)
    return jnp.sum(kept, axis=0, keepdims=True)


class Totals:
    def __init__(self, count):
        self.values = [None] * count

    def add(self, at, term):
        self.values[at] = term if self.values[at] is None else self.values[at] + term

    def by_label(self, labels, field):
        for k in range(LABELS):
            self.add(k, fold(jnp.where(labels == float(k), field, 0.0)))


def start_kernel(
    low_ref, mid_ref, high_ref, km_ref, ke_ref, diag_ref, y_ref, place_ref,
    x_out, r_out, image_ref, slot_ref, v_ref, w_ref,
):
    k_ref = Planes(km_ref, ke_ref)
    def label_of(plane):
        return piece(low_ref, mid_ref, high_ref, 3, plane)

    for plane in range(-3, 11):
        v_ref[plane + 3] = spread_field(y_ref, place_ref, label_of, plane)

    def put_residual(plane, image):
        load = piece(low_ref, mid_ref, high_ref, 0, plane)
        w_ref[plane + 2] = masked(load - image, present_flags(place_ref, plane))

    stencil(lambda plane: v_ref[plane + 3], k_ref, diag_ref, -2, 10, put_residual)
    totals = Totals(9)

    def put_image(plane, image):
        image_ref[plane + 1] = image
        if 0 <= plane < 8:
            totals.by_label(mid_ref[3, plane, 0:16], image[:16])
            own = w_ref[plane + 2, 0:16]
            totals.add(8, fold(own * own))

    stencil(lambda plane: w_ref[plane + 2], k_ref, diag_ref, -1, 9, put_image)
    for plane in range(8):
        x_out[plane] = v_ref[plane + 3, 0:16]
        r_out[plane] = w_ref[plane + 2, 0:16]
    slot_ref[...] = jnp.broadcast_to(slot_row(totals.values), (256, 128))


def label_chooser():
    shape = (128, BLOCK)
    return jnp.where(sublanes(shape) == lanes(shape) // 16, 1.0, 0.0).astype(BF16)


def first_kernel(
    got_ref, right_ref, left_ref, last_ref, low_ref, mid_ref, high_ref, km_ref, ke_ref, diag_ref, image_ref,
    r_ref, place_ref, w_out, d_out, aw_out, slot_ref, y_ref, v_ref, w_ref,
):
    k_ref = Planes(km_ref, ke_ref)
    got = got_ref[...]
    coarse_rhs = coarse_rows(got, label_chooser())
    y_ref[...] = coarse_solve(coarse_rhs, right_ref, left_ref, last_ref)

    def label_of(plane):
        return piece(low_ref, mid_ref, high_ref, 3, plane)

    for plane in range(-2, 10):
        v_ref[plane + 2] = spread_field(y_ref, place_ref, label_of, plane)
    totals = Totals(12)

    def put_direction_image(plane, image):
        w_ref[plane + 1] = masked(image_ref[plane + 1] - image, present_flags(place_ref, plane))

    stencil(lambda plane: v_ref[plane + 2], k_ref, diag_ref, -1, 9, put_direction_image)

    def put_second(plane, image):
        own = w_ref[plane + 1, 0:16]
        image = image[:16]
        residual = r_ref[plane]
        direction = residual - v_ref[plane + 2, 0:16]
        w_out[plane] = own
        d_out[plane] = direction
        aw_out[plane] = image
        totals.by_label(mid_ref[3, plane, 0:16], image)
        totals.add(8, fold(direction * own))
        totals.add(9, fold(own * own))
        totals.add(10, fold(residual * own))
        totals.add(11, fold(own * image))

    stencil(lambda plane: w_ref[plane + 1], k_ref, diag_ref, 0, 8, put_second)
    square = jnp.sum(got, axis=0, keepdims=True) * (1.0 / 256.0)
    shape = (1, 128)
    square = jnp.sum(jnp.where(lanes(shape) == 8, square, 0.0), axis=1, keepdims=True)
    row = slot_row(totals.values) + jnp.where(lanes(shape) == 12, square, 0.0)
    slot_ref[...] = jnp.broadcast_to(row, (256, 128))


def last_kernel(
    got_ref, right_ref, left_ref, last_ref, low_ref, mid_ref, high_ref, km_ref, ke_ref, diag_ref,
    x_ref, r_ref, w_ref, d_ref, aw_ref, place_ref, x_out, r_out, y_ref, v_ref,
):
    k_ref = Planes(km_ref, ke_ref)
    got = got_ref[...]
    coarse_rhs = coarse_rows(got, label_chooser())
    solved = coarse_solve(coarse_rhs, right_ref, left_ref, last_ref)
    y_ref[...] = solved
    row = jnp.sum(got, axis=0, keepdims=True)

    def scalar(at):
        return jnp.sum(jnp.where(lanes((1, 128)) == at, row, 0.0), axis=1, keepdims=True)

    dw, ww, rw, waw, rr = (scalar(at) for at in (8, 9, 10, 11, 12))
    hq = jnp.sum(jnp.sum(coarse_rhs * solved, axis=1, keepdims=True), axis=0, keepdims=True)
    alpha = rr / dw
    rr_next = rr - 2.0 * alpha * rw + alpha * alpha * ww
    beta = rr_next / rr
    gain = 1.0 + beta
    curvature = gain * gain * dw - 2.0 * gain * alpha * ww + alpha * alpha * (waw - hq)
    alpha_next = rr_next / curvature

    def label_of(plane):
        return piece(low_ref, mid_ref, high_ref, 3, plane)

    for plane in range(-1, 9):
        v_ref[plane + 1] = spread_field(y_ref, place_ref, label_of, plane)

    def put(plane, image):
        w = w_ref[plane]
        d = d_ref[plane]
        u = aw_ref[plane] - image[:16]
        d_next = gain * d - alpha * (w - v_ref[plane + 1, 0:16])
        w_next = gain * w - alpha * u
        x_out[plane] = x_ref[plane] + alpha * d + alpha_next * d_next
        r_out[plane] = r_ref[plane] - alpha * w - alpha_next * w_next

    stencil(lambda plane: v_ref[plane + 1], k_ref, diag_ref, 0, 8, put)


VMEM = pl.BlockSpec(memory_space=pltpu.VMEM)
SMEM = pl.BlockSpec(memory_space=pltpu.SMEM)


def shape_of(*dims):
    return jax.ShapeDtypeStruct(dims, F32)


def call(kernel, name, outs, scratch, in_specs, mib, cost=None):
    return pl.pallas_call(
        kernel,
        name=name,
        out_shape=outs,
        in_specs=in_specs,
        out_specs=tuple(VMEM for _ in outs),
        scratch_shapes=scratch,
        cost_estimate=cost,
        compiler_params=pltpu.CompilerParams(vmem_limit_bytes=mib * 1024 * 1024),
    )


def ring_pairs(peers):
    up = [(i, (i + 1) % peers) for i in range(peers)]
    return up, [(j, i) for i, j in up]


def exchange_all(slots):
    width = slots.shape[0] // 256
    return lax.all_to_all(slots.reshape(256, width * 128), AXIAL_CIRC, 0, 0, tiled=True).reshape(
        256 * width, 128
    )


def exchange(slots, count):
    return lax.all_to_all(slots.reshape(256, count, 128), AXIAL_CIRC, 0, 0, tiled=True).reshape(
        256 * count, 128
    )


def shards(right_side, stiffness, material, groups):
    place = jnp.stack([lax.axis_index(AXIAL), lax.axis_index(CIRC)]).astype(jnp.int32)

    def fields(rows):
        parts = (right_side, stiffness, material, groups)
        return jnp.stack([part[:, rows].astype(F32) for part in parts])

    up, down = ring_pairs(16)
    before = lax.ppermute(fields(slice(16 - EDGE, 16)), CIRC, up)
    after = lax.ppermute(fields(slice(0, EDGE)), CIRC, down)
    middle = jnp.concatenate([fields(slice(0, 16)), after, before], axis=2)
    low = lax.ppermute(middle[:, 8 - DEPTH :], AXIAL, up)
    high = lax.ppermute(middle[:, :DEPTH], AXIAL, down)
    table = np.zeros((16, 128), np.float32)
    table[:13, :CLASSES] = coefficient_table().T
    ext = (ROWS, 256)
    table = jnp.asarray(table)
    k_mid, even, odd = call(
        inner_kernel,
        "inner",
        (shape_of(8, 13, *ext), shape_of(64, 80), shape_of(64, 144)),
        [pltpu.VMEM((8, 9, 16, 256), F32)],
        [VMEM, VMEM],
        20,
        pl.CostEstimate(flops=40_000_000, transcendentals=0, bytes_accessed=4_000_000),
    )(middle, table)
    k_end, diag, slots = call(
        setup_kernel,
        "setup",
        (shape_of(6, 13, *ext), shape_of(12, *ext), shape_of(768, 128)),
        [],
        [VMEM, VMEM, VMEM, VMEM, SMEM, VMEM, VMEM, VMEM],
        20,
    )(low, middle, high, table, place, k_mid, even, odd)
    gathered = exchange_all(slots)
    square = (BLOCK, BLOCK)
    double = (2 * BLOCK, 2 * BLOCK)
    right, left, last, y = call(
        factor_kernel,
        "factor",
        (shape_of(14, BLOCK, 3 * BLOCK), shape_of(14, 2 * BLOCK, BLOCK), shape_of(*double), shape_of(16, BLOCK)),
        [
            pltpu.VMEM((16, *square), F32),
            pltpu.VMEM((16, *square), F32),
            pltpu.VMEM((8, *square), F32),
            pltpu.VMEM((8, *square), F32),
            pltpu.VMEM((1, *double), F32),
            pltpu.VMEM((1, *double), F32),
            pltpu.VMEM((16, BLOCK), F32),
            pltpu.VMEM((16, BLOCK), F32),
        ],
        [VMEM, SMEM],
        24,
    )(gathered, jnp.asarray(np.array(SCALES, np.float32)))
    own = (8, 16, 256)
    x0, r0, image, slots = call(
        start_kernel,
        "start",
        (shape_of(*own), shape_of(*own), shape_of(10, *ext), shape_of(256, 128)),
        [pltpu.VMEM((14, *ext), F32), pltpu.VMEM((12, *ext), F32)],
        [VMEM] * 7 + [SMEM],
        24,
    )(low, middle, high, k_mid, k_end, diag, y, place)
    gathered = exchange(slots, 1)
    w0, d0, aw0, slots = call(
        first_kernel,
        "first",
        (shape_of(*own), shape_of(*own), shape_of(*own), shape_of(256, 128)),
        [pltpu.VMEM((16, BLOCK), F32), pltpu.VMEM((12, *ext), F32), pltpu.VMEM((10, *ext), F32)],
        [VMEM] * 12 + [SMEM],
        24,
    )(gathered, right, left, last, low, middle, high, k_mid, k_end, diag, image, r0, place)
    gathered = exchange(slots, 1)
    return call(
        last_kernel,
        "last",
        (shape_of(*own), shape_of(*own)),
        [pltpu.VMEM((16, BLOCK), F32), pltpu.VMEM((10, *ext), F32)],
        [VMEM] * 15 + [SMEM],
        24,
    )(gathered, right, left, last, low, middle, high, k_mid, k_end, diag, x0, r0, w0, d0, aw0, place)


def solution(mesh):
    split = Mesh(mesh.devices.reshape(8, 2, 4, 4), ("axial_0", "axial_1", "circ_0", "circ_1"))
    placed = P(AXIAL, CIRC, None)
    return jax.shard_map(
        shards,
        mesh=split,
        in_specs=(placed,) * 4,
        out_specs=(placed, placed),
        check_vma=False,
    )
```
